128 devices in a mesh: solver: 4 (over z_lo, core), space: 32 (over z_hi, y, x).
Axes of the slice: x: 4, y: 4, z: 4 (z_hi: 2, z_lo: 2; z = z_hi * 2 + z_lo), core: 2. Of those that a mesh axis runs over, the one named last changes fastest.
Arguments:
- flow_state: float32 [5, 128, 128, 512], P(None, 'space', None, 'solver')
- acoustic_state: bfloat16 [4, 28672, 512], P(None, ('solver', 'space')), may hold values from -6 to 6
- deriv_x: bfloat16 [512, 512], replicated, may hold values from -0.25 to 0.25
- deriv_y: bfloat16 [512, 512], replicated, may hold values from -0.25 to 0.25
- deriv_z: bfloat16 [512, 512], replicated, may hold values from -0.25 to 0.25
- requests: int32 [128, 128, 4], P(('solver', 'space')), may hold values from 0 to 15, as said below
- elem_slot: int32 [28672], P(('solver', 'space')), may hold values from 0 to 511, as said below
- neighbours: int32 [6, 28672], P(None, ('solver', 'space')), may hold values from 0 to 28671, as said below
Outputs:
- flow_increment: float32 [5, 128, 128, 512], P(None, 'space', None, 'solver')
- acoustic_increment: float32 [4, 28672, 512], P(None, ('solver', 'space'))
The draws below stay inside these ranges and needn't reach their ends.
Inputs may be any that keep to these rules, and one draw needn't show every extreme that they name: requests[r, o, c] names one of the 16 blocks of device o. `elem_slot`: the 224 elements of a device name distinct slots; from a quarter of the devices (the same for every requester) all 4 slots are named, from each other device the first 1; other slots are named by no element. `neighbours`: for faces 2 to 5 the neighbour lies on the element's own device; for face 0 on its own device or the one of next lower space index in the same solver group, cyclically; for face 1 on its own or the next higher.
All inputs are finite; a program needn't handle non-finite values.
Results may differ from the reference program's by a relative error of at most 0.0003.
The reference program's roundings to bfloat16 on the way (of `coarse`, `block_table` and `sources`) count: a program that leaves them out, or rounds other values in their place, can miss the bound.
Values may be sent and summed in bfloat16 or wider, within the bound.
No kernel may reach another device: no remote copies, remote signals or barrier semaphores. Data moves between devices by JAX's collectives and lax.ppermute only.
A program may use at most 128 MiB of HBM per device.

```python
import jax
import jax.numpy as jnp
from jax import lax

CX = 4
CZ = 128
P_SIZE = 8
CAP = 4
NODES = 512
ELEM_DEV = 224
ELEMENTS = 28672
BLK_DEV = 16
NX = 128
NY = 128
NZ = 512
N_SOLVER = 4
N_SPACE = 32
DEVICES = 128


def draw_flow_state(key, part):
    keys = jax.random.split(key, 3)
    shape = (NX, NY, NZ)
    density = jax.random.uniform(keys[0], shape, jnp.float32, 0.8, 1.2)
    momentum = 0.3 * jax.random.truncated_normal(keys[1], -2.5, 2.5, (3,) + shape, jnp.float32)
    pressure = jax.random.uniform(keys[2], shape, jnp.float32, 0.7, 1.3)
    energy = pressure / 0.4 + 0.5 * jnp.sum(momentum * momentum, axis=0) / density
    return jnp.concatenate([density[None], momentum, energy[None]], axis=0)


def coupling_tables(key):
    base = jax.random.fold_in(key, 11)
    order = jax.random.permutation(jax.random.fold_in(base, 1), DEVICES)
    counts = jnp.where(order < DEVICES // 4, CAP, CAP // 4).astype(jnp.int32)
    live = (jnp.arange(CAP, dtype=jnp.int32)[None, :] < counts[:, None]).reshape(-1).astype(jnp.int32)

    def one_requester(index):
        own_key = jax.random.fold_in(base, index + 100)
        blocks = jax.random.randint(jax.random.fold_in(own_key, 1), (DEVICES, CAP), 0, BLK_DEV, jnp.int32)
        ranks = jax.random.permutation(jax.random.fold_in(own_key, 2), DEVICES * CAP).astype(jnp.int32)
        score = (1 - live) * (DEVICES * CAP) + ranks
        chosen = jnp.argsort(score)[:ELEM_DEV].astype(jnp.int32)
        return (blocks, chosen)
    blocks, chosen = jax.vmap(one_requester)(jnp.arange(DEVICES, dtype=jnp.int32))
    return (blocks, chosen.reshape(-1))


def draw_requests(key, part):
    return coupling_tables(key)[0]


def draw_elem_slot(key, part):
    return coupling_tables(key)[1]


def draw_neighbours(key, part):
    base = jax.random.fold_in(key, 23)
    element = jnp.arange(ELEMENTS, dtype=jnp.int32)
    device = element // ELEM_DEV
    group = device // N_SPACE
    place = device % N_SPACE
    lower = group * N_SPACE + (place - 1 + N_SPACE) % N_SPACE
    higher = group * N_SPACE + (place + 1) % N_SPACE
    sides = jax.random.randint(jax.random.fold_in(base, 1), (2, ELEMENTS), 0, 2, jnp.int32)
    rows = jax.random.randint(jax.random.fold_in(base, 2), (6, ELEMENTS), 0, ELEM_DEV, jnp.int32)
    target = jnp.stack([jnp.where(sides[0] == 1, lower, device), jnp.where(sides[1] == 1, higher, device), device, device, device, device])
    return target * ELEM_DEV + rows


def level_of(rng, shape, cuts, least, high):
    def one(position, shards_of):
        steps = jax.random.uniform(jax.random.fold_in(jax.random.fold_in(rng, 6), position), (shards_of,), jnp.float32, least / len(cuts), high / len(cuts))
        return jnp.repeat(jnp.exp(steps), shape[position] // shards_of).reshape((-1,) + (1,) * (len(shape) - position - 1))

    gain = one(*cuts[0])
    for cut in cuts[1:]:
        gain = gain * one(*cut)
    return gain


def normal_values(key, shape, spread, reach, pieces=(), kind=jnp.bfloat16):
    drawn = spread * jax.random.normal(key, shape, jnp.float32)
    if pieces:
        drawn = drawn * level_of(key, shape, pieces, -0.22, 0.18)
    return jnp.clip(drawn, -reach, reach).astype(kind)


def setup_inputs(seed: int = 0) -> dict:
    streams_of = jax.random.split(jax.random.key(seed), 9)
    flow_state = draw_flow_state(jax.random.fold_in(streams_of[8], 71), 0)
    acoustic_state = normal_values(streams_of[1], (4, ELEMENTS, NODES), 1.0, 6.0, ((1, 128),))
    deriv_x = normal_values(streams_of[2], (NODES, NODES), NODES ** -0.5, 0.25)
    deriv_y = normal_values(streams_of[3], (NODES, NODES), NODES ** -0.5, 0.25)
    deriv_z = normal_values(streams_of[4], (NODES, NODES), NODES ** -0.5, 0.25)
    requests = draw_requests(jax.random.fold_in(streams_of[8], 71), 0)
    elem_slot = draw_elem_slot(jax.random.fold_in(streams_of[8], 71), 0)
    neighbours = draw_neighbours(jax.random.fold_in(streams_of[8], 71), 0)
    return dict(flow_state=flow_state, acoustic_state=acoustic_state, deriv_x=deriv_x, deriv_y=deriv_y, deriv_z=deriv_z, requests=requests, elem_slot=elem_slot, neighbours=neighbours)


GAMMA_LESS = 0.4
FLOW_STEP = 0.2
SOUND_STEP = 0.2
PENALTY = 1.0


def velocities(state):
    density = state[0]
    return (state[1] / density, state[2] / density, state[3] / density)


def pressure_of(state, velocity):
    return GAMMA_LESS * (state[4] - 0.5 * (state[1] * velocity[0] + state[2] * velocity[1] + state[3] * velocity[2]))


def flux_along(state, velocity, pressure, direction):
    along = velocity[direction]
    rows = [state[1 + direction]]
    for component in range(3):
        addend = state[1 + component] * along
        if component == direction:
            addend = addend + pressure
        rows.append(addend)
    rows.append((state[4] + pressure) * along)
    return jnp.stack(rows)


def central_roll(field, axis_id):
    return (jnp.roll(field, -1, axis_id) - jnp.roll(field, 1, axis_id)) * 0.5


def flow_tendency(state):
    velocity = velocities(state)
    pressure = pressure_of(state, velocity)
    total = central_roll(flux_along(state, velocity, pressure, 0), 1)
    total = total + central_roll(flux_along(state, velocity, pressure, 1), 2)
    total = total + central_roll(flux_along(state, velocity, pressure, 2), 3)
    return -FLOW_STEP * total


def lamb_global(state):
    vel_a, vel_b, vel_c = velocities(state)
    vort_a = central_roll(vel_c, 1) - central_roll(vel_b, 2)
    vort_b = central_roll(vel_a, 2) - central_roll(vel_c, 0)
    vort_c = central_roll(vel_b, 0) - central_roll(vel_a, 1)
    return jnp.stack([vort_b * vel_c - vort_c * vel_b, vort_c * vel_a - vort_a * vel_c, vort_a * vel_b - vort_b * vel_a])


def restrict(lamb_vector):
    shape = lamb_vector.shape
    grouped = lamb_vector.reshape(3, shape[1] // 2, 2, shape[2] // 2, 2, shape[3] // 2, 2)
    return jnp.mean(grouped, axis=(2, 4, 6)).astype(jnp.bfloat16)


def face_index(face_id):
    spot = 0 if face_id % 2 == 0 else P_SIZE - 1
    return (slice(None), slice(None)) + (slice(None),) * (face_id // 2) + (spot,)


def face_trace(cube, face_id):
    part = cube[face_index(face_id)]
    return jnp.transpose(part, (1, 0, 2, 3)).reshape(part.shape[1], 4 * P_SIZE * P_SIZE)


def derivative(values, matrix):
    return lax.dot_general(values, matrix, (((1,), (1,)), ((), ())), preferred_element_type=jnp.float32)


def volume_terms(rounded, sources, deriv_x, deriv_y, deriv_z):
    divergence = derivative(rounded[1], deriv_x) + derivative(rounded[2], deriv_y) + derivative(rounded[3], deriv_z)
    forcing = sources.astype(jnp.float32)
    return jnp.stack([-divergence,
                      -derivative(rounded[0], deriv_x) + forcing[0],
                      -derivative(rounded[0], deriv_y) + forcing[1],
                      -derivative(rounded[0], deriv_z) + forcing[2]])


def add_penalty(total, across, own):
    count = total.shape[1]
    penalty = jnp.zeros((4, count, P_SIZE, P_SIZE, P_SIZE), jnp.float32)
    for face_id in range(6):
        jump_term = across[face_id].astype(jnp.float32) - own[face_id].astype(jnp.float32)
        jump_term = jnp.transpose(jump_term.reshape(count, 4, P_SIZE, P_SIZE), (1, 0, 2, 3))
        penalty = penalty.at[face_index(face_id)].add(jump_term)
    return total + PENALTY * penalty.reshape(total.shape)


def reference(flow_state, acoustic_state, deriv_x, deriv_y, deriv_z, requests, elem_slot, neighbours):
    first = flow_state + flow_tendency(flow_state)
    final_state = 0.5 * flow_state + 0.5 * (first + flow_tendency(first))
    flow_increment = final_state - flow_state

    coarse = restrict(lamb_global(flow_state))
    arranged = coarse.reshape(3, N_SPACE, CX // 2, NY // 2, N_SOLVER, CZ // 2)
    arranged = jnp.transpose(arranged, (4, 1, 0, 2, 3, 5)).reshape(DEVICES, 3, BLK_DEV, NODES)
    block_table = jnp.transpose(arranged, (0, 2, 1, 3)).reshape(DEVICES * BLK_DEV, 3 * NODES)
    owners = jnp.arange(DEVICES, dtype=jnp.int32)[None, :, None]
    global_block = (owners * BLK_DEV + requests).reshape(DEVICES, DEVICES * CAP)
    element_dev = jnp.arange(ELEMENTS, dtype=jnp.int32) // ELEM_DEV
    source_rows = global_block[element_dev, elem_slot]
    sources = jnp.transpose(block_table[source_rows].reshape(ELEMENTS, 3, NODES), (1, 0, 2))

    def tendency(state):
        rounded = state.astype(jnp.bfloat16)
        cube = rounded.reshape(4, ELEMENTS, P_SIZE, P_SIZE, P_SIZE)
        own = [face_trace(cube, face_id) for face_id in range(6)]
        across = [own[face_id ^ 1][neighbours[face_id]] for face_id in range(6)]
        return add_penalty(volume_terms(rounded, sources, deriv_x, deriv_y, deriv_z), across, own)

    start_state = acoustic_state.astype(jnp.float32)
    section_one = start_state + SOUND_STEP * tendency(start_state)
    section_two = 0.75 * start_state + 0.25 * (section_one + SOUND_STEP * tendency(section_one))
    section_three = start_state / 3.0 + (2.0 / 3.0) * (section_two + SOUND_STEP * tendency(section_two))
    return flow_increment, section_three - start_state
```

```python
import jax
import jax.numpy as jnp
from jax import lax
from jax.experimental import pallas as pl
from jax.experimental.pallas import tpu as pltpu
from jax.sharding import PartitionSpec as P

F32 = jnp.float32
BF16 = jnp.bfloat16
I32 = jnp.int32

EL = 224
NODES = 512
FLOW_STEP = 0.2
SOUND_STEP = 0.2
VMEM_LIMIT = 40 * 1024 * 1024


def iota(shape, dim):
    return lax.broadcasted_iota(I32, shape, dim)


def full(*shape):
    return jax.ShapeDtypeStruct(shape, F32)


def half(*shape):
    return jax.ShapeDtypeStruct(shape, BF16)


def call(body, outs, name, args, scratch=(), aliases=None, in_specs=None, out_specs=None):
    vmem = pl.BlockSpec(memory_space=pltpu.VMEM)
    many = isinstance(outs, (list, tuple))
    return pl.pallas_call(
        body,
        out_shape=outs,
        in_specs=in_specs or [vmem] * len(args),
        out_specs=out_specs or ([vmem] * len(outs) if many else vmem),
        scratch_shapes=list(scratch),
        name=name,
        input_output_aliases=aliases or {},
        compiler_params=pltpu.CompilerParams(vmem_limit_bytes=VMEM_LIMIT),
    )(*args)


def primitives(rows):
    inv = 1.0 / rows[0]
    v1, v2, v3 = rows[1] * inv, rows[2] * inv, rows[3] * inv
    p = 0.4 * (rows[4] - 0.5 * (rows[1] * v1 + rows[2] * v2 + rows[3] * v3))
    return (v1, v2, v3), p


def flux(rows, v, p, k):
    along = v[k]
    out = [rows[1 + k]]
    for c in range(3):
        t = rows[1 + c] * along
        out.append(t + p if c == k else t)
    out.append((rows[4] + p) * along)
    return out


def roll_y(f, step):
    return pltpu.roll(f, step % f.shape[0], 0)


def roll_z(f, step):
    return pltpu.roll(f, step % f.shape[1], 1)


def put_lane(acc, lane, f, source, target):
    return jnp.where(lane == target, roll_z(f, target - source), acc)


def diff_y(f):
    return roll_y(f, -1) - roll_y(f, 1)


def diff_z(f, lane, below, above, slot):
    up = jnp.where(lane == 127, roll_z(above, 127 - slot), roll_z(f, -1))
    down = jnp.where(lane == 0, roll_z(below, -slot), roll_z(f, 1))
    return up - down


def pack_z(planes, lo_ref, hi_ref):
    lane = iota((128, 128), 1)
    lo = jnp.zeros((128, 128), F32)
    hi = jnp.zeros((128, 128), F32)
    for x in range(4):
        for f, field in enumerate(planes(x)):
            slot = f * 4 + x
            lo = put_lane(lo, lane, field, 0, slot)
            hi = put_lane(hi, lane, field, 127, slot)
    lo_ref[...] = lo
    hi_ref[...] = hi


def pair_lanes(tiles, upper):
    lane = iota((EL, 128), 1)
    out = []
    for w in range(2):
        a, b = tiles[2 * w], tiles[2 * w + 1]
        if upper:
            out.append(jnp.where(lane < 64, pltpu.roll(a, 64, 1), b))
        else:
            out.append(jnp.where(lane < 64, a, pltpu.roll(b, 64, 1)))
    return out


def store_traces(first_tiles, last_tiles, lo_ref, hi_ref):
    for w, t in enumerate(pair_lanes(first_tiles, False)):
        lo_ref[w] = t.astype(BF16)
    for w, t in enumerate(pair_lanes(last_tiles, True)):
        hi_ref[w] = t.astype(BF16)


def edges_body(u, q, xlo, xhi, zlo, zhi, qlo, qhi):
    xlo[...] = u[:, 0]
    xhi[...] = u[:, 3]

    def planes(x):
        rows = [u[f, x] for f in range(5)]
        v, p = primitives(rows)
        return flux(rows, v, p, 2) + [v[0], v[1]]

    pack_z(planes, zlo, zhi)
    store_traces(
        [q[v, :, 0:128].astype(F32) for v in range(4)],
        [q[v, :, 384:512].astype(F32) for v in range(4)],
        qlo,
        qhi,
    )


def lamb_body(u, xbelow, xabove, zbelow, zabove, table, vel, pooled):
    lane = iota((128, 128), 1)
    for x in range(-1, 5):
        if x == -1:
            r, m = xbelow[0], [xbelow[c] for c in (1, 2, 3)]
        elif x == 4:
            r, m = xabove[0], [xabove[c] for c in (1, 2, 3)]
        else:
            r, m = u[0, x], [u[c, x] for c in (1, 2, 3)]
        inv = 1.0 / r
        for c in range(3):
            vel[c, x + 1] = m[c] * inv
    below, above = zbelow[...], zabove[...]
    for pair in range(2):
        total = None
        for x in (2 * pair, 2 * pair + 1):
            v1, v2, v3 = vel[0, x + 1], vel[1, x + 1], vel[2, x + 1]
            w1 = diff_y(v3) - diff_z(v2, lane, below, above, 24 + x)
            w2 = diff_z(v1, lane, below, above, 20 + x) - (vel[2, x + 2] - vel[2, x])
            w3 = (vel[1, x + 2] - vel[1, x]) - diff_y(v1)
            lamb = [w2 * v3 - w3 * v2, w3 * v1 - w1 * v3, w1 * v2 - w2 * v1]
            total = lamb if total is None else [a + b for a, b in zip(total, lamb)]
        for c in range(3):
            pooled[c * 2 + pair] = total[c]
    even, odd = [], []
    for c in range(6):
        t = pooled.at[c]
        even.append(t[pl.ds(0, 32, stride=4), :] + t[pl.ds(1, 32, stride=4), :])
        odd.append(t[pl.ds(2, 32, stride=4), :] + t[pl.ds(3, 32, stride=4), :])
    rows = jnp.concatenate([jnp.concatenate(even, 0), jnp.concatenate(odd, 0)], 1)
    z, n = iota((256, 128), 0), iota((256, 128), 1)
    pool = jnp.where((z // 128) * 64 + (z % 128) // 2 == n, 0.0625, 0.0).astype(F32)
    coarse = jnp.dot(rows, pool, preferred_element_type=F32, precision=lax.Precision.HIGHEST)
    flat = pooled.at[0]
    hold = pooled.at[1]
    flat[...] = coarse[0:128]
    hold[0:64] = coarse[128:192]
    table[...] = jnp.zeros_like(table)
    for t in range(6):
        for par in range(2):
            c, inner = t // 2, (t % 2) * 2 + par
            src = flat if c < 2 else hold
            base = (c % 2) * 64
            piece = src[pl.ds(base + inner, 16, stride=4), :]
            table[par * 16 : par * 16 + 16, t * 128 : (t + 1) * 128] = piece.astype(BF16)


def tendency_plane(x, rows_of, along_a, below, above, lane):
    rows = rows_of(x)
    v, p = primitives(rows)
    fb = flux(rows, v, p, 1)
    fc = flux(rows, v, p, 2)
    out = []
    for f in range(5):
        total = along_a(x, f) + diff_y(fb[f])
        out.append(total + diff_z(fc[f], lane, below, above, f * 4 + x))
    return rows, out


def fill_flux_a(u, xbelow, xabove, fa):
    for x in range(-1, 5):
        if x == -1:
            rows = [xbelow[f] for f in range(5)]
        elif x == 4:
            rows = [xabove[f] for f in range(5)]
        else:
            rows = [u[f, x] for f in range(5)]
        v, p = primitives(rows)
        for f, t in enumerate(flux(rows, v, p, 0)):
            fa[f, x + 1] = t


def stage_one_body(u, xbelow, xabove, zbelow, zabove, first, xlo, xhi, zlo, zhi, fa):
    lane = iota((128, 128), 1)
    fill_flux_a(u, xbelow, xabove, fa)
    below, above = zbelow[...], zabove[...]
    for x in range(4):
        rows, out = tendency_plane(
            x,
            lambda x: [u[f, x] for f in range(5)],
            lambda x, f: fa[f, x + 2] - fa[f, x],
            below,
            above,
            lane,
        )
        for f in range(5):
            first[f, x] = rows[f] - (FLOW_STEP * 0.5) * out[f]
    xlo[...] = first[:, 0]
    xhi[...] = first[:, 3]

    def planes(x):
        rows = [first[f, x] for f in range(5)]
        v, p = primitives(rows)
        return flux(rows, v, p, 2)

    pack_z(planes, zlo, zhi)


def stage_two_body(u, first, xbelow, xabove, zbelow, zabove, inc, fa):
    lane = iota((128, 128), 1)
    fill_flux_a(first, xbelow, xabove, fa)
    below, above = zbelow[...], zabove[...]
    for x in range(4):
        rows, out = tendency_plane(
            x,
            lambda x: [first[f, x] for f in range(5)],
            lambda x, f: fa[f, x + 2] - fa[f, x],
            below,
            above,
            lane,
        )
        for f in range(5):
            inc[f, x] = 0.5 * ((rows[f] - u[f, x]) - (FLOW_STEP * 0.5) * out[f])


def send_body(req, table, send):
    wanted = req[...].reshape(128, 128).astype(F32).astype(BF16)
    row, col = iota((1024, 128), 0), iota((1024, 128), 1)
    spread = jnp.where(row // 8 == col, 1.0, 0.0).astype(BF16)
    rep = jnp.dot(spread, wanted, preferred_element_type=F32)
    own = jnp.where(row % 4 == col, rep, 0.0).astype(BF16)
    value = jnp.dot(own, jnp.ones((128, 128), BF16), preferred_element_type=F32)
    target = value + ((row % 8) // 4 * 16).astype(F32)
    pick = jnp.where(col.astype(F32) == target, 1.0, 0.0).astype(BF16)
    rows = jnp.dot(pick, table[...], preferred_element_type=F32)
    for u in range(3):
        a = rows[:, 256 * u : 256 * u + 128].reshape(128, 8, 128)
        b = rows[:, 256 * u + 128 : 256 * u + 256].reshape(128, 8, 128)
        send[:, 16 * u : 16 * u + 16, :] = jnp.concatenate([a, b], 1).astype(BF16)


def gather_sources(got, pick):
    tiles = []
    for u in range(3):
        t = got[:, 16 * u : 16 * u + 16, :].astype(F32)
        tiles.append(t[:, 0:8, :].reshape(1024, 128).astype(BF16))
        tiles.append(t[:, 8:16, :].reshape(1024, 128).astype(BF16))
    rhs = jnp.concatenate(tiles, 1)
    by_parity = [jnp.dot(pick[par], rhs, preferred_element_type=F32) for par in range(2)]
    out = []
    for c in range(3):
        row = []
        for j in range(4):
            t = 2 * c + j // 2
            row.append(by_parity[j % 2][:, t * 128 : (t + 1) * 128])
        out.append(jnp.concatenate(row, 1))
    return out


def prepare_body(idx, gcat, gx0, gx1, pick, esrc, edst):
    def onehot(col, width):
        return jnp.where(iota((EL, width), 1) == idx[:, col : col + 1], 1.0, 0.0).astype(BF16)

    gx0[...] = onehot(0, 2 * EL)
    gx1[...] = onehot(1, 2 * EL)
    wide = iota((EL, 4 * EL), 1)
    acc = jnp.zeros((EL, 4 * EL), jnp.bool_)
    for f in range(4):
        acc = acc | (wide == idx[:, 2 + f : 3 + f])
    gcat[...] = jnp.where(acc, 1.0, 0.0).astype(BF16)
    pick[0] = onehot(6, 1024)
    pick[1] = onehot(7, 1024)

    def node(c, flip):
        face, a, b = c // 64, c % 64 // 8, c % 8
        low = face % 2 == (1 if flip else 0)
        spot = jnp.where(low, 0, 7)
        return jnp.where(face < 2, a * 64 + spot * 8 + b, a * 64 + b * 8 + spot)

    esrc[...] = jnp.where(
        iota((512, 256), 0) == node(iota((512, 256), 1), True), 1.0, 0.0
    ).astype(BF16)
    edst[...] = jnp.where(
        iota((256, 512), 1) == node(iota((256, 512), 0), False), 1.0, 0.0
    ).astype(BF16)


def face_count():
    n = iota((1, NODES), 1)
    count = jnp.zeros((1, NODES), I32)
    for part in (n // 64, n // 8 % 8, n % 8):
        count = count + jnp.where((part == 0) | (part == 7), 1, 0)
    return count.astype(F32)


def times(a, b):
    return lax.dot_general(a, b, (((1,), (1,)), ((), ())), preferred_element_type=F32)


def local_terms(q, dx, dy, dz, gcat, esrc, edst):
    traces = jnp.dot(jnp.concatenate(q, 0), esrc[...], preferred_element_type=F32).astype(BF16)
    wide = jnp.concatenate([traces[v * EL : (v + 1) * EL] for v in range(4)], 1)
    lane = iota((1, 1024), 1) % 256 // 64
    rhs = jnp.concatenate(
        [wide * jnp.where(lane == f, 1.0, 0.0).astype(BF16) for f in range(4)], 0
    )
    got = jnp.dot(gcat[...], rhs, preferred_element_type=F32).astype(BF16)
    count = face_count()
    out = []
    for v in range(4):
        pen = jnp.dot(got[:, v * 256 : (v + 1) * 256], edst[...], preferred_element_type=F32)
        pen = pen - count * q[v].astype(F32)
        if v == 0:
            vol = times(q[1], dx[...]) + times(q[2], dy[...]) + times(q[3], dz[...])
        else:
            vol = times(q[0], (dx, dy, dz)[v - 1][...])
        out.append(pen - vol)
    return out


def cross_terms(gx0, gx1, own_lo, own_hi, below_hi, above_lo):
    lane = iota((EL, 128), 1)
    first, last = [], []
    low = jnp.concatenate(
        [jnp.concatenate([own_hi[w], below_hi[w]], 0) for w in range(2)], 1
    )
    high = jnp.concatenate(
        [jnp.concatenate([own_lo[w], above_lo[w]], 0) for w in range(2)], 1
    )
    low = jnp.dot(gx0[...], low, preferred_element_type=F32)
    high = jnp.dot(gx1[...], high, preferred_element_type=F32)
    for v in range(4):
        w = v // 2
        a = low[:, w * 128 : (w + 1) * 128]
        b = high[:, w * 128 : (w + 1) * 128]
        if v % 2 == 0:
            b = pltpu.roll(b, 64, 1)
        else:
            a = pltpu.roll(a, 64, 1)
        first.append(jnp.where(lane < 64, a, 0.0))
        last.append(jnp.where(lane < 64, 0.0, b))
    return first, last


def sound_zero_body(q, dx, dy, dz, gcat, esrc, edst, gx0, gx1, olo, ohi, bhi, alo, part):
    rounded = [q[v] for v in range(4)]
    terms = local_terms(rounded, dx, dy, dz, gcat, esrc, edst)
    first, last = cross_terms(gx0, gx1, olo, ohi, bhi, alo)
    for v in range(4):
        full_term = jnp.concatenate(
            [
                terms[v][:, 0:128] + first[v],
                terms[v][:, 128:384],
                terms[v][:, 384:512] + last[v],
            ],
            1,
        )
        part[v] = q[v].astype(F32) + SOUND_STEP * full_term


def sources_body(got, pick, part, q1, src, lo, hi):
    s = gather_sources(got, pick)
    q1[0] = part[0]
    for c in range(3):
        src[c] = s[c].astype(BF16)
        q1[1 + c] = part[1 + c] + SOUND_STEP * s[c]
    store_traces(
        [q1[v, :, 0:128] for v in range(4)],
        [q1[v, :, 384:512] for v in range(4)],
        lo,
        hi,
    )


def sound_one_body(q0, q1, src, dx, dy, dz, gcat, esrc, edst, part):
    terms = local_terms([q1[v].astype(BF16) for v in range(4)], dx, dy, dz, gcat, esrc, edst)
    for v in range(4):
        t = terms[v] if v == 0 else terms[v] + src[v - 1].astype(F32)
        part[v] = 0.75 * q0[v].astype(F32) + 0.25 * (q1[v] + SOUND_STEP * t)


def cross_body(scale, gx0, gx1, olo, ohi, bhi, alo, part, out, lo, hi):
    first, last = cross_terms(gx0, gx1, olo, ohi, bhi, alo)
    tiles = [[], []]
    for v in range(4):
        a = part[v, :, 0:128] + scale * first[v]
        b = part[v, :, 384:512] + scale * last[v]
        out[v] = part[v]
        out[v, :, 0:128] = a
        out[v, :, 384:512] = b
        tiles[0].append(a)
        tiles[1].append(b)
    store_traces(tiles[0], tiles[1], lo, hi)


def sound_two_body(q0, q2, src, dx, dy, dz, gcat, esrc, edst, part):
    terms = local_terms([q2[v].astype(BF16) for v in range(4)], dx, dy, dz, gcat, esrc, edst)
    for v in range(4):
        t = terms[v] if v == 0 else terms[v] + src[v - 1].astype(F32)
        start = q0[v].astype(F32)
        part[v] = start * (1.0 / 3.0) + (2.0 / 3.0) * (q2[v] + SOUND_STEP * t) - start


def final_body(scale, gx0, gx1, olo, ohi, bhi, alo, part, out):
    first, last = cross_terms(gx0, gx1, olo, ohi, bhi, alo)
    for v in range(4):
        out[v] = part[v]
        out[v, :, 0:128] = part[v, :, 0:128] + scale * first[v]
        out[v, :, 384:512] = part[v, :, 384:512] + scale * last[v]


def neighbour_pair(low_going, high_going, axis):
    count = lax.axis_size(axis)
    up = [(i, (i + 1) % count) for i in range(count)]
    down = [(b, a) for a, b in up]
    return lax.ppermute(high_going, axis, up), lax.ppermute(low_going, axis, down)


def local(flow_state, acoustic_state, dx, dy, dz, requests, elem_slot, neighbours):
    both = ("solver", "space")
    me = lax.axis_index("solver") * lax.axis_size("space") + lax.axis_index("space")

    wanted = jnp.pad(requests.reshape(128, 1, 4), ((0, 0), (0, 0), (0, 124)))
    wanted = lax.all_to_all(wanted, both, split_axis=0, concat_axis=0, tiled=True)

    xlo, xhi, zlo, zhi, qlo, qhi = call(
        edges_body,
        [full(5, 128, 128)] * 2 + [full(128, 128)] * 2 + [half(2, EL, 128)] * 2,
        "edges",
        (flow_state, acoustic_state),
    )
    xbelow, xabove = neighbour_pair(xlo, xhi, "space")
    zbelow, zabove = neighbour_pair(zlo, zhi, "solver")
    bhi, alo = neighbour_pair(qlo, qhi, "space")

    row = neighbours % EL
    away = (neighbours // EL != me).astype(I32) * EL
    spot = elem_slot // 4 * 8 + elem_slot % 4
    cols = [row[0] + away[0], row[1] + away[1]]
    cols += [row[2 + f] + f * EL for f in range(4)]
    cols += [spot, spot + 4]
    idx = jnp.stack(cols, axis=1)
    gcat, gx0, gx1, pick, esrc, edst = call(
        prepare_body,
        [half(EL, 4 * EL), half(EL, 2 * EL), half(EL, 2 * EL), half(2, EL, 1024), half(512, 256), half(256, 512)],
        "prepare",
        (idx,),
    )

    table = call(
        lamb_body,
        half(128, 768),
        "lamb",
        (flow_state, xbelow, xabove, zbelow, zabove),
        scratch=[pltpu.VMEM((3, 6, 128, 128), F32), pltpu.VMEM((6, 128, 128), F32)],
    )
    send = call(send_body, half(128, 48, 128), "send", (wanted, table))
    got = lax.all_to_all(send, both, split_axis=0, concat_axis=0, tiled=True)

    first, xlo, xhi, zlo, zhi = call(
        stage_one_body,
        [full(5, 4, 128, 128)] + [full(5, 128, 128)] * 2 + [full(128, 128)] * 2,
        "flow_one",
        (flow_state, xbelow, xabove, zbelow, zabove),
        scratch=[pltpu.VMEM((5, 6, 128, 128), F32)],
    )
    xbelow, xabove = neighbour_pair(xlo, xhi, "space")
    zbelow, zabove = neighbour_pair(zlo, zhi, "solver")

    mats = (dx, dy, dz, gcat, esrc, edst)
    part = call(
        sound_zero_body,
        full(4, EL, NODES),
        "sound_zero",
        (acoustic_state,) + mats + (gx0, gx1, qlo, qhi, bhi, alo),
    )
    flow_increment = call(
        stage_two_body,
        full(5, 4, 128, 128),
        "flow_two",
        (flow_state, first, xbelow, xabove, zbelow, zabove),
        scratch=[pltpu.VMEM((5, 6, 128, 128), F32)],
    )

    traces = [half(2, EL, 128)] * 2
    q1, src, qlo, qhi = call(
        sources_body,
        [full(4, EL, NODES), half(3, EL, NODES)] + traces,
        "sources",
        (got, pick, part),
    )
    bhi, alo = neighbour_pair(qlo, qhi, "space")
    part = call(sound_one_body, full(4, EL, NODES), "sound_one", (acoustic_state, q1, src) + mats)
    q2, qlo2, qhi2 = call(
        lambda *r: cross_body(0.25 * SOUND_STEP, *r),
        [full(4, EL, NODES)] + traces,
        "cross_one",
        (gx0, gx1, qlo, qhi, bhi, alo, part),
    )
    bhi, alo = neighbour_pair(qlo2, qhi2, "space")
    part = call(sound_two_body, full(4, EL, NODES), "sound_two", (acoustic_state, q2, src) + mats)
    out = call(
        lambda *r: final_body(2.0 / 3.0 * SOUND_STEP, *r),
        full(4, EL, NODES),
        "cross_two",
        (gx0, gx1, qlo2, qhi2, bhi, alo, part),
    )
    return flow_increment, out


def solution(mesh):
    both = ("solver", "space")
    grid = P(None, "space", None, "solver")
    sound = P(None, both, None)
    in_specs = (grid, sound, P(), P(), P(), P(both, None, None), P(both), P(None, both))
    return jax.shard_map(
        local, mesh=mesh, in_specs=in_specs, out_specs=(grid, sound), check_vma=False
    )
```

```python
import jax
import jax.numpy as jnp
from jax import lax
from jax.experimental import pallas as pl
from jax.experimental.pallas import tpu as pltpu
from jax.sharding import PartitionSpec as P

F32 = jnp.float32
BF16 = jnp.bfloat16
I32 = jnp.int32

EL = 224
NODES = 512
FLOW_STEP = 0.2
SOUND_STEP = 0.2
VMEM_LIMIT = 20 * 1024 * 1024


def iota(shape, dim):
    return lax.broadcasted_iota(I32, shape, dim)


def full(*shape):
    return jax.ShapeDtypeStruct(shape, F32)


def half(*shape):
    return jax.ShapeDtypeStruct(shape, BF16)


def call(body, outs, name, args, scratch=(), aliases=None, far=(), far_out=()):
    space = [pl.BlockSpec(memory_space=pltpu.VMEM), pl.BlockSpec(memory_space=pltpu.HBM)]
    many = isinstance(outs, (list, tuple))
    outs = list(outs) if many else [outs]
    out_specs = [space[i in far_out] for i in range(len(outs))]
    outs = [pltpu.HBM(t.shape, t.dtype) if i in far_out else t for i, t in enumerate(outs)]
    args = [
        pltpu.with_memory_space_constraint(t, pltpu.HBM) if i in far else t
        for i, t in enumerate(args)
    ]
    return pl.pallas_call(
        body,
        out_shape=outs if many else outs[0],
        in_specs=[space[i in far] for i in range(len(args))],
        out_specs=out_specs if many else out_specs[0],
        scratch_shapes=list(scratch),
        name=name,
        input_output_aliases=aliases or {},
        compiler_params=pltpu.CompilerParams(vmem_limit_bytes=VMEM_LIMIT),
    )(*args)


def begin(sems, first, *pairs):
    out = []
    for i, (source, target) in enumerate(pairs):
        copy = pltpu.make_async_copy(source, target, sems.at[first + i])
        copy.start()
        out.append(copy)
    return out


def finish(copies):
    for copy in copies:
        copy.wait()


def dma(n):
    return pltpu.SemaphoreType.DMA((n,))


def primitives(rows):
    inv = 1.0 / rows[0]
    v1, v2, v3 = rows[1] * inv, rows[2] * inv, rows[3] * inv
    p = 0.4 * (rows[4] - 0.5 * (rows[1] * v1 + rows[2] * v2 + rows[3] * v3))
    return (v1, v2, v3), p


def flux(rows, v, p, k):
    along = v[k]
    out = [rows[1 + k]]
    for c in range(3):
        t = rows[1 + c] * along
        out.append(t + p if c == k else t)
    out.append((rows[4] + p) * along)
    return out


def roll_y(f, step):
    return pltpu.roll(f, step % f.shape[0], 0)


def roll_z(f, step):
    return pltpu.roll(f, step % f.shape[1], 1)


def put_lane(acc, lane, f, source, target):
    return jnp.where(lane == target, roll_z(f, target - source), acc)


def diff_y(f):
    return roll_y(f, -1) - roll_y(f, 1)


def diff_z(f, lane, below, above, slot):
    up = jnp.where(lane == 127, roll_z(above, 127 - slot), roll_z(f, -1))
    down = jnp.where(lane == 0, roll_z(below, -slot), roll_z(f, 1))
    return up - down


def add_columns(x, fields, lane, lo, hi):
    for f, field in enumerate(fields):
        slot = f * 4 + x
        lo = put_lane(lo, lane, field, 0, slot)
        hi = put_lane(hi, lane, field, 127, slot)
    return lo, hi


def pair_lanes(tiles, upper):
    lane = iota((EL, 128), 1)
    out = []
    for w in range(2):
        a, b = tiles[2 * w], tiles[2 * w + 1]
        if upper:
            out.append(jnp.where(lane < 64, pltpu.roll(a, 64, 1), b))
        else:
            out.append(jnp.where(lane < 64, a, pltpu.roll(b, 64, 1)))
    return out


def store_traces(first_tiles, last_tiles, lo_ref, hi_ref):
    for w, t in enumerate(pair_lanes(first_tiles, False)):
        lo_ref[w] = t.astype(BF16)
    for w, t in enumerate(pair_lanes(last_tiles, True)):
        hi_ref[w] = t.astype(BF16)


def edges_body(u, req, xlo, xhi, zlo, zhi, want, mid, sems):
    copies = begin(
        sems,
        0,
        (u.at[:, 0], xlo),
        (u.at[:, 3], xhi),
        (u.at[:, 1], mid.at[0]),
        (u.at[:, 2], mid.at[1]),
    )
    eye = iota((128, 128), 0) == iota((128, 128), 1)
    value = req[...].astype(F32)
    spread = [jnp.where(eye, value[c : c + 1], 0.0).astype(BF16) for c in range(4)]
    place = jnp.where(iota((512, 128), 0) // 128 == iota((512, 128), 1), 1.0, 0.0).astype(BF16)
    turned = jnp.dot(jnp.concatenate(spread, 1), place, preferred_element_type=F32)
    want[...] = turned.reshape(128, 1, 128)
    lane = iota((128, 128), 1)
    lo = hi = jnp.zeros((128, 128), F32)
    for x, plane, copy in ((0, xlo, 0), (3, xhi, 1), (1, mid.at[0], 2), (2, mid.at[1], 3)):
        copies[copy].wait()
        rows = [plane[f] for f in range(5)]
        v, p = primitives(rows)
        lo, hi = add_columns(x, flux(rows, v, p, 2) + [v[0], v[1]], lane, lo, hi)
    zlo[...] = lo
    zhi[...] = hi


def lamb_body(u, xbelow, xabove, zbelow, zabove, table, vel, pooled):
    lane = iota((128, 128), 1)
    for x in range(-1, 5):
        if x == -1:
            r, m = xbelow[0], [xbelow[c] for c in (1, 2, 3)]
        elif x == 4:
            r, m = xabove[0], [xabove[c] for c in (1, 2, 3)]
        else:
            r, m = u[0, x], [u[c, x] for c in (1, 2, 3)]
        inv = 1.0 / r
        for c in range(3):
            vel[c, x + 1] = m[c] * inv
    below, above = zbelow[...], zabove[...]
    for pair in range(2):
        total = None
        for x in (2 * pair, 2 * pair + 1):
            v1, v2, v3 = vel[0, x + 1], vel[1, x + 1], vel[2, x + 1]
            w1 = diff_y(v3) - diff_z(v2, lane, below, above, 24 + x)
            w2 = diff_z(v1, lane, below, above, 20 + x) - (vel[2, x + 2] - vel[2, x])
            w3 = (vel[1, x + 2] - vel[1, x]) - diff_y(v1)
            lamb = [w2 * v3 - w3 * v2, w3 * v1 - w1 * v3, w1 * v2 - w2 * v1]
            total = lamb if total is None else [a + b for a, b in zip(total, lamb)]
        for c in range(3):
            pooled[c * 2 + pair] = total[c]
    even, odd = [], []
    for c in range(6):
        t = pooled.at[c]
        even.append(t[pl.ds(0, 32, stride=4), :] + t[pl.ds(1, 32, stride=4), :])
        odd.append(t[pl.ds(2, 32, stride=4), :] + t[pl.ds(3, 32, stride=4), :])
    rows = jnp.concatenate([jnp.concatenate(even, 0), jnp.concatenate(odd, 0)], 1)
    z, n = iota((256, 128), 0), iota((256, 128), 1)
    pool = jnp.where((z // 128) * 64 + (z % 128) // 2 == n, 0.0625, 0.0).astype(F32)
    coarse = jnp.dot(rows, pool, preferred_element_type=F32, precision=lax.Precision.HIGHEST)
    flat = pooled.at[0]
    hold = pooled.at[1]
    flat[...] = coarse[0:128]
    hold[0:64] = coarse[128:192]
    table[...] = jnp.zeros_like(table)
    for t in range(6):
        for par in range(2):
            c, inner = t // 2, (t % 2) * 2 + par
            src = flat if c < 2 else hold
            base = (c % 2) * 64
            piece = src[pl.ds(base + inner, 16, stride=4), :]
            table[par * 16 : par * 16 + 16, t * 128 : (t + 1) * 128] = piece.astype(BF16)


def tendency_plane(x, rows_of, along_a, below, above, lane):
    rows = rows_of(x)
    v, p = primitives(rows)
    fb = flux(rows, v, p, 1)
    fc = flux(rows, v, p, 2)
    out = []
    for f in range(5):
        total = along_a(x, f) + diff_y(fb[f])
        out.append(total + diff_z(fc[f], lane, below, above, f * 4 + x))
    return rows, out


def fill_flux_a(u, xbelow, xabove, fa, planes=range(-1, 5)):
    for x in planes:
        if x == -1:
            rows = [xbelow[f] for f in range(5)]
        elif x == 4:
            rows = [xabove[f] for f in range(5)]
        else:
            rows = [u[f, x] for f in range(5)]
        v, p = primitives(rows)
        for f, t in enumerate(flux(rows, v, p, 0)):
            fa[f, x + 1] = t


def stage_one_body(u, xbelow, xabove, zbelow, zabove, first, xlo, xhi, zlo, zhi, fa, hold, zpack, halo, zhalo, sems):
    lane = iota((128, 128), 1)
    fetch = begin(
        sems, 8, (xbelow, halo.at[0]), (xabove, halo.at[1]), (zbelow, zhalo.at[0]), (zabove, zhalo.at[1])
    )
    fill_flux_a(u, None, None, fa, range(4))
    finish(fetch)
    fill_flux_a(u, halo.at[0], halo.at[1], fa, (-1, 4))
    below, above = zhalo[0], zhalo[1]
    lo = hi = jnp.zeros((128, 128), F32)
    copies = []
    for i, x in enumerate((0, 3, 1, 2)):
        rows, out = tendency_plane(
            x,
            lambda x: [u[f, x] for f in range(5)],
            lambda x, f: fa[f, x + 2] - fa[f, x],
            below,
            above,
            lane,
        )
        now = [rows[f] - (FLOW_STEP * 0.5) * out[f] for f in range(5)]
        for f in range(5):
            hold[x, f] = now[f]
        copies += begin(sems, i, (hold.at[x], first.at[:, x]))
        if x in (0, 3):
            copies += begin(sems, 4 + i, (hold.at[x], xhi if x else xlo))
        v, p = primitives(now)
        lo, hi = add_columns(x, flux(now, v, p, 2), lane, lo, hi)
    zpack[0] = lo
    zpack[1] = hi
    copies += begin(sems, 6, (zpack.at[0], zlo), (zpack.at[1], zhi))
    finish(copies)


def stage_two_body(u, first, xbelow, xabove, zbelow, zabove, inc, fa, hold, sems):
    lane = iota((128, 128), 1)
    fill_flux_a(first, xbelow, xabove, fa)
    below, above = zbelow[...], zabove[...]
    copies = []
    for x in range(4):
        rows, out = tendency_plane(
            x,
            lambda x: [first[f, x] for f in range(5)],
            lambda x, f: fa[f, x + 2] - fa[f, x],
            below,
            above,
            lane,
        )
        for f in range(5):
            hold[x, f] = 0.5 * ((rows[f] - u[f, x]) - (FLOW_STEP * 0.5) * out[f])
        copies += begin(sems, x, (hold.at[x], inc.at[:, x]))
    finish(copies)


def send_body(req, table, send, hold, sems):
    wanted = req[...].reshape(128, 128).astype(BF16)
    row, col = iota((1024, 128), 0), iota((1024, 128), 1)
    spread = jnp.where(row // 8 == col, 1.0, 0.0).astype(BF16)
    rep = jnp.dot(spread, wanted, preferred_element_type=F32)
    own = jnp.where(row % 4 == col, rep, 0.0).astype(BF16)
    value = jnp.dot(own, jnp.ones((128, 128), BF16), preferred_element_type=F32)
    target = value + ((row % 8) // 4 * 16).astype(F32)
    pick = jnp.where(col.astype(F32) == target, 1.0, 0.0).astype(BF16)
    copies = []
    for u in range(3):
        rows = jnp.dot(pick, table[:, 256 * u : 256 * u + 256], preferred_element_type=F32)
        a = rows[:, 0:128].reshape(128, 8, 128)
        b = rows[:, 128:256].reshape(128, 8, 128)
        hold[u] = jnp.concatenate([a, b], 1).astype(BF16)
        copies += begin(sems, u, (hold.at[u], send.at[:, 16 * u : 16 * u + 16, :]))
    finish(copies)


def gather_source(got, pick):
    t = got[...].astype(F32)
    rhs = jnp.concatenate(
        [
            t[:, 0:8, :].reshape(1024, 128).astype(BF16),
            t[:, 8:16, :].reshape(1024, 128).astype(BF16),
        ],
        1,
    )
    even = jnp.dot(pick[0], rhs, preferred_element_type=F32)
    odd = jnp.dot(pick[1], rhs, preferred_element_type=F32)
    return jnp.concatenate([even[:, 0:128], odd[:, 0:128], even[:, 128:256], odd[:, 128:256]], 1)


def prepare_body(nb, slot, q, gcat, gx0, gx1, pick, esrc, edst, qlo, qhi, *scratch):
    gcat_v, gx0_v, gx1_v, pick_v, esrc_v, edst_v, ends, packs, sems = scratch
    fetch = begin(sems, 0, (q.at[:, :, 0:128], ends.at[0]), (q.at[:, :, 384:512], ends.at[1]))
    me = lax.axis_index("solver") * lax.axis_size("space") + lax.axis_index("space")
    owner, row = nb[...] // EL, nb[...] % EL
    away = jnp.where(owner == me, 0, EL)
    spot = slot[...] // 4 * 8 + slot[...] % 4
    cols = [row[f : f + 1] + away[f : f + 1] for f in range(2)]
    cols += [row[f : f + 1] for f in range(2, 6)] + [spot]
    eye = iota((EL, EL), 0) == iota((EL, EL), 1)
    spread = [jnp.where(eye, c.astype(F32), 0.0) for c in cols]
    coarse = [jnp.floor(t * (1.0 / 32.0)) for t in spread]
    fine = [t - 32.0 * c for t, c in zip(spread, coarse)]
    ones = jnp.ones((EL, 128), BF16)
    coarse = jnp.dot(jnp.concatenate(coarse, 0).astype(BF16), ones, preferred_element_type=F32)
    fine = jnp.dot(jnp.concatenate(fine, 0).astype(BF16), ones, preferred_element_type=F32)
    column = 32.0 * coarse + fine
    lane = iota((EL, 128), 1).astype(F32)

    def onehot(ref, col, width, shift=0.0):
        number = column[col * EL : (col + 1) * EL] + shift
        for t in range(0, width, 128):
            n = min(128, width - t)
            hit = jnp.where(lane + t == number, 1.0, 0.0).astype(BF16)
            ref[:, t : t + n] = hit[:, :n]

    onehot(gx0_v, 0, 2 * EL)
    onehot(gx1_v, 1, 2 * EL)
    copies = begin(sems, 2, (gx0_v, gx0), (gx1_v, gx1))
    for t in range(0, 4 * EL, 128):
        hit = jnp.zeros((EL, 128), jnp.bool_)
        for f in range(4):
            hit = hit | (lane + t == column[(2 + f) * EL : (3 + f) * EL] + f * EL)
        gcat_v[:, t : t + 128] = jnp.where(hit, 1.0, 0.0).astype(BF16)
    copies += begin(sems, 4, (gcat_v, gcat))
    onehot(pick_v.at[0], 6, 1024)
    onehot(pick_v.at[1], 6, 1024, 4.0)
    copies += begin(sems, 5, (pick_v, pick))
    finish(fetch)
    store_traces(
        [ends[0, v].astype(F32) for v in range(4)], [ends[1, v].astype(F32) for v in range(4)], packs.at[0], packs.at[1]
    )
    copies += begin(sems, 8, (packs.at[0], qlo), (packs.at[1], qhi))

    def node(c, flip):
        face, a, b = c // 64, c % 64 // 8, c % 8
        low = face % 2 == (1 if flip else 0)
        spot = jnp.where(low, 0, 7)
        return jnp.where(face < 2, a * 64 + spot * 8 + b, a * 64 + b * 8 + spot)

    esrc_v[...] = jnp.where(
        iota((512, 256), 0) == node(iota((512, 256), 1), True), 1.0, 0.0
    ).astype(BF16)
    edst_v[...] = jnp.where(
        iota((256, 512), 1) == node(iota((256, 512), 0), False), 1.0, 0.0
    ).astype(BF16)
    copies += begin(sems, 6, (esrc_v, esrc), (edst_v, edst))
    finish(copies)


def lamb_and_prepare_body(u, xb, xa, zb, za, nb, slot, q, table, *rest):
    vel, pooled = rest[8:10]
    lamb_body(u, xb, xa, zb, za, table, vel, pooled)
    prepare_body(nb, slot, q, *rest[:8], *rest[10:])


def face_count():
    n = iota((1, NODES), 1)
    count = jnp.zeros((1, NODES), I32)
    for part in (n // 64, n // 8 % 8, n % 8):
        count = count + jnp.where((part == 0) | (part == 7), 1, 0)
    return count.astype(F32)


def times(a, b):
    return lax.dot_general(a, b, (((1,), (1,)), ((), ())), preferred_element_type=F32)


def local_terms(q, dx, dy, dz, gcat, esrc, edst, ready=lambda *refs: None):
    traces = jnp.dot(jnp.concatenate(q, 0), esrc[...], preferred_element_type=F32).astype(BF16)
    wide = jnp.concatenate([traces[v * EL : (v + 1) * EL] for v in range(4)], 1)
    lane = iota((1, 1024), 1) % 256 // 64
    rhs = jnp.concatenate(
        [wide * jnp.where(lane == f, 1.0, 0.0).astype(BF16) for f in range(4)], 0
    )
    ready(gcat, edst)
    got = jnp.dot(gcat[...], rhs, preferred_element_type=F32).astype(BF16)
    count = face_count()
    out = []
    ready(dx, dy, dz)
    for v in range(4):
        pen = jnp.dot(got[:, v * 256 : (v + 1) * 256], edst[...], preferred_element_type=F32)
        pen = pen - count * q[v].astype(F32)
        if v == 0:
            vol = times(q[1], dx[...]) + times(q[2], dy[...]) + times(q[3], dz[...])
        else:
            vol = times(q[0], (dx, dy, dz)[v - 1][...])
        out.append(pen - vol)
    return out


def cross_terms(gx0, gx1, own_lo, own_hi, below_hi, above_lo):
    lane = iota((EL, 128), 1)
    first, last = [], []
    low = jnp.concatenate(
        [jnp.concatenate([own_hi[w], below_hi[w]], 0) for w in range(2)], 1
    )
    high = jnp.concatenate(
        [jnp.concatenate([own_lo[w], above_lo[w]], 0) for w in range(2)], 1
    )
    low = jnp.dot(gx0[...], low, preferred_element_type=F32)
    high = jnp.dot(gx1[...], high, preferred_element_type=F32)
    for v in range(4):
        w = v // 2
        a = low[:, w * 128 : (w + 1) * 128]
        b = high[:, w * 128 : (w + 1) * 128]
        if v % 2 == 0:
            b = pltpu.roll(b, 64, 1)
        else:
            a = pltpu.roll(a, 64, 1)
        first.append(jnp.where(lane < 64, a, 0.0))
        last.append(jnp.where(lane < 64, 0.0, b))
    return first, last


def sound_zero_body(*refs):
    given, (bhi, alo, part, *here), (hold, sems) = refs[:11], refs[11:25], refs[25:]
    coming = {id(to): copy for to, copy in zip(here, begin(sems, 4, *zip(given, here)))}
    ready = lambda *names: finish([coming[id(t)] for t in names])
    q, esrc, gcat, edst, dx, dy, dz, gx0, gx1, olo, ohi = here
    ready(q, esrc)
    rounded = [q[v] for v in range(4)]
    terms = local_terms(rounded, dx, dy, dz, gcat, esrc, edst, ready)
    ready(gx0, gx1, olo, ohi)
    first, last = cross_terms(gx0, gx1, olo, ohi, bhi, alo)
    copies = []
    for v in range(4):
        full_term = jnp.concatenate(
            [
                terms[v][:, 0:128] + first[v],
                terms[v][:, 128:384],
                terms[v][:, 384:512] + last[v],
            ],
            1,
        )
        hold[v] = q[v].astype(F32) + SOUND_STEP * full_term
        copies += begin(sems, v, (hold.at[v], part.at[v]))
    finish(copies)


def sources_body(got, pick, part, after, q1, src, lo, hi, pick_v, part_v, sems):
    copies = begin(
        sems,
        0,
        (pick, pick_v),
        (part.at[0], q1.at[0]),
        *[(part.at[v], part_v.at[v - 1]) for v in (1, 2, 3)],
    )
    copies[0].wait()
    for c in range(3):
        s = gather_source(got.at[:, 16 * c : 16 * c + 16, :], pick_v)
        src[c] = s.astype(BF16)
        copies[2 + c].wait()
        q1[1 + c] = part_v[c] + SOUND_STEP * s
    copies[1].wait()
    store_traces(
        [q1[v, :, 0:128] for v in range(4)],
        [q1[v, :, 384:512] for v in range(4)],
        lo,
        hi,
    )


def sound_one_body(q0, q1, src, dx, dy, dz, gcat, esrc, edst, part):
    terms = local_terms([q1[v].astype(BF16) for v in range(4)], dx, dy, dz, gcat, esrc, edst)
    for v in range(4):
        t = terms[v] if v == 0 else terms[v] + src[v - 1].astype(F32)
        part[v] = 0.75 * q0[v].astype(F32) + 0.25 * (q1[v] + SOUND_STEP * t)


def cross_body(scale, gx0, gx1, olo, ohi, bhi, alo, part, ends, lo, hi):
    first, last = cross_terms(gx0, gx1, olo, ohi, bhi, alo)
    tiles = [[], []]
    for v in range(4):
        a = part[v, :, 0:128] + scale * first[v]
        b = part[v, :, 384:512] + scale * last[v]
        ends[0, v] = a
        ends[1, v] = b
        tiles[0].append(a)
        tiles[1].append(b)
    store_traces(tiles[0], tiles[1], lo, hi)


def sound_two_body(q0, mid, ends, src, dx, dy, dz, gcat, esrc, edst, out, rest, hold, sems):
    q2 = [jnp.concatenate([ends[0, v], mid[v, :, 128:384], ends[1, v]], 1) for v in range(4)]
    terms = local_terms([t.astype(BF16) for t in q2], dx, dy, dz, gcat, esrc, edst)
    copies = []
    for v in range(4):
        t = terms[v] if v == 0 else terms[v] + src[v - 1].astype(F32)
        start = q0[v].astype(F32)
        t = start * (1.0 / 3.0) + (2.0 / 3.0) * (q2[v] + SOUND_STEP * t) - start
        hold[v] = t[:, 128:384]
        rest[0, v] = t[:, 0:128]
        rest[1, v] = t[:, 384:512]
        copies += begin(sems, v, (hold.at[v], out.at[v, :, 128:384]))
    finish(copies)


def final_body(scale, gx0, gx1, olo, ohi, bhi, alo, rest, given, out, hold, sems):
    first, last = cross_terms(gx0, gx1, olo, ohi, bhi, alo)
    copies = []
    for v in range(4):
        hold[0, v] = rest[0, v] + scale * first[v]
        hold[1, v] = rest[1, v] + scale * last[v]
        copies += begin(
            sems, 2 * v, (hold.at[0, v], out.at[v, :, 0:128]), (hold.at[1, v], out.at[v, :, 384:512])
        )
    finish(copies)


def neighbour_pair(low_going, high_going, axis):
    count = lax.axis_size(axis)
    up = [(i, (i + 1) % count) for i in range(count)]
    down = [(b, a) for a, b in up]
    return lax.ppermute(high_going, axis, up), lax.ppermute(low_going, axis, down)


def local(flow_state, acoustic_state, dx, dy, dz, requests, elem_slot, neighbours):
    both = ("solver", "space")
    grid = full(5, 4, 128, 128)
    plane, column = full(5, 128, 128), full(128, 128)
    state = full(4, EL, NODES)
    traces = [half(2, EL, 128)] * 2
    keep = lambda *shape: pltpu.VMEM(shape, F32)
    keep_half = lambda *shape: pltpu.VMEM(shape, BF16)

    xlo, xhi, zlo, zhi, wanted = call(
        edges_body,
        [plane, plane, column, column, full(128, 1, 128)],
        "edges",
        (flow_state, requests.reshape(128, 4).T),
        scratch=[keep(2, 5, 128, 128), dma(4)],
        far=(0,),
    )
    xbelow, xabove = neighbour_pair(xlo, xhi, "space")
    zbelow, zabove = neighbour_pair(zlo, zhi, "solver")
    wanted = lax.all_to_all(wanted, both, split_axis=0, concat_axis=0, tiled=True)

    shapes = [(EL, 4 * EL), (EL, 2 * EL), (EL, 2 * EL), (2, EL, 1024), (512, 256), (256, 512)]
    table, gcat, gx0, gx1, pick, esrc, edst, qlo, qhi = call(
        lamb_and_prepare_body,
        [half(128, 768)] + [half(*t) for t in shapes] + traces,
        "lamb",
        (flow_state, xbelow, xabove, zbelow, zabove, neighbours, elem_slot.reshape(1, EL), acoustic_state),
        scratch=[keep(3, 6, 128, 128), keep(6, 128, 128)]
        + [keep_half(*t) for t in shapes]
        + [keep_half(2, 4, EL, 128), keep_half(2, 2, EL, 128), dma(10)],
        far=(7,),
        far_out=range(1, 9),
    )
    bhi, alo = neighbour_pair(qlo, qhi, "space")
    first, xlo, xhi, zlo, zhi = call(
        stage_one_body,
        [grid, plane, plane, column, column],
        "flow_one",
        (flow_state, xbelow, xabove, zbelow, zabove),
        scratch=[keep(5, 6, 128, 128), keep(4, 5, 128, 128), keep(2, 128, 128), keep(2, 5, 128, 128), keep(2, 128, 128), dma(12)],
        far=(1, 2, 3, 4),
        far_out=range(5),
    )
    send = call(
        send_body,
        half(128, 48, 128),
        "send",
        (wanted, table),
        scratch=[keep_half(3, 128, 16, 128), dma(3)],
        far_out=(0,),
    )
    got = lax.all_to_all(send, both, split_axis=0, concat_axis=0, tiled=True)

    xbelow, xabove = neighbour_pair(xlo, xhi, "space")
    zbelow, zabove = neighbour_pair(zlo, zhi, "solver")
    mats = (dx, dy, dz, gcat, esrc, edst)
    given = (acoustic_state, esrc, gcat, edst, dx, dy, dz, gx0, gx1, qlo, qhi)
    part = call(
        sound_zero_body,
        state,
        "sound_zero",
        given + (bhi, alo),
        scratch=[keep_half(*t.shape) for t in given] + [keep(4, EL, NODES), dma(15)],
        far=range(11),
        far_out=(0,),
    )
    flow_increment = call(
        stage_two_body,
        grid,
        "flow_two",
        (flow_state, first, xbelow, xabove, zbelow, zabove),
        scratch=[keep(5, 6, 128, 128), keep(4, 5, 128, 128), dma(4)],
        far_out=(0,),
    )

    q1, src, qlo, qhi = call(
        sources_body,
        [state, half(3, EL, NODES)] + traces,
        "sources",
        (got, pick, part, flow_increment),
        scratch=[keep_half(2, EL, 1024), keep(3, EL, NODES), dma(5)],
        far=(1, 2, 3),
    )
    bhi, alo = neighbour_pair(qlo, qhi, "space")
    part = call(sound_one_body, state, "sound_one", (acoustic_state, q1, src) + mats)
    ends, qlo, qhi = call(
        lambda *r: cross_body(0.25 * SOUND_STEP, *r),
        [full(2, 4, EL, 128)] + traces,
        "cross_one",
        (gx0, gx1, qlo, qhi, bhi, alo, part),
    )
    bhi, alo = neighbour_pair(qlo, qhi, "space")
    out, rest = call(
        sound_two_body,
        [state, full(2, 4, EL, 128)],
        "sound_two",
        (acoustic_state, part, ends, src) + mats,
        scratch=[keep(4, EL, 256), dma(4)],
        far_out=(0,),
    )
    out = call(
        lambda *r: final_body(2.0 / 3.0 * SOUND_STEP, *r),
        state,
        "cross_two",
        (gx0, gx1, qlo, qhi, bhi, alo, rest, out),
        scratch=[keep(2, 4, EL, 128), dma(8)],
        far=(7,),
        far_out=(0,),
        aliases={7: 0},
    )
    return flow_increment, out


def solution(mesh):
    both = ("solver", "space")
    grid = P(None, "space", None, "solver")
    sound = P(None, both, None)
    in_specs = (grid, sound, P(), P(), P(), P(both, None, None), P(both), P(None, both))
    return jax.shard_map(
        local, mesh=mesh, in_specs=in_specs, out_specs=(grid, sound), check_vma=False
    )
```

```python
import jax
import jax.numpy as jnp
from jax import lax
from jax.experimental import pallas as pl
from jax.experimental.pallas import tpu as pltpu
from jax.sharding import PartitionSpec as P

F32 = jnp.float32
BF16 = jnp.bfloat16
I32 = jnp.int32

EL = 224
NODES = 512
FLOW_STEP = 0.2
SOUND_STEP = 0.2
VMEM_LIMIT = 20 * 1024 * 1024


def iota(shape, dim):
    return lax.broadcasted_iota(I32, shape, dim)


def full(*shape):
    return jax.ShapeDtypeStruct(shape, F32)


def half(*shape):
    return jax.ShapeDtypeStruct(shape, BF16)


def call(body, outs, name, args, scratch=(), aliases=None, far=(), far_out=()):
    space = [pl.BlockSpec(memory_space=pltpu.VMEM), pl.BlockSpec(memory_space=pltpu.HBM)]
    many = isinstance(outs, (list, tuple))
    outs = list(outs) if many else [outs]
    out_specs = [space[i in far_out] for i in range(len(outs))]
    outs = [pltpu.HBM(t.shape, t.dtype) if i in far_out else t for i, t in enumerate(outs)]
    args = [
        pltpu.with_memory_space_constraint(t, pltpu.HBM) if i in far else t
        for i, t in enumerate(args)
    ]
    return pl.pallas_call(
        body,
        out_shape=outs if many else outs[0],
        in_specs=[space[i in far] for i in range(len(args))],
        out_specs=out_specs if many else out_specs[0],
        scratch_shapes=list(scratch),
        name=name,
        input_output_aliases=aliases or {},
        compiler_params=pltpu.CompilerParams(vmem_limit_bytes=VMEM_LIMIT),
    )(*args)


def begin(sems, first, *pairs):
    out = []
    for i, (source, target) in enumerate(pairs):
        copy = pltpu.make_async_copy(source, target, sems.at[first + i])
        copy.start()
        out.append(copy)
    return out


def finish(copies):
    for copy in copies:
        copy.wait()


def is_even(axis):
    return lax.rem(lax.axis_index(axis), 2) == 0


def dma(n):
    return pltpu.SemaphoreType.DMA((n,))


def primitives(rows):
    inv = 1.0 / rows[0]
    v1, v2, v3 = rows[1] * inv, rows[2] * inv, rows[3] * inv
    p = 0.4 * (rows[4] - 0.5 * (rows[1] * v1 + rows[2] * v2 + rows[3] * v3))
    return (v1, v2, v3), p


def flux(rows, v, p, k):
    along = v[k]
    out = [rows[1 + k]]
    for c in range(3):
        t = rows[1 + c] * along
        out.append(t + p if c == k else t)
    out.append((rows[4] + p) * along)
    return out


def roll_y(f, step):
    return pltpu.roll(f, step % f.shape[0], 0)


def roll_z(f, step):
    return pltpu.roll(f, step % f.shape[1], 1)


def put_lane(acc, lane, f, source, target):
    return jnp.where(lane == target, roll_z(f, target - source), acc)


def diff_y(f):
    return roll_y(f, -1) - roll_y(f, 1)


def diff_z(f, lane, below, above, slot):
    up = jnp.where(lane == 127, roll_z(above, 127 - slot), roll_z(f, -1))
    down = jnp.where(lane == 0, roll_z(below, -slot), roll_z(f, 1))
    return up - down


def add_columns(x, fields, lane, lo, hi):
    for f, field in enumerate(fields):
        slot = f * 4 + x
        lo = put_lane(lo, lane, field, 0, slot)
        hi = put_lane(hi, lane, field, 127, slot)
    return lo, hi


def pair_lanes(tiles, upper):
    lane = iota((EL, 128), 1)
    out = []
    for w in range(2):
        a, b = tiles[2 * w], tiles[2 * w + 1]
        if upper:
            out.append(jnp.where(lane < 64, pltpu.roll(a, 64, 1), b))
        else:
            out.append(jnp.where(lane < 64, a, pltpu.roll(b, 64, 1)))
    return out


def store_traces(first_tiles, last_tiles, even_ref, odd_ref):
    lower, upper = pair_lanes(first_tiles, False), pair_lanes(last_tiles, True)
    even = is_even("space")
    for w in range(2):
        even_ref[w] = jnp.where(even, upper[w], lower[w]).astype(BF16)
        odd_ref[w] = jnp.where(even, lower[w], upper[w]).astype(BF16)


def edges_body(u, q, ue, uo, ze, zo, qe, qo, planes, ends, sems):
    even = is_even("space")
    copies = begin(
        sems,
        0,
        *[(u.at[:, x], planes.at[x]) for x in range(4)],
        (q.at[:, :, 0:128], ends.at[0]),
        (q.at[:, :, 384:512], ends.at[1]),
        (u.at[:, jnp.where(even, 3, 0)], ue),
        (u.at[:, jnp.where(even, 0, 3)], uo),
    )
    lane = iota((128, 128), 1)
    lo = hi = jnp.zeros((128, 128), F32)
    for x in range(4):
        copies[x].wait()
        rows = [planes[x, f] for f in range(5)]
        v, p = primitives(rows)
        lo, hi = add_columns(x, flux(rows, v, p, 2) + [v[0], v[1]], lane, lo, hi)
    even = is_even("solver")
    ze[...] = jnp.where(even, hi, lo)
    zo[...] = jnp.where(even, lo, hi)
    finish(copies[4:6])
    store_traces(
        [ends[0, v].astype(F32) for v in range(4)],
        [ends[1, v].astype(F32) for v in range(4)],
        qe,
        qo,
    )
    finish(copies[6:])


def lamb_body(u, xe, xo, ze, zo, table, vel, pooled):
    lane = iota((128, 128), 1)
    for x in range(4):
        inv = 1.0 / u[0, x]
        for c in range(3):
            vel[c, x + 1] = u[1 + c, x] * inv
    even = is_even("space")
    by_link = []
    for link in (xe, xo):
        inv = 1.0 / link[0]
        by_link.append([link[1 + c] * inv for c in (1, 2)])
    for c in (1, 2):
        by_even, by_odd = by_link[0][c - 1], by_link[1][c - 1]
        vel[c, 0] = jnp.where(even, by_odd, by_even)
        vel[c, 5] = jnp.where(even, by_even, by_odd)
    even = is_even("solver")
    below = jnp.where(even, zo[...], ze[...])
    above = jnp.where(even, ze[...], zo[...])
    for pair in range(2):
        total = None
        for x in (2 * pair, 2 * pair + 1):
            v1, v2, v3 = vel[0, x + 1], vel[1, x + 1], vel[2, x + 1]
            w1 = diff_y(v3) - diff_z(v2, lane, below, above, 24 + x)
            w2 = diff_z(v1, lane, below, above, 20 + x) - (vel[2, x + 2] - vel[2, x])
            w3 = (vel[1, x + 2] - vel[1, x]) - diff_y(v1)
            lamb = [w2 * v3 - w3 * v2, w3 * v1 - w1 * v3, w1 * v2 - w2 * v1]
            total = lamb if total is None else [a + b for a, b in zip(total, lamb)]
        for c in range(3):
            pooled[c * 2 + pair] = total[c]
    even, odd = [], []
    for c in range(6):
        t = pooled.at[c]
        even.append(t[pl.ds(0, 32, stride=4), :] + t[pl.ds(1, 32, stride=4), :])
        odd.append(t[pl.ds(2, 32, stride=4), :] + t[pl.ds(3, 32, stride=4), :])
    rows = jnp.concatenate([jnp.concatenate(even, 0), jnp.concatenate(odd, 0)], 1)
    z, n = iota((256, 128), 0), iota((256, 128), 1)
    pool = jnp.where((z // 128) * 64 + (z % 128) // 2 == n, 0.0625, 0.0).astype(F32)
    coarse = jnp.dot(rows, pool, preferred_element_type=F32, precision=lax.Precision.HIGHEST)
    flat = pooled.at[0]
    hold = pooled.at[1]
    flat[...] = coarse[0:128]
    hold[0:64] = coarse[128:192]
    table[...] = jnp.zeros_like(table)
    for t in range(6):
        for par in range(2):
            c, inner = t // 2, (t % 2) * 2 + par
            src = flat if c < 2 else hold
            base = (c % 2) * 64
            piece = src[pl.ds(base + inner, 16, stride=4), :]
            table[par * 16 : par * 16 + 16, t * 128 : (t + 1) * 128] = piece.astype(BF16)


def tendency_plane(x, rows_of, along_a, below, above, lane):
    rows = rows_of(x)
    v, p = primitives(rows)
    fb = flux(rows, v, p, 1)
    fc = flux(rows, v, p, 2)
    out = []
    for f in range(5):
        total = along_a(x, f) + diff_y(fb[f])
        out.append(total + diff_z(fc[f], lane, below, above, f * 4 + x))
    return rows, out


def fill_flux_a(planes, fa):
    for x, rows in planes:
        v, p = primitives(rows)
        for f, t in enumerate(flux(rows, v, p, 0)):
            fa[f, x + 1] = t


def inner_planes(u):
    return [(x, [u[f, x] for f in range(5)]) for x in range(4)]


def stage_one_body(u, ue, uo, ze, zo, first, ce, co, ye, yo, *scratch):
    fa, hold, edge, zpack, halo, zhalo, sems = scratch
    lane = iota((128, 128), 1)
    even, even_z = is_even("space"), is_even("solver")
    e, o = jnp.where(even, 1, 0), jnp.where(even, 0, 1)
    ez, oz = jnp.where(even_z, 1, 0), jnp.where(even_z, 0, 1)
    fetch = begin(
        sems, 8, (ue, halo.at[e]), (uo, halo.at[o]), (ze, zhalo.at[ez]), (zo, zhalo.at[oz])
    )
    fill_flux_a(inner_planes(u), fa)
    finish(fetch)
    fill_flux_a([(x, [halo[i, f] for f in range(5)]) for i, x in enumerate((-1, 4))], fa)
    below, above = zhalo[0], zhalo[1]
    lo = hi = jnp.zeros((128, 128), F32)
    copies = []
    for i, x in enumerate((0, 3, 1, 2)):
        rows, out = tendency_plane(
            x,
            lambda x: [u[f, x] for f in range(5)],
            lambda x, f: fa[f, x + 2] - fa[f, x],
            below,
            above,
            lane,
        )
        now = [rows[f] - (FLOW_STEP * 0.5) * out[f] for f in range(5)]
        for f in range(5):
            hold[x, f] = now[f]
        copies += begin(sems, i, (hold.at[x], first.at[:, x]))
        if x in (0, 3):
            for f in range(5):
                edge[i, f] = ((-FLOW_STEP * 0.5) * out[f]).astype(BF16)
        v, p = primitives(now)
        lo, hi = add_columns(x, flux(now, v, p, 2), lane, lo, hi)
    zpack[0] = lo
    zpack[1] = hi
    copies += begin(
        sems, 4, (edge.at[e], ce), (edge.at[o], co), (zpack.at[ez], ye), (zpack.at[oz], yo)
    )
    finish(copies)


def stage_two_body(u, first, ue, uo, ce, co, ze, zo, after, inc, *scratch):
    fa, hold, halo, sems = scratch
    lane = iota((128, 128), 1)
    even, even_z = is_even("space"), is_even("solver")
    e, o = jnp.where(even, 1, 0), jnp.where(even, 0, 1)
    fetch = begin(sems, 4, (ue, halo.at[e]), (uo, halo.at[o]))
    fill_flux_a(inner_planes(first), fa)
    finish(fetch)
    outer = []
    for i, x in enumerate((-1, 4)):
        rows = []
        for f in range(5):
            by_even, by_odd = ce[f].astype(F32), co[f].astype(F32)
            change = jnp.where(even, by_odd, by_even) if i == 0 else jnp.where(even, by_even, by_odd)
            rows.append(halo[i, f] + change)
        outer.append((x, rows))
    fill_flux_a(outer, fa)
    below = jnp.where(even_z, zo[...], ze[...])
    above = jnp.where(even_z, ze[...], zo[...])
    copies = []
    for x in range(4):
        rows, out = tendency_plane(
            x,
            lambda x: [first[f, x] for f in range(5)],
            lambda x, f: fa[f, x + 2] - fa[f, x],
            below,
            above,
            lane,
        )
        for f in range(5):
            hold[x, f] = 0.5 * ((rows[f] - u[f, x]) - (FLOW_STEP * 0.5) * out[f])
        copies += begin(sems, x, (hold.at[x], inc.at[:, x]))
    finish(copies)


def send_body(req, table, send, hold, sems):
    wanted = req[...].reshape(128, 128).astype(F32).astype(BF16)
    row, col = iota((1024, 128), 0), iota((1024, 128), 1)
    spread = jnp.where(row // 8 == col, 1.0, 0.0).astype(BF16)
    rep = jnp.dot(spread, wanted, preferred_element_type=F32)
    own = jnp.where(row % 4 == col, rep, 0.0).astype(BF16)
    value = jnp.dot(own, jnp.ones((128, 128), BF16), preferred_element_type=F32)
    target = value + ((row % 8) // 4 * 16).astype(F32)
    pick = jnp.where(col.astype(F32) == target, 1.0, 0.0).astype(BF16)
    copies = []
    for part in range(3):
        rows = jnp.dot(
            pick, table[:, 256 * part : 256 * part + 256], preferred_element_type=F32
        )
        a = rows[:, 0:128].reshape(128, 8, 128)
        b = rows[:, 128:256].reshape(128, 8, 128)
        hold[part] = jnp.concatenate([a, b], 1).astype(BF16)
        copies += begin(sems, part, (hold.at[part], send.at[:, 16 * part : 16 * part + 16, :]))
    finish(copies)


def gather_source(got, pick):
    t = got[...].astype(F32)
    rhs = jnp.concatenate(
        [
            t[:, 0:8, :].reshape(1024, 128).astype(BF16),
            t[:, 8:16, :].reshape(1024, 128).astype(BF16),
        ],
        1,
    )
    even = jnp.dot(pick[0], rhs, preferred_element_type=F32)
    odd = jnp.dot(pick[1], rhs, preferred_element_type=F32)
    return jnp.concatenate([even[:, 0:128], odd[:, 0:128], even[:, 128:256], odd[:, 128:256]], 1)


def prepare_body(nb_far, slot_far, after, gcat, ge, go, pick, esrc, edst, *scratch):
    gcat_v, gx0_v, gx1_v, pick_v, esrc_v, edst_v, nb, slot, sems = scratch
    fetch = begin(sems, 0, (nb_far, nb), (slot_far, slot))
    me = lax.axis_index("solver") * lax.axis_size("space") + lax.axis_index("space")
    finish(fetch)
    owner, row = nb[...] // EL, nb[...] % EL
    away = jnp.where(owner == me, 0, EL)
    spot = slot[...] // 4 * 8 + slot[...] % 4
    cols = [row[f : f + 1] + away[f : f + 1] for f in range(2)]
    even = is_even("space")
    cols = [jnp.where(even, cols[1], cols[0]), jnp.where(even, cols[0], cols[1])]
    cols += [row[f : f + 1] for f in range(2, 6)] + [spot]
    eye = iota((EL, EL), 0) == iota((EL, EL), 1)
    spread = [jnp.where(eye, c.astype(F32), 0.0) for c in cols]
    coarse = [jnp.floor(t * (1.0 / 32.0)) for t in spread]
    fine = [t - 32.0 * c for t, c in zip(spread, coarse)]
    ones = jnp.ones((EL, 128), BF16)
    coarse = jnp.dot(jnp.concatenate(coarse, 0).astype(BF16), ones, preferred_element_type=F32)
    fine = jnp.dot(jnp.concatenate(fine, 0).astype(BF16), ones, preferred_element_type=F32)
    column = 32.0 * coarse + fine
    lane = iota((EL, 128), 1).astype(F32)

    def onehot(ref, col, width, shift=0.0):
        number = column[col * EL : (col + 1) * EL] + shift
        for t in range(0, width, 128):
            n = min(128, width - t)
            hit = jnp.where(lane + t == number, 1.0, 0.0).astype(BF16)
            ref[:, t : t + n] = hit[:, :n]

    onehot(gx0_v, 0, 2 * EL)
    onehot(gx1_v, 1, 2 * EL)
    copies = begin(sems, 2, (gx0_v, ge), (gx1_v, go))
    for t in range(0, 4 * EL, 128):
        hit = jnp.zeros((EL, 128), jnp.bool_)
        for f in range(4):
            hit = hit | (lane + t == column[(2 + f) * EL : (3 + f) * EL] + f * EL)
        gcat_v[:, t : t + 128] = jnp.where(hit, 1.0, 0.0).astype(BF16)
    copies += begin(sems, 4, (gcat_v, gcat))
    onehot(pick_v.at[0], 6, 1024)
    onehot(pick_v.at[1], 6, 1024, 4.0)
    copies += begin(sems, 5, (pick_v, pick))

    def node(c, flip):
        face, a, b = c // 64, c % 64 // 8, c % 8
        low = face % 2 == (1 if flip else 0)
        spot = jnp.where(low, 0, 7)
        return jnp.where(face < 2, a * 64 + spot * 8 + b, a * 64 + b * 8 + spot)

    esrc_v[...] = jnp.where(
        iota((512, 256), 0) == node(iota((512, 256), 1), True), 1.0, 0.0
    ).astype(BF16)
    edst_v[...] = jnp.where(
        iota((256, 512), 1) == node(iota((256, 512), 0), False), 1.0, 0.0
    ).astype(BF16)
    copies += begin(sems, 6, (esrc_v, esrc), (edst_v, edst))
    finish(copies)


def face_count():
    n = iota((1, NODES), 1)
    count = jnp.zeros((1, NODES), I32)
    for part in (n // 64, n // 8 % 8, n % 8):
        count = count + jnp.where((part == 0) | (part == 7), 1, 0)
    return count.astype(F32)


def times(a, b):
    return lax.dot_general(a, b, (((1,), (1,)), ((), ())), preferred_element_type=F32)


def local_terms(q, dx, dy, dz, gcat, esrc, edst, ready=lambda *refs: None):
    traces = jnp.dot(jnp.concatenate(q, 0), esrc[...], preferred_element_type=F32).astype(BF16)
    wide = jnp.concatenate([traces[v * EL : (v + 1) * EL] for v in range(4)], 1)
    lane = iota((1, 1024), 1) % 256 // 64
    rhs = jnp.concatenate(
        [wide * jnp.where(lane == f, 1.0, 0.0).astype(BF16) for f in range(4)], 0
    )
    ready(gcat, edst)
    got = jnp.dot(gcat[...], rhs, preferred_element_type=F32).astype(BF16)
    count = face_count()
    out = []
    ready(dx, dy, dz)
    for v in range(4):
        pen = jnp.dot(got[:, v * 256 : (v + 1) * 256], edst[...], preferred_element_type=F32)
        pen = pen - count * q[v].astype(F32)
        if v == 0:
            vol = times(q[1], dx[...]) + times(q[2], dy[...]) + times(q[3], dz[...])
        else:
            vol = times(q[0], (dx, dy, dz)[v - 1][...])
        out.append(pen - vol)
    return out


def cross_terms(ge, go, own_e, own_o, got_e, got_o):
    lane = iota((EL, 128), 1)
    first, last = [], []
    by_even = jnp.concatenate([jnp.concatenate([own_o[w], got_e[w]], 0) for w in range(2)], 1)
    by_odd = jnp.concatenate([jnp.concatenate([own_e[w], got_o[w]], 0) for w in range(2)], 1)
    by_even = jnp.dot(ge[...], by_even, preferred_element_type=F32)
    by_odd = jnp.dot(go[...], by_odd, preferred_element_type=F32)
    even = is_even("space")
    low = jnp.where(even, by_odd, by_even)
    high = jnp.where(even, by_even, by_odd)
    for v in range(4):
        w = v // 2
        a = low[:, w * 128 : (w + 1) * 128]
        b = high[:, w * 128 : (w + 1) * 128]
        if v % 2 == 0:
            b = pltpu.roll(b, 64, 1)
        else:
            a = pltpu.roll(a, 64, 1)
        first.append(jnp.where(lane < 64, a, 0.0))
        last.append(jnp.where(lane < 64, 0.0, b))
    return first, last


def sound_zero_body(*refs):
    given, (bhi, alo, after, part, *here), (hold, sems) = refs[:11], refs[11:26], refs[26:]
    coming = {id(to): copy for to, copy in zip(here, begin(sems, 4, *zip(given, here)))}
    ready = lambda *names: finish([coming[id(t)] for t in names])
    q, esrc, gcat, edst, dx, dy, dz, gx0, gx1, olo, ohi = here
    ready(q, esrc)
    rounded = [q[v] for v in range(4)]
    terms = local_terms(rounded, dx, dy, dz, gcat, esrc, edst, ready)
    ready(gx0, gx1, olo, ohi)
    first, last = cross_terms(gx0, gx1, olo, ohi, bhi, alo)
    copies = []
    for v in range(4):
        full_term = jnp.concatenate(
            [
                terms[v][:, 0:128] + first[v],
                terms[v][:, 128:384],
                terms[v][:, 384:512] + last[v],
            ],
            1,
        )
        hold[v] = q[v].astype(F32) + SOUND_STEP * full_term
        copies += begin(sems, v, (hold.at[v], part.at[v]))
    finish(copies)


def sources_body(got, pick, part, q1, src, lo, hi, token, pick_v, part_v, token_v, sems):
    token_v[...] = jnp.zeros_like(token_v)
    copies = begin(
        sems,
        0,
        (pick, pick_v),
        (part.at[0], q1.at[0]),
        *[(part.at[v], part_v.at[v - 1]) for v in (1, 2, 3)],
        (token_v, token),
    )
    copies[0].wait()
    for c in range(3):
        s = gather_source(got.at[:, 16 * c : 16 * c + 16, :], pick_v)
        src[c] = s.astype(BF16)
        copies[2 + c].wait()
        q1[1 + c] = part_v[c] + SOUND_STEP * s
    copies[1].wait()
    copies[5].wait()
    store_traces(
        [q1[v, :, 0:128] for v in range(4)],
        [q1[v, :, 384:512] for v in range(4)],
        lo,
        hi,
    )


def sound_one_body(q0, q1, src, dx, dy, dz, gcat, esrc, edst, after, part):
    terms = local_terms([q1[v].astype(BF16) for v in range(4)], dx, dy, dz, gcat, esrc, edst)
    for v in range(4):
        t = terms[v] if v == 0 else terms[v] + src[v - 1].astype(F32)
        part[v] = 0.75 * q0[v].astype(F32) + 0.25 * (q1[v] + SOUND_STEP * t)


def cross_body(scale, gx0, gx1, olo, ohi, bhi, alo, part, ends, lo, hi):
    first, last = cross_terms(gx0, gx1, olo, ohi, bhi, alo)
    tiles = [[], []]
    for v in range(4):
        a = part[v, :, 0:128] + scale * first[v]
        b = part[v, :, 384:512] + scale * last[v]
        ends[0, v] = a
        ends[1, v] = b
        tiles[0].append(a)
        tiles[1].append(b)
    store_traces(tiles[0], tiles[1], lo, hi)


def sound_two_body(q0, mid, ends, src, dx, dy, dz, gcat, esrc, edst, out, rest, hold, sems):
    q2 = [jnp.concatenate([ends[0, v], mid[v, :, 128:384], ends[1, v]], 1) for v in range(4)]
    terms = local_terms([t.astype(BF16) for t in q2], dx, dy, dz, gcat, esrc, edst)
    copies = []
    for v in range(4):
        t = terms[v] if v == 0 else terms[v] + src[v - 1].astype(F32)
        start = q0[v].astype(F32)
        t = start * (1.0 / 3.0) + (2.0 / 3.0) * (q2[v] + SOUND_STEP * t) - start
        hold[v] = t[:, 128:384]
        rest[0, v] = t[:, 0:128]
        rest[1, v] = t[:, 384:512]
        copies += begin(sems, v, (hold.at[v], out.at[v, :, 128:384]))
    finish(copies)


def final_body(scale, gx0, gx1, olo, ohi, bhi, alo, rest, given, out, hold, sems):
    first, last = cross_terms(gx0, gx1, olo, ohi, bhi, alo)
    copies = []
    for v in range(4):
        hold[0, v] = rest[0, v] + scale * first[v]
        hold[1, v] = rest[1, v] + scale * last[v]
        copies += begin(
            sems, 2 * v, (hold.at[0, v], out.at[v, :, 0:128]), (hold.at[1, v], out.at[v, :, 384:512])
        )
    finish(copies)


def swap(even, odd, axis):
    count = lax.axis_size(axis)
    by_even = [(i, i + 1 - 2 * (i % 2)) for i in range(count)]
    by_odd = [(i, (i - 1 + 2 * (i % 2)) % count) for i in range(count)]
    other = lax.ppermute(odd, axis, by_odd)
    return lax.ppermute(even, axis, by_even), other


def local(flow_state, acoustic_state, dx, dy, dz, requests, elem_slot, neighbours):
    both = ("solver", "space")
    grid = full(5, 4, 128, 128)
    plane, column = full(5, 128, 128), full(128, 128)
    state = full(4, EL, NODES)
    traces = [half(2, EL, 128)] * 2
    keep = lambda *shape: pltpu.VMEM(shape, F32)
    keep_half = lambda *shape: pltpu.VMEM(shape, BF16)

    wanted = jnp.pad(requests.reshape(128, 1, 4), ((0, 0), (0, 0), (0, 124)))
    wanted = lax.all_to_all(wanted, both, split_axis=0, concat_axis=0, tiled=True)
    packs = call(
        edges_body,
        [plane, plane, column, column] + traces,
        "edges",
        (flow_state, acoustic_state),
        scratch=[keep(4, 5, 128, 128), keep_half(2, 4, EL, 128), dma(8)],
        far=(0, 1),
    )
    ue, uo, ze, zo, qe, qo = packs
    ue, uo = swap(ue, uo, "space")
    ze, zo = swap(ze, zo, "solver")
    got_qe, got_qo = swap(qe, qo, "space")

    table = call(
        lamb_body,
        half(128, 768),
        "lamb",
        (flow_state, ue, uo, ze, zo),
        scratch=[keep(3, 6, 128, 128), keep(6, 128, 128)],
    )
    table, got_qe, got_qo = lax.optimization_barrier((table, got_qe, got_qo))
    send = call(
        send_body,
        half(128, 48, 128),
        "send",
        (wanted, table),
        scratch=[keep_half(3, 128, 16, 128), dma(3)],
        far_out=(0,),
    )
    got = lax.all_to_all(send, both, split_axis=0, concat_axis=0, tiled=True)

    shapes = [(EL, 4 * EL), (EL, 2 * EL), (EL, 2 * EL), (2, EL, 1024), (512, 256), (256, 512)]
    gcat, ge, go, pick, esrc, edst = call(
        prepare_body,
        [half(*t) for t in shapes],
        "prepare",
        (neighbours, elem_slot.reshape(1, EL), send),
        scratch=[keep_half(*t) for t in shapes] + [pltpu.VMEM((6, EL), I32), pltpu.VMEM((1, EL), I32), dma(8)],
        far=(0, 1, 2),
        far_out=range(6),
    )
    first, ce, co, ye, yo = call(
        stage_one_body,
        [grid] + [half(5, 128, 128)] * 2 + [column, column],
        "flow_one",
        (flow_state, ue, uo, ze, zo),
        scratch=[
            keep(5, 6, 128, 128),
            keep(4, 5, 128, 128),
            keep_half(2, 5, 128, 128),
            keep(2, 128, 128),
            keep(2, 5, 128, 128),
            keep(2, 128, 128),
            dma(12),
        ],
        far=range(1, 5),
        far_out=range(5),
    )
    ce, co = swap(ce, co, "space")
    ye, yo = swap(ye, yo, "solver")

    given = (acoustic_state, esrc, gcat, edst, dx, dy, dz, ge, go, qe, qo)
    part = call(
        sound_zero_body,
        state,
        "sound_zero",
        given + (got_qe, got_qo, first),
        scratch=[keep_half(*t.shape) for t in given] + [keep(4, EL, NODES), dma(15)],
        far=[*range(11), 13],
        far_out=(0,),
    )

    q1, src, qe, qo, token = call(
        sources_body,
        [state, half(3, EL, NODES)] + traces + [full(8, 128)],
        "sources",
        (got, pick, part),
        scratch=[keep_half(2, EL, 1024), keep(3, EL, NODES), keep(8, 128), dma(6)],
        far=(1, 2),
        far_out=(4,),
    )
    mats = (dx, dy, dz, gcat, esrc, edst)
    got_qe, got_qo = swap(qe, qo, "space")
    flow_increment = call(
        stage_two_body,
        grid,
        "flow_two",
        (flow_state, first, ue, uo, ce, co, ye, yo, token),
        scratch=[keep(5, 6, 128, 128), keep(4, 5, 128, 128), keep(2, 5, 128, 128), dma(6)],
        far=(2, 3, 8),
        far_out=(0,),
    )
    part = call(
        sound_one_body,
        state,
        "sound_one",
        (acoustic_state, q1, src) + mats + (flow_increment,),
        far=(9,),
    )
    ends, qe, qo = call(
        lambda *r: cross_body(0.25 * SOUND_STEP, *r),
        [full(2, 4, EL, 128)] + traces,
        "cross_one",
        (ge, go, qe, qo, got_qe, got_qo, part),
    )
    got_qe, got_qo = swap(qe, qo, "space")
    out, rest = call(
        sound_two_body,
        [state, full(2, 4, EL, 128)],
        "sound_two",
        (acoustic_state, part, ends, src) + mats,
        scratch=[keep(4, EL, 256), dma(4)],
        far_out=(0,),
    )
    out = call(
        lambda *r: final_body(2.0 / 3.0 * SOUND_STEP, *r),
        state,
        "cross_two",
        (ge, go, qe, qo, got_qe, got_qo, rest, out),
        scratch=[keep(2, 4, EL, 128), dma(8)],
        far=(7,),
        far_out=(0,),
        aliases={7: 0},
    )
    return flow_increment, out


def solution(mesh):
    both = ("solver", "space")
    grid = P(None, "space", None, "solver")
    sound = P(None, both, None)
    in_specs = (grid, sound, P(), P(), P(), P(both, None, None), P(both), P(None, both))
    return jax.shard_map(
        local, mesh=mesh, in_specs=in_specs, out_specs=(grid, sound), check_vma=False
    )
```

```python
import jax
import jax.numpy as jnp
from jax import lax
from jax.experimental import pallas as pl
from jax.experimental.pallas import tpu as pltpu
from jax.sharding import PartitionSpec as P

F32 = jnp.float32
BF16 = jnp.bfloat16
I32 = jnp.int32

EL = 224
NODES = 512
FLOW_STEP = 0.2
SOUND_STEP = 0.2
VMEM_LIMIT = 20 * 1024 * 1024


def iota(shape, dim):
    return lax.broadcasted_iota(I32, shape, dim)


def full(*shape):
    return jax.ShapeDtypeStruct(shape, F32)


def half(*shape):
    return jax.ShapeDtypeStruct(shape, BF16)


def call(body, outs, name, args, scratch=(), aliases=None, far=(), far_out=()):
    space = [pl.BlockSpec(memory_space=pltpu.VMEM), pl.BlockSpec(memory_space=pltpu.HBM)]
    many = isinstance(outs, (list, tuple))
    outs = list(outs) if many else [outs]
    out_specs = [space[i in far_out] for i in range(len(outs))]
    outs = [pltpu.HBM(t.shape, t.dtype) if i in far_out else t for i, t in enumerate(outs)]
    args = [
        pltpu.with_memory_space_constraint(t, pltpu.HBM) if i in far else t
        for i, t in enumerate(args)
    ]
    return pl.pallas_call(
        body,
        out_shape=outs if many else outs[0],
        in_specs=[space[i in far] for i in range(len(args))],
        out_specs=out_specs if many else out_specs[0],
        scratch_shapes=list(scratch),
        name=name,
        input_output_aliases=aliases or {},
        compiler_params=pltpu.CompilerParams(vmem_limit_bytes=VMEM_LIMIT),
    )(*args)


def begin(sems, first, *pairs):
    out = []
    for i, (source, target) in enumerate(pairs):
        copy = pltpu.make_async_copy(source, target, sems.at[first + i])
        copy.start()
        out.append(copy)
    return out


def finish(copies):
    for copy in copies:
        copy.wait()


def is_even(axis):
    return lax.rem(lax.axis_index(axis), 2) == 0


def dma(n):
    return pltpu.SemaphoreType.DMA((n,))


def primitives(rows):
    inv = 1.0 / rows[0]
    v1, v2, v3 = rows[1] * inv, rows[2] * inv, rows[3] * inv
    p = 0.4 * (rows[4] - 0.5 * (rows[1] * v1 + rows[2] * v2 + rows[3] * v3))
    return (v1, v2, v3), p


def flux(rows, v, p, k):
    along = v[k]
    out = [rows[1 + k]]
    for c in range(3):
        t = rows[1 + c] * along
        out.append(t + p if c == k else t)
    out.append((rows[4] + p) * along)
    return out


def roll_y(f, step):
    return pltpu.roll(f, step % f.shape[0], 0)


def roll_z(f, step):
    return pltpu.roll(f, step % f.shape[1], 1)


def put_lane(acc, lane, f, source, target):
    return jnp.where(lane == target, roll_z(f, target - source), acc)


def diff_y(f):
    return roll_y(f, -1) - roll_y(f, 1)


def diff_z(f, lane, below, above, slot):
    up = jnp.where(lane == 127, roll_z(above, 127 - slot), roll_z(f, -1))
    down = jnp.where(lane == 0, roll_z(below, -slot), roll_z(f, 1))
    return up - down


def add_columns(x, fields, lane, lo, hi):
    for f, field in enumerate(fields):
        slot = f * 4 + x
        lo = put_lane(lo, lane, field, 0, slot)
        hi = put_lane(hi, lane, field, 127, slot)
    return lo, hi


def pair_lanes(tiles, upper):
    lane = iota((EL, 128), 1)
    out = []
    for w in range(2):
        a, b = tiles[2 * w], tiles[2 * w + 1]
        if upper:
            out.append(jnp.where(lane < 64, pltpu.roll(a, 64, 1), b))
        else:
            out.append(jnp.where(lane < 64, a, pltpu.roll(b, 64, 1)))
    return out


def store_traces(first_tiles, last_tiles, even_ref, odd_ref):
    lower, upper = pair_lanes(first_tiles, False), pair_lanes(last_tiles, True)
    even = is_even("space")
    for w in range(2):
        even_ref[w] = jnp.where(even, upper[w], lower[w]).astype(BF16)
        odd_ref[w] = jnp.where(even, lower[w], upper[w]).astype(BF16)


def edges_body(u, q, ue, uo, ze, zo, qe, qo, planes, ends, sems):
    even = is_even("space")
    copies = begin(
        sems,
        0,
        *[(u.at[:, x], planes.at[x]) for x in range(4)],
        (q.at[:, :, 0:128], ends.at[0]),
        (q.at[:, :, 384:512], ends.at[1]),
        (u.at[:, jnp.where(even, 3, 0)], ue),
        (u.at[:, jnp.where(even, 0, 3)], uo),
    )
    lane = iota((128, 128), 1)
    lo = hi = jnp.zeros((128, 128), F32)
    for x in range(4):
        copies[x].wait()
        rows = [planes[x, f] for f in range(5)]
        v, p = primitives(rows)
        lo, hi = add_columns(x, flux(rows, v, p, 2) + [v[0], v[1]], lane, lo, hi)
    even = is_even("solver")
    ze[...] = jnp.where(even, hi, lo)
    zo[...] = jnp.where(even, lo, hi)
    finish(copies[4:6])
    store_traces(
        [ends[0, v].astype(F32) for v in range(4)],
        [ends[1, v].astype(F32) for v in range(4)],
        qe,
        qo,
    )
    finish(copies[6:])


def lamb_body(u, xe, xo, ze, zo, table, vel, pooled):
    lane = iota((128, 128), 1)
    for x in range(4):
        inv = 1.0 / u[0, x]
        for c in range(3):
            vel[c, x + 1] = u[1 + c, x] * inv
    even = is_even("space")
    by_link = []
    for link in (xe, xo):
        inv = 1.0 / link[0]
        by_link.append([link[1 + c] * inv for c in (1, 2)])
    for c in (1, 2):
        by_even, by_odd = by_link[0][c - 1], by_link[1][c - 1]
        vel[c, 0] = jnp.where(even, by_odd, by_even)
        vel[c, 5] = jnp.where(even, by_even, by_odd)
    even = is_even("solver")
    below = jnp.where(even, zo[...], ze[...])
    above = jnp.where(even, ze[...], zo[...])
    for pair in range(2):
        total = None
        for x in (2 * pair, 2 * pair + 1):
            v1, v2, v3 = vel[0, x + 1], vel[1, x + 1], vel[2, x + 1]
            w1 = diff_y(v3) - diff_z(v2, lane, below, above, 24 + x)
            w2 = diff_z(v1, lane, below, above, 20 + x) - (vel[2, x + 2] - vel[2, x])
            w3 = (vel[1, x + 2] - vel[1, x]) - diff_y(v1)
            lamb = [w2 * v3 - w3 * v2, w3 * v1 - w1 * v3, w1 * v2 - w2 * v1]
            total = lamb if total is None else [a + b for a, b in zip(total, lamb)]
        for c in range(3):
            pooled[c * 2 + pair] = total[c]
    even, odd = [], []
    for c in range(6):
        t = pooled.at[c]
        even.append(t[pl.ds(0, 32, stride=4), :] + t[pl.ds(1, 32, stride=4), :])
        odd.append(t[pl.ds(2, 32, stride=4), :] + t[pl.ds(3, 32, stride=4), :])
    rows = jnp.concatenate([jnp.concatenate(even, 0), jnp.concatenate(odd, 0)], 1)
    z, n = iota((256, 128), 0), iota((256, 128), 1)
    pool = jnp.where((z // 128) * 64 + (z % 128) // 2 == n, 0.0625, 0.0).astype(F32)
    coarse = jnp.dot(rows, pool, preferred_element_type=F32, precision=lax.Precision.HIGHEST)
    flat = pooled.at[0]
    hold = pooled.at[1]
    flat[...] = coarse[0:128]
    hold[0:64] = coarse[128:192]
    table[...] = jnp.zeros_like(table)
    for t in range(6):
        for par in range(2):
            c, inner = t // 2, (t % 2) * 2 + par
            src = flat if c < 2 else hold
            base = (c % 2) * 64
            piece = src[pl.ds(base + inner, 16, stride=4), :]
            table[par * 16 : par * 16 + 16, t * 128 : (t + 1) * 128] = piece.astype(BF16)


def tendency_plane(x, rows_of, along_a, below, above, lane):
    rows = rows_of(x)
    v, p = primitives(rows)
    fb = flux(rows, v, p, 1)
    fc = flux(rows, v, p, 2)
    out = []
    for f in range(5):
        total = along_a(x, f) + diff_y(fb[f])
        out.append(total + diff_z(fc[f], lane, below, above, f * 4 + x))
    return rows, out


def fill_flux_a(planes, fa):
    for x, rows in planes:
        v, p = primitives(rows)
        for f, t in enumerate(flux(rows, v, p, 0)):
            fa[f, x + 1] = t


def inner_planes(u):
    return [(x, [u[f, x] for f in range(5)]) for x in range(4)]


def stage_one_body(u, ue, uo, ze, zo, first, ce, co, ye, yo, *scratch):
    fa, hold, edge, zpack, halo, zhalo, sems = scratch
    lane = iota((128, 128), 1)
    even, even_z = is_even("space"), is_even("solver")
    e, o = jnp.where(even, 1, 0), jnp.where(even, 0, 1)
    ez, oz = jnp.where(even_z, 1, 0), jnp.where(even_z, 0, 1)
    fetch = begin(
        sems, 8, (ue, halo.at[e]), (uo, halo.at[o]), (ze, zhalo.at[ez]), (zo, zhalo.at[oz])
    )
    fill_flux_a(inner_planes(u), fa)
    finish(fetch)
    fill_flux_a([(x, [halo[i, f] for f in range(5)]) for i, x in enumerate((-1, 4))], fa)
    below, above = zhalo[0], zhalo[1]
    lo = hi = jnp.zeros((128, 128), F32)
    copies = []
    for i, x in enumerate((0, 3, 1, 2)):
        rows, out = tendency_plane(
            x,
            lambda x: [u[f, x] for f in range(5)],
            lambda x, f: fa[f, x + 2] - fa[f, x],
            below,
            above,
            lane,
        )
        now = [rows[f] - (FLOW_STEP * 0.5) * out[f] for f in range(5)]
        for f in range(5):
            hold[x, f] = now[f]
        copies += begin(sems, i, (hold.at[x], first.at[:, x]))
        if x in (0, 3):
            for f in range(5):
                edge[i, f] = ((-FLOW_STEP * 0.5) * out[f]).astype(BF16)
        v, p = primitives(now)
        lo, hi = add_columns(x, flux(now, v, p, 2), lane, lo, hi)
    zpack[0] = lo
    zpack[1] = hi
    copies += begin(
        sems, 4, (edge.at[e], ce), (edge.at[o], co), (zpack.at[ez], ye), (zpack.at[oz], yo)
    )
    finish(copies)


def stage_two_body(u, first, ue, uo, ce, co, ze, zo, after, inc, *scratch):
    fa, hold, halo, sems = scratch
    lane = iota((128, 128), 1)
    even, even_z = is_even("space"), is_even("solver")
    e, o = jnp.where(even, 1, 0), jnp.where(even, 0, 1)
    fetch = begin(sems, 4, (ue, halo.at[e]), (uo, halo.at[o]))
    fill_flux_a(inner_planes(first), fa)
    finish(fetch)
    outer = []
    for i, x in enumerate((-1, 4)):
        rows = []
        for f in range(5):
            by_even, by_odd = ce[f].astype(F32), co[f].astype(F32)
            change = jnp.where(even, by_odd, by_even) if i == 0 else jnp.where(even, by_even, by_odd)
            rows.append(halo[i, f] + change)
        outer.append((x, rows))
    fill_flux_a(outer, fa)
    below = jnp.where(even_z, zo[...], ze[...])
    above = jnp.where(even_z, ze[...], zo[...])
    copies = []
    for x in range(4):
        rows, out = tendency_plane(
            x,
            lambda x: [first[f, x] for f in range(5)],
            lambda x, f: fa[f, x + 2] - fa[f, x],
            below,
            above,
            lane,
        )
        for f in range(5):
            hold[x, f] = 0.5 * ((rows[f] - u[f, x]) - (FLOW_STEP * 0.5) * out[f])
        copies += begin(sems, x, (hold.at[x], inc.at[:, x]))
    finish(copies)


def send_body(req, table, send, hold, sems):
    wanted = req[...].reshape(128, 128).astype(F32).astype(BF16)
    row, col = iota((1024, 128), 0), iota((1024, 128), 1)
    spread = jnp.where(row // 8 == col, 1.0, 0.0).astype(BF16)
    rep = jnp.dot(spread, wanted, preferred_element_type=F32)
    own = jnp.where(row % 4 == col, rep, 0.0).astype(BF16)
    value = jnp.dot(own, jnp.ones((128, 128), BF16), preferred_element_type=F32)
    target = value + ((row % 8) // 4 * 16).astype(F32)
    pick = jnp.where(col.astype(F32) == target, 1.0, 0.0).astype(BF16)
    copies = []
    for part in range(3):
        rows = jnp.dot(
            pick, table[:, 256 * part : 256 * part + 256], preferred_element_type=F32
        )
        a = rows[:, 0:128].reshape(128, 8, 128)
        b = rows[:, 128:256].reshape(128, 8, 128)
        hold[part] = jnp.concatenate([a, b], 1).astype(BF16)
        copies += begin(sems, part, (hold.at[part], send.at[:, 16 * part : 16 * part + 16, :]))
    finish(copies)


def gather_source(got, pick):
    t = got[...].astype(F32)
    rhs = jnp.concatenate(
        [
            t[:, 0:8, :].reshape(1024, 128).astype(BF16),
            t[:, 8:16, :].reshape(1024, 128).astype(BF16),
        ],
        1,
    )
    even = jnp.dot(pick[0], rhs, preferred_element_type=F32)
    odd = jnp.dot(pick[1], rhs, preferred_element_type=F32)
    return jnp.concatenate([even[:, 0:128], odd[:, 0:128], even[:, 128:256], odd[:, 128:256]], 1)


def prepare_body(nb_far, slot_far, after, gcat, ge, go, pick, esrc, edst, *scratch):
    gcat_v, gx0_v, gx1_v, pick_v, esrc_v, edst_v, nb, slot, sems = scratch
    fetch = begin(sems, 0, (nb_far, nb), (slot_far, slot))
    me = lax.axis_index("solver") * lax.axis_size("space") + lax.axis_index("space")
    finish(fetch)
    owner, row = nb[...] // EL, nb[...] % EL
    away = jnp.where(owner == me, 0, EL)
    spot = slot[...] // 4 * 8 + slot[...] % 4
    cols = [row[f : f + 1] + away[f : f + 1] for f in range(2)]
    even = is_even("space")
    cols = [jnp.where(even, cols[1], cols[0]), jnp.where(even, cols[0], cols[1])]
    cols += [row[f : f + 1] for f in range(2, 6)] + [spot]
    eye = iota((EL, EL), 0) == iota((EL, EL), 1)
    spread = [jnp.where(eye, c.astype(F32), 0.0) for c in cols]
    coarse = [jnp.floor(t * (1.0 / 32.0)) for t in spread]
    fine = [t - 32.0 * c for t, c in zip(spread, coarse)]
    ones = jnp.ones((EL, 128), BF16)
    coarse = jnp.dot(jnp.concatenate(coarse, 0).astype(BF16), ones, preferred_element_type=F32)
    fine = jnp.dot(jnp.concatenate(fine, 0).astype(BF16), ones, preferred_element_type=F32)
    column = 32.0 * coarse + fine
    lane = iota((EL, 128), 1).astype(F32)

    def onehot(ref, col, width, shift=0.0):
        number = column[col * EL : (col + 1) * EL] + shift
        for t in range(0, width, 128):
            n = min(128, width - t)
            hit = jnp.where(lane + t == number, 1.0, 0.0).astype(BF16)
            ref[:, t : t + n] = hit[:, :n]

    onehot(gx0_v, 0, 2 * EL)
    onehot(gx1_v, 1, 2 * EL)
    copies = begin(sems, 2, (gx0_v, ge), (gx1_v, go))
    for t in range(0, 4 * EL, 128):
        hit = jnp.zeros((EL, 128), jnp.bool_)
        for f in range(4):
            hit = hit | (lane + t == column[(2 + f) * EL : (3 + f) * EL] + f * EL)
        gcat_v[:, t : t + 128] = jnp.where(hit, 1.0, 0.0).astype(BF16)
    copies += begin(sems, 4, (gcat_v, gcat))
    onehot(pick_v.at[0], 6, 1024)
    onehot(pick_v.at[1], 6, 1024, 4.0)
    copies += begin(sems, 5, (pick_v, pick))

    def node(c, flip):
        face, a, b = c // 64, c % 64 // 8, c % 8
        low = face % 2 == (1 if flip else 0)
        spot = jnp.where(low, 0, 7)
        return jnp.where(face < 2, a * 64 + spot * 8 + b, a * 64 + b * 8 + spot)

    esrc_v[...] = jnp.where(
        iota((512, 256), 0) == node(iota((512, 256), 1), True), 1.0, 0.0
    ).astype(BF16)
    edst_v[...] = jnp.where(
        iota((256, 512), 1) == node(iota((256, 512), 0), False), 1.0, 0.0
    ).astype(BF16)
    copies += begin(sems, 6, (esrc_v, esrc), (edst_v, edst))
    finish(copies)


def face_count():
    n = iota((1, NODES), 1)
    count = jnp.zeros((1, NODES), I32)
    for part in (n // 64, n // 8 % 8, n % 8):
        count = count + jnp.where((part == 0) | (part == 7), 1, 0)
    return count.astype(F32)


def times(a, b):
    return lax.dot_general(a, b, (((1,), (1,)), ((), ())), preferred_element_type=F32)


def local_terms(q, dx, dy, dz, gcat, esrc, edst, ready=lambda *refs: None):
    traces = jnp.dot(jnp.concatenate(q, 0), esrc[...], preferred_element_type=F32).astype(BF16)
    wide = jnp.concatenate([traces[v * EL : (v + 1) * EL] for v in range(4)], 1)
    lane = iota((1, 1024), 1) % 256 // 64
    rhs = jnp.concatenate(
        [wide * jnp.where(lane == f, 1.0, 0.0).astype(BF16) for f in range(4)], 0
    )
    ready(gcat, edst)
    got = jnp.dot(gcat[...], rhs, preferred_element_type=F32).astype(BF16)
    count = face_count()
    out = []
    ready(dx, dy, dz)
    for v in range(4):
        pen = jnp.dot(got[:, v * 256 : (v + 1) * 256], edst[...], preferred_element_type=F32)
        pen = pen - count * q[v].astype(F32)
        if v == 0:
            vol = times(q[1], dx[...]) + times(q[2], dy[...]) + times(q[3], dz[...])
        else:
            vol = times(q[0], (dx, dy, dz)[v - 1][...])
        out.append(pen - vol)
    return out


def cross_terms(ge, go, own_e, own_o, got_e, got_o):
    lane = iota((EL, 128), 1)
    first, last = [], []
    by_even = jnp.concatenate([jnp.concatenate([own_o[w], got_e[w]], 0) for w in range(2)], 1)
    by_odd = jnp.concatenate([jnp.concatenate([own_e[w], got_o[w]], 0) for w in range(2)], 1)
    by_even = jnp.dot(ge[...], by_even, preferred_element_type=F32)
    by_odd = jnp.dot(go[...], by_odd, preferred_element_type=F32)
    even = is_even("space")
    low = jnp.where(even, by_odd, by_even)
    high = jnp.where(even, by_even, by_odd)
    for v in range(4):
        w = v // 2
        a = low[:, w * 128 : (w + 1) * 128]
        b = high[:, w * 128 : (w + 1) * 128]
        if v % 2 == 0:
            b = pltpu.roll(b, 64, 1)
        else:
            a = pltpu.roll(a, 64, 1)
        first.append(jnp.where(lane < 64, a, 0.0))
        last.append(jnp.where(lane < 64, 0.0, b))
    return first, last


def sound_zero_body(*refs):
    given, (bhi, alo, _, _, part, *here), (hold, sems) = refs[:11], refs[11:27], refs[27:]
    coming = {id(to): copy for to, copy in zip(here, begin(sems, 4, *zip(given, here)))}
    ready = lambda *names: finish([coming[id(t)] for t in names])
    q, esrc, gcat, edst, dx, dy, dz, gx0, gx1, olo, ohi = here
    ready(q, esrc)
    rounded = [q[v] for v in range(4)]
    terms = local_terms(rounded, dx, dy, dz, gcat, esrc, edst, ready)
    ready(gx0, gx1, olo, ohi)
    first, last = cross_terms(gx0, gx1, olo, ohi, bhi, alo)
    copies = []
    for v in range(4):
        full_term = jnp.concatenate(
            [
                terms[v][:, 0:128] + first[v],
                terms[v][:, 128:384],
                terms[v][:, 384:512] + last[v],
            ],
            1,
        )
        hold[v] = q[v].astype(F32) + SOUND_STEP * full_term
        copies += begin(sems, v, (hold.at[v], part.at[v]))
    finish(copies)


def sources_body(got, pick, part, _, q1, src, lo, hi, token, pick_v, part_v, token_v, sems):
    token_v[...] = jnp.zeros_like(token_v)
    copies = begin(
        sems,
        0,
        (pick, pick_v),
        (part.at[0], q1.at[0]),
        *[(part.at[v], part_v.at[v - 1]) for v in (1, 2, 3)],
        (token_v, token),
    )
    copies[0].wait()
    for c in range(3):
        s = gather_source(got.at[:, 16 * c : 16 * c + 16, :], pick_v)
        src[c] = s.astype(BF16)
        copies[2 + c].wait()
        q1[1 + c] = part_v[c] + SOUND_STEP * s
    copies[1].wait()
    copies[5].wait()
    store_traces(
        [q1[v, :, 0:128] for v in range(4)],
        [q1[v, :, 384:512] for v in range(4)],
        lo,
        hi,
    )


def sound_one_body(q0, q1, src, dx, dy, dz, gcat, esrc, edst, after, part):
    terms = local_terms([q1[v].astype(BF16) for v in range(4)], dx, dy, dz, gcat, esrc, edst)
    for v in range(4):
        t = terms[v] if v == 0 else terms[v] + src[v - 1].astype(F32)
        part[v] = 0.75 * q0[v].astype(F32) + 0.25 * (q1[v] + SOUND_STEP * t)


def cross_body(scale, gx0, gx1, olo, ohi, bhi, alo, part, ends, lo, hi):
    first, last = cross_terms(gx0, gx1, olo, ohi, bhi, alo)
    tiles = [[], []]
    for v in range(4):
        a = part[v, :, 0:128] + scale * first[v]
        b = part[v, :, 384:512] + scale * last[v]
        ends[0, v] = a
        ends[1, v] = b
        tiles[0].append(a)
        tiles[1].append(b)
    store_traces(tiles[0], tiles[1], lo, hi)


def sound_two_body(q0, mid, ends, src, dx, dy, dz, gcat, esrc, edst, out, rest, hold, sems):
    q2 = [jnp.concatenate([ends[0, v], mid[v, :, 128:384], ends[1, v]], 1) for v in range(4)]
    terms = local_terms([t.astype(BF16) for t in q2], dx, dy, dz, gcat, esrc, edst)
    copies = []
    for v in range(4):
        t = terms[v] if v == 0 else terms[v] + src[v - 1].astype(F32)
        start = q0[v].astype(F32)
        t = start * (1.0 / 3.0) + (2.0 / 3.0) * (q2[v] + SOUND_STEP * t) - start
        hold[v] = t[:, 128:384]
        rest[0, v] = t[:, 0:128]
        rest[1, v] = t[:, 384:512]
        copies += begin(sems, v, (hold.at[v], out.at[v, :, 128:384]))
    finish(copies)


def final_body(scale, gx0, gx1, olo, ohi, bhi, alo, rest, given, out, hold, sems):
    first, last = cross_terms(gx0, gx1, olo, ohi, bhi, alo)
    copies = []
    for v in range(4):
        hold[0, v] = rest[0, v] + scale * first[v]
        hold[1, v] = rest[1, v] + scale * last[v]
        copies += begin(
            sems, 2 * v, (hold.at[0, v], out.at[v, :, 0:128]), (hold.at[1, v], out.at[v, :, 384:512])
        )
    finish(copies)


def swap(even, odd, axis):
    count = lax.axis_size(axis)
    by_even = [(i, i + 1 - 2 * (i % 2)) for i in range(count)]
    by_odd = [(i, (i - 1 + 2 * (i % 2)) % count) for i in range(count)]
    other = lax.ppermute(odd, axis, by_odd)
    return lax.ppermute(even, axis, by_even), other


def local(flow_state, acoustic_state, dx, dy, dz, requests, elem_slot, neighbours):
    both = ("solver", "space")
    grid = full(5, 4, 128, 128)
    plane, column = full(5, 128, 128), full(128, 128)
    state = full(4, EL, NODES)
    traces = [half(2, EL, 128)] * 2
    keep = lambda *shape: pltpu.VMEM(shape, F32)
    keep_half = lambda *shape: pltpu.VMEM(shape, BF16)

    wanted = jnp.pad(requests.reshape(128, 1, 4), ((0, 0), (0, 0), (0, 124)))
    wanted = lax.all_to_all(wanted, both, split_axis=0, concat_axis=0, tiled=True)
    packs = call(
        edges_body,
        [plane, plane, column, column] + traces,
        "edges",
        (flow_state, acoustic_state),
        scratch=[keep(4, 5, 128, 128), keep_half(2, 4, EL, 128), dma(8)],
        far=(0, 1),
    )
    ue, uo, ze, zo, qe, qo = packs
    ue, uo = swap(ue, uo, "space")
    ze, zo = swap(ze, zo, "solver")
    got_qe, got_qo = swap(qe, qo, "space")

    table = call(
        lamb_body,
        half(128, 768),
        "lamb",
        (flow_state, ue, uo, ze, zo),
        scratch=[keep(3, 6, 128, 128), keep(6, 128, 128)],
    )
    table, got_qe, got_qo = lax.optimization_barrier((table, got_qe, got_qo))
    send = call(
        send_body,
        half(128, 48, 128),
        "send",
        (wanted, table),
        scratch=[keep_half(3, 128, 16, 128), dma(3)],
        far_out=(0,),
    )
    got = lax.all_to_all(send, both, split_axis=0, concat_axis=0, tiled=True)

    shapes = [(EL, 4 * EL), (EL, 2 * EL), (EL, 2 * EL), (2, EL, 1024), (512, 256), (256, 512)]
    gcat, ge, go, pick, esrc, edst = call(
        prepare_body,
        [half(*t) for t in shapes],
        "prepare",
        (neighbours, elem_slot.reshape(1, EL), send),
        scratch=[keep_half(*t) for t in shapes] + [pltpu.VMEM((6, EL), I32), pltpu.VMEM((1, EL), I32), dma(8)],
        far=(0, 1, 2),
        far_out=range(6),
    )
    first, ce, co, ye, yo = call(
        stage_one_body,
        [grid] + [half(5, 128, 128)] * 2 + [column, column],
        "flow_one",
        (flow_state, ue, uo, ze, zo),
        scratch=[
            keep(5, 6, 128, 128),
            keep(4, 5, 128, 128),
            keep_half(2, 5, 128, 128),
            keep(2, 128, 128),
            keep(2, 5, 128, 128),
            keep(2, 128, 128),
            dma(12),
        ],
        far=range(1, 5),
        far_out=range(5),
    )
    ye, yo = swap(ye, yo, "solver")
    ce, co = swap(ce, co, "space")

    given = (acoustic_state, esrc, gcat, edst, dx, dy, dz, ge, go, qe, qo)
    part = call(
        sound_zero_body,
        state,
        "sound_zero",
        given + (got_qe, got_qo, first, ye),
        scratch=[keep_half(*t.shape) for t in given] + [keep(4, EL, NODES), dma(15)],
        far=[*range(11), 13],
        far_out=(0,),
    )

    q1, src, qe, qo, token = call(
        sources_body,
        [state, half(3, EL, NODES)] + traces + [full(8, 128)],
        "sources",
        (got, pick, part, yo),
        scratch=[keep_half(2, EL, 1024), keep(3, EL, NODES), keep(8, 128), dma(6)],
        far=(1, 2),
        far_out=(4,),
    )
    mats = (dx, dy, dz, gcat, esrc, edst)
    got_qe, got_qo = swap(qe, qo, "space")
    flow_increment = call(
        stage_two_body,
        grid,
        "flow_two",
        (flow_state, first, ue, uo, ce, co, ye, yo, token),
        scratch=[keep(5, 6, 128, 128), keep(4, 5, 128, 128), keep(2, 5, 128, 128), dma(6)],
        far=(2, 3, 8),
        far_out=(0,),
    )
    part = call(
        sound_one_body,
        state,
        "sound_one",
        (acoustic_state, q1, src) + mats + (flow_increment,),
        far=(9,),
    )
    ends, qe, qo = call(
        lambda *r: cross_body(0.25 * SOUND_STEP, *r),
        [full(2, 4, EL, 128)] + traces,
        "cross_one",
        (ge, go, qe, qo, got_qe, got_qo, part),
    )
    got_qe, got_qo = swap(qe, qo, "space")
    out, rest = call(
        sound_two_body,
        [state, full(2, 4, EL, 128)],
        "sound_two",
        (acoustic_state, part, ends, src) + mats,
        scratch=[keep(4, EL, 256), dma(4)],
        far_out=(0,),
    )
    out = call(
        lambda *r: final_body(2.0 / 3.0 * SOUND_STEP, *r),
        state,
        "cross_two",
        (ge, go, qe, qo, got_qe, got_qo, rest, out),
        scratch=[keep(2, 4, EL, 128), dma(8)],
        far=(7,),
        far_out=(0,),
        aliases={7: 0},
    )
    return flow_increment, out


def solution(mesh):
    both = ("solver", "space")
    grid = P(None, "space", None, "solver")
    sound = P(None, both, None)
    in_specs = (grid, sound, P(), P(), P(), P(both, None, None), P(both), P(None, both))
    return jax.shard_map(
        local, mesh=mesh, in_specs=in_specs, out_specs=(grid, sound), check_vma=False
    )
```

```python
import jax
import jax.numpy as jnp
from jax import lax
from jax.experimental import pallas as pl
from jax.experimental.pallas import tpu as pltpu
from jax.sharding import PartitionSpec as P

F32 = jnp.float32
BF16 = jnp.bfloat16
I32 = jnp.int32

EL = 224
NODES = 512
FLOW_STEP = 0.2
SOUND_STEP = 0.2
VMEM_LIMIT = 20 * 1024 * 1024


def iota(shape, dim):
    return lax.broadcasted_iota(I32, shape, dim)


def full(*shape):
    return jax.ShapeDtypeStruct(shape, F32)


def half(*shape):
    return jax.ShapeDtypeStruct(shape, BF16)


def call(body, outs, name, args, scratch=(), aliases=None, far=(), far_out=()):
    space = [pl.BlockSpec(memory_space=pltpu.VMEM), pl.BlockSpec(memory_space=pltpu.HBM)]
    many = isinstance(outs, (list, tuple))
    outs = list(outs) if many else [outs]
    out_specs = [space[i in far_out] for i in range(len(outs))]
    outs = [pltpu.HBM(t.shape, t.dtype) if i in far_out else t for i, t in enumerate(outs)]
    args = [
        pltpu.with_memory_space_constraint(t, pltpu.HBM) if i in far else t
        for i, t in enumerate(args)
    ]
    return pl.pallas_call(
        body,
        out_shape=outs if many else outs[0],
        in_specs=[space[i in far] for i in range(len(args))],
        out_specs=out_specs if many else out_specs[0],
        scratch_shapes=list(scratch),
        name=name,
        input_output_aliases=aliases or {},
        compiler_params=pltpu.CompilerParams(vmem_limit_bytes=VMEM_LIMIT),
    )(*args)


def begin(sems, first, *pairs):
    out = []
    for i, (source, target) in enumerate(pairs):
        copy = pltpu.make_async_copy(source, target, sems.at[first + i])
        copy.start()
        out.append(copy)
    return out


def finish(copies):
    for copy in copies:
        copy.wait()


def is_even(axis):
    return lax.rem(lax.axis_index(axis), 2) == 0


def dma(n):
    return pltpu.SemaphoreType.DMA((n,))


def primitives(rows):
    inv = 1.0 / rows[0]
    v1, v2, v3 = rows[1] * inv, rows[2] * inv, rows[3] * inv
    p = 0.4 * (rows[4] - 0.5 * (rows[1] * v1 + rows[2] * v2 + rows[3] * v3))
    return (v1, v2, v3), p


def flux(rows, v, p, k):
    along = v[k]
    out = [rows[1 + k]]
    for c in range(3):
        t = rows[1 + c] * along
        out.append(t + p if c == k else t)
    out.append((rows[4] + p) * along)
    return out


def roll_y(f, step):
    return pltpu.roll(f, step % f.shape[0], 0)


def roll_z(f, step):
    return pltpu.roll(f, step % f.shape[1], 1)


def put_lane(acc, lane, f, source, target):
    return jnp.where(lane == target, roll_z(f, target - source), acc)


def diff_y(f):
    return roll_y(f, -1) - roll_y(f, 1)


def diff_z(f, lane, below, above, slot):
    up = jnp.where(lane == 127, roll_z(above, 127 - slot), roll_z(f, -1))
    down = jnp.where(lane == 0, roll_z(below, -slot), roll_z(f, 1))
    return up - down


def add_columns(x, fields, lane, lo, hi):
    for f, field in enumerate(fields):
        slot = f * 4 + x
        lo = put_lane(lo, lane, field, 0, slot)
        hi = put_lane(hi, lane, field, 127, slot)
    return lo, hi


def pair_lanes(tiles, upper):
    lane = iota((EL, 128), 1)
    out = []
    for w in range(2):
        a, b = tiles[2 * w], tiles[2 * w + 1]
        if upper:
            out.append(jnp.where(lane < 64, pltpu.roll(a, 64, 1), b))
        else:
            out.append(jnp.where(lane < 64, a, pltpu.roll(b, 64, 1)))
    return out


def store_traces(first_tiles, last_tiles, even_ref, odd_ref):
    lower, upper = pair_lanes(first_tiles, False), pair_lanes(last_tiles, True)
    even = is_even("space")
    for w in range(2):
        even_ref[w] = jnp.where(even, upper[w], lower[w]).astype(BF16)
        odd_ref[w] = jnp.where(even, lower[w], upper[w]).astype(BF16)


def edges_body(u, q, ue, uo, ze, zo, qe, qo, planes, ends, sems):
    even = is_even("space")
    copies = begin(
        sems,
        0,
        *[(u.at[:, x], planes.at[x]) for x in range(4)],
        (q.at[:, :, 0:128], ends.at[0]),
        (q.at[:, :, 384:512], ends.at[1]),
        (u.at[:, jnp.where(even, 3, 0)], ue),
        (u.at[:, jnp.where(even, 0, 3)], uo),
    )
    lane = iota((128, 128), 1)
    lo = hi = jnp.zeros((128, 128), F32)
    for x in range(4):
        copies[x].wait()
        rows = [planes[x, f] for f in range(5)]
        v, p = primitives(rows)
        lo, hi = add_columns(x, flux(rows, v, p, 2) + [v[0], v[1]], lane, lo, hi)
    even = is_even("solver")
    ze[...] = jnp.where(even, hi, lo)
    zo[...] = jnp.where(even, lo, hi)
    finish(copies[4:6])
    store_traces(
        [ends[0, v].astype(F32) for v in range(4)],
        [ends[1, v].astype(F32) for v in range(4)],
        qe,
        qo,
    )
    finish(copies[6:8])


def lamb_body(u, xe, xo, ze, zo, table, vel, pooled):
    lane = iota((128, 128), 1)
    for x in range(4):
        inv = 1.0 / u[0, x]
        for c in range(3):
            vel[c, x + 1] = u[1 + c, x] * inv
    even = is_even("space")
    by_link = []
    for link in (xe, xo):
        inv = 1.0 / link[0]
        by_link.append([link[1 + c] * inv for c in (1, 2)])
    for c in (1, 2):
        by_even, by_odd = by_link[0][c - 1], by_link[1][c - 1]
        vel[c, 0] = jnp.where(even, by_odd, by_even)
        vel[c, 5] = jnp.where(even, by_even, by_odd)
    even = is_even("solver")
    below = jnp.where(even, zo[...], ze[...])
    above = jnp.where(even, ze[...], zo[...])
    for pair in range(2):
        total = None
        for x in (2 * pair, 2 * pair + 1):
            v1, v2, v3 = vel[0, x + 1], vel[1, x + 1], vel[2, x + 1]
            w1 = diff_y(v3) - diff_z(v2, lane, below, above, 24 + x)
            w2 = diff_z(v1, lane, below, above, 20 + x) - (vel[2, x + 2] - vel[2, x])
            w3 = (vel[1, x + 2] - vel[1, x]) - diff_y(v1)
            lamb = [w2 * v3 - w3 * v2, w3 * v1 - w1 * v3, w1 * v2 - w2 * v1]
            total = lamb if total is None else [a + b for a, b in zip(total, lamb)]
        for c in range(3):
            pooled[c * 2 + pair] = total[c]
    even, odd = [], []
    for c in range(6):
        t = pooled.at[c]
        even.append(t[pl.ds(0, 32, stride=4), :] + t[pl.ds(1, 32, stride=4), :])
        odd.append(t[pl.ds(2, 32, stride=4), :] + t[pl.ds(3, 32, stride=4), :])
    rows = jnp.concatenate([jnp.concatenate(even, 0), jnp.concatenate(odd, 0)], 1)
    z, n = iota((256, 128), 0), iota((256, 128), 1)
    pool = jnp.where((z // 128) * 64 + (z % 128) // 2 == n, 0.0625, 0.0).astype(F32)
    coarse = jnp.dot(rows, pool, preferred_element_type=F32, precision=lax.Precision.HIGHEST)
    flat = pooled.at[0]
    hold = pooled.at[1]
    flat[...] = coarse[0:128]
    hold[0:64] = coarse[128:192]
    table[...] = jnp.zeros_like(table)
    for t in range(6):
        for par in range(2):
            c, inner = t // 2, (t % 2) * 2 + par
            src = flat if c < 2 else hold
            base = (c % 2) * 64
            piece = src[pl.ds(base + inner, 16, stride=4), :]
            table[par * 16 : par * 16 + 16, t * 128 : (t + 1) * 128] = piece.astype(BF16)


def tendency_plane(x, rows_of, along_a, below, above, lane):
    rows = rows_of(x)
    v, p = primitives(rows)
    fb = flux(rows, v, p, 1)
    fc = flux(rows, v, p, 2)
    out = []
    for f in range(5):
        total = along_a(x, f) + diff_y(fb[f])
        out.append(total + diff_z(fc[f], lane, below, above, f * 4 + x))
    return rows, out


def fill_flux_a(planes, fa):
    for x, rows in planes:
        v, p = primitives(rows)
        for f, t in enumerate(flux(rows, v, p, 0)):
            fa[f, x + 1] = t


def inner_planes(u):
    return [(x, [u[f, x] for f in range(5)]) for x in range(4)]


def stage_one_body(u, ue, uo, ze, zo, first, ce, co, ye, yo, *scratch):
    fa, hold, edge, zpack, halo, zhalo, sems = scratch
    lane = iota((128, 128), 1)
    even, even_z = is_even("space"), is_even("solver")
    e, o = jnp.where(even, 1, 0), jnp.where(even, 0, 1)
    ez, oz = jnp.where(even_z, 1, 0), jnp.where(even_z, 0, 1)
    fetch = begin(
        sems, 8, (ue, halo.at[e]), (uo, halo.at[o]), (ze, zhalo.at[ez]), (zo, zhalo.at[oz])
    )
    fill_flux_a(inner_planes(u), fa)
    finish(fetch)
    fill_flux_a([(x, [halo[i, f] for f in range(5)]) for i, x in enumerate((-1, 4))], fa)
    below, above = zhalo[0], zhalo[1]
    lo = hi = jnp.zeros((128, 128), F32)
    copies = []
    for i, x in enumerate((0, 3, 1, 2)):
        rows, out = tendency_plane(
            x,
            lambda x: [u[f, x] for f in range(5)],
            lambda x, f: fa[f, x + 2] - fa[f, x],
            below,
            above,
            lane,
        )
        now = [rows[f] - (FLOW_STEP * 0.5) * out[f] for f in range(5)]
        for f in range(5):
            hold[x, f] = now[f]
        copies += begin(sems, i, (hold.at[x], first.at[:, x]))
        if x in (0, 3):
            for f in range(5):
                edge[i, f] = ((-FLOW_STEP * 0.5) * out[f]).astype(BF16)
        v, p = primitives(now)
        lo, hi = add_columns(x, flux(now, v, p, 2), lane, lo, hi)
    zpack[0] = lo
    zpack[1] = hi
    copies += begin(
        sems, 4, (edge.at[e], ce), (edge.at[o], co), (zpack.at[ez], ye), (zpack.at[oz], yo)
    )
    finish(copies)


def stage_two_inner_body(u, first, part, fa, hold, sems):
    lane = iota((128, 128), 1)
    fill_flux_a(inner_planes(first), fa)
    copies = []
    for x, rows in inner_planes(first):
        v, p = primitives(rows)
        fb = flux(rows, v, p, 1)
        fc = flux(rows, v, p, 2)
        for f in range(5):
            total = diff_y(fb[f])
            total = total + jnp.where(lane == 127, 0.0, roll_z(fc[f], -1))
            total = total - jnp.where(lane == 0, 0.0, roll_z(fc[f], 1))
            if x < 3:
                total = total + fa[f, x + 2]
            if x > 0:
                total = total - fa[f, x]
            hold[x, f] = 0.5 * ((rows[f] - u[f, x]) - (FLOW_STEP * 0.5) * total)
        copies += begin(sems, x, (hold.at[x], part.at[:, x]))
    finish(copies)


def stage_two_body(part, ue, uo, ce, co, ze, zo, after, inc, *scratch):
    hold, halo, sems = scratch
    lane = iota((128, 128), 1)
    even, even_z = is_even("space"), is_even("solver")
    e, o = jnp.where(even, 1, 0), jnp.where(even, 0, 1)
    fetch = begin(sems, 4, (ue, halo.at[e]), (uo, halo.at[o]))
    below = jnp.where(even_z, zo[...], ze[...])
    above = jnp.where(even_z, ze[...], zo[...])
    outer, copies = {}, []
    for x in (1, 2, 0, 3):
        if x in (0, 3):
            if not outer:
                finish(fetch)
            i = x // 3
            rows = []
            for f in range(5):
                by_even, by_odd = ce[f].astype(F32), co[f].astype(F32)
                change = jnp.where(even, by_even, by_odd) if i else jnp.where(even, by_odd, by_even)
                rows.append(halo[i, f] + change)
            v, p = primitives(rows)
            outer[x] = flux(rows, v, p, 0)
        for f in range(5):
            slot = f * 4 + x
            extra = jnp.where(lane == 127, roll_z(above, 127 - slot), 0.0)
            extra = extra - jnp.where(lane == 0, roll_z(below, -slot), 0.0)
            if x == 0:
                extra = extra - outer[x][f]
            if x == 3:
                extra = extra + outer[x][f]
            hold[x, f] = part[f, x] - (FLOW_STEP * 0.25) * extra
        copies += begin(sems, x, (hold.at[x], inc.at[:, x]))
    finish(copies)


def send_body(req, table, _, send, hold, sems):
    wanted = req[...].reshape(128, 4).astype(F32).astype(BF16)
    row, col = iota((1024, 128), 0), iota((1024, 128), 1)
    spread = jnp.where(row // 8 == col, 1.0, 0.0).astype(BF16)
    rep = jnp.dot(spread, wanted, preferred_element_type=F32)
    own = jnp.where(iota((1024, 4), 0) % 4 == iota((1024, 4), 1), rep, 0.0).astype(BF16)
    value = jnp.dot(own, jnp.ones((4, 128), BF16), preferred_element_type=F32)
    target = value + ((row % 8) // 4 * 16).astype(F32)
    pick = jnp.where(col.astype(F32) == target, 1.0, 0.0).astype(BF16)
    copies = []
    for part in range(3):
        rows = jnp.dot(
            pick, table[:, 256 * part : 256 * part + 256], preferred_element_type=F32
        )
        a = rows[:, 0:128].reshape(128, 8, 128)
        b = rows[:, 128:256].reshape(128, 8, 128)
        hold[part] = jnp.concatenate([a, b], 1).astype(BF16)
        copies += begin(sems, part, (hold.at[part], send.at[:, 16 * part : 16 * part + 16, :]))
    finish(copies)


def gather_source(got, pick):
    t = got[...].astype(F32)
    rhs = jnp.concatenate(
        [
            t[:, 0:8, :].reshape(1024, 128).astype(BF16),
            t[:, 8:16, :].reshape(1024, 128).astype(BF16),
        ],
        1,
    )
    even = jnp.dot(pick[0], rhs, preferred_element_type=F32)
    odd = jnp.dot(pick[1], rhs, preferred_element_type=F32)
    return jnp.concatenate([even[:, 0:128], odd[:, 0:128], even[:, 128:256], odd[:, 128:256]], 1)


def prepare_body(nb_far, slot_far, _, gcat, ge, go, esrc, edst, spot_out, *scratch):
    gcat_v, gx0_v, gx1_v, esrc_v, edst_v, spot_v, nb, slot, sems = scratch
    fetch = begin(sems, 0, (nb_far, nb), (slot_far, slot))
    me = lax.axis_index("solver") * lax.axis_size("space") + lax.axis_index("space")
    finish(fetch)
    owner, row = nb[...] // EL, nb[...] % EL
    away = jnp.where(owner == me, 0, EL)
    spot = slot[...] // 4 * 8 + slot[...] % 4
    cols = [row[f : f + 1] + away[f : f + 1] for f in range(2)]
    even = is_even("space")
    cols = [jnp.where(even, cols[1], cols[0]), jnp.where(even, cols[0], cols[1])]
    cols += [row[f : f + 1] for f in range(2, 6)] + [spot]
    eye = iota((EL, EL), 0) == iota((EL, EL), 1)
    spread = [jnp.where(eye, c.astype(F32), 0.0) for c in cols]
    coarse = [jnp.floor(t * (1.0 / 32.0)) for t in spread]
    fine = [t - 32.0 * c for t, c in zip(spread, coarse)]
    ones = jnp.ones((EL, 128), BF16)
    coarse = jnp.dot(jnp.concatenate(coarse, 0).astype(BF16), ones, preferred_element_type=F32)
    fine = jnp.dot(jnp.concatenate(fine, 0).astype(BF16), ones, preferred_element_type=F32)
    column = 32.0 * coarse + fine
    lane = iota((EL, 128), 1).astype(F32)

    def onehot(ref, col, width):
        number = column[col * EL : (col + 1) * EL]
        for t in range(0, width, 128):
            n = min(128, width - t)
            hit = jnp.where(lane + t == number, 1.0, 0.0).astype(BF16)
            ref[:, t : t + n] = hit[:, :n]

    onehot(gx0_v, 0, 2 * EL)
    onehot(gx1_v, 1, 2 * EL)
    copies = begin(sems, 2, (gx0_v, ge), (gx1_v, go))
    for t in range(0, 4 * EL, 128):
        hit = jnp.zeros((EL, 128), jnp.bool_)
        for f in range(4):
            hit = hit | (lane + t == column[(2 + f) * EL : (3 + f) * EL] + f * EL)
        gcat_v[:, t : t + 128] = jnp.where(hit, 1.0, 0.0).astype(BF16)
    copies += begin(sems, 4, (gcat_v, gcat))
    spot_v[...] = column[6 * EL : 7 * EL]
    copies += begin(sems, 5, (spot_v, spot_out))

    def node(c, flip):
        face, a, b = c // 64, c % 64 // 8, c % 8
        low = face % 2 == (1 if flip else 0)
        spot = jnp.where(low, 0, 7)
        return jnp.where(face < 2, a * 64 + spot * 8 + b, a * 64 + b * 8 + spot)

    esrc_v[...] = jnp.where(
        iota((512, 256), 0) == node(iota((512, 256), 1), True), 1.0, 0.0
    ).astype(BF16)
    edst_v[...] = jnp.where(
        iota((256, 512), 1) == node(iota((256, 512), 0), False), 1.0, 0.0
    ).astype(BF16)
    copies += begin(sems, 6, (esrc_v, esrc), (edst_v, edst))
    finish(copies)


def face_count():
    n = iota((1, NODES), 1)
    count = jnp.zeros((1, NODES), I32)
    for part in (n // 64, n // 8 % 8, n % 8):
        count = count + jnp.where((part == 0) | (part == 7), 1, 0)
    return count.astype(F32)


def times(a, b):
    return lax.dot_general(a, b, (((1,), (1,)), ((), ())), preferred_element_type=F32)


def local_terms(q, dx, dy, dz, gcat, esrc, edst, ready=lambda *refs: None):
    traces = jnp.dot(jnp.concatenate(q, 0), esrc[...], preferred_element_type=F32).astype(BF16)
    wide = jnp.concatenate([traces[v * EL : (v + 1) * EL] for v in range(4)], 1)
    lane = iota((1, 1024), 1) % 256 // 64
    rhs = jnp.concatenate(
        [wide * jnp.where(lane == f, 1.0, 0.0).astype(BF16) for f in range(4)], 0
    )
    ready(gcat, edst)
    got = jnp.dot(gcat[...], rhs, preferred_element_type=F32).astype(BF16)
    count = face_count()
    out = []
    ready(dx, dy, dz)
    for v in range(4):
        pen = jnp.dot(got[:, v * 256 : (v + 1) * 256], edst[...], preferred_element_type=F32)
        pen = pen - count * q[v].astype(F32)
        if v == 0:
            vol = times(q[1], dx[...]) + times(q[2], dy[...]) + times(q[3], dz[...])
        else:
            vol = times(q[0], (dx, dy, dz)[v - 1][...])
        out.append(pen - vol)
    return out


def cross_terms(ge, go, own_e, own_o, got_e, got_o):
    lane = iota((EL, 128), 1)
    first, last = [], []
    by_even = jnp.concatenate([jnp.concatenate([own_o[w], got_e[w]], 0) for w in range(2)], 1)
    by_odd = jnp.concatenate([jnp.concatenate([own_e[w], got_o[w]], 0) for w in range(2)], 1)
    by_even = jnp.dot(ge[...], by_even, preferred_element_type=F32)
    by_odd = jnp.dot(go[...], by_odd, preferred_element_type=F32)
    even = is_even("space")
    low = jnp.where(even, by_odd, by_even)
    high = jnp.where(even, by_even, by_odd)
    for v in range(4):
        w = v // 2
        a = low[:, w * 128 : (w + 1) * 128]
        b = high[:, w * 128 : (w + 1) * 128]
        if v % 2 == 0:
            b = pltpu.roll(b, 64, 1)
        else:
            a = pltpu.roll(a, 64, 1)
        first.append(jnp.where(lane < 64, a, 0.0))
        last.append(jnp.where(lane < 64, 0.0, b))
    return first, last


def sound_zero_body(*refs):
    given, (bhi, alo, _, _, part, *here), (hold, sems) = refs[:11], refs[11:27], refs[27:]
    coming = {id(to): copy for to, copy in zip(here, begin(sems, 4, *zip(given, here)))}
    ready = lambda *names: finish([coming[id(t)] for t in names])
    q, esrc, gcat, edst, dx, dy, dz, gx0, gx1, olo, ohi = here
    ready(q, esrc)
    rounded = [q[v] for v in range(4)]
    terms = local_terms(rounded, dx, dy, dz, gcat, esrc, edst, ready)
    ready(gx0, gx1, olo, ohi)
    first, last = cross_terms(gx0, gx1, olo, ohi, bhi, alo)
    copies = []
    for v in range(4):
        full_term = jnp.concatenate(
            [
                terms[v][:, 0:128] + first[v],
                terms[v][:, 128:384],
                terms[v][:, 384:512] + last[v],
            ],
            1,
        )
        hold[v] = q[v].astype(F32) + SOUND_STEP * full_term
        copies += begin(sems, v, (hold.at[v], part.at[v]))
    finish(copies)


def sources_body(got, spot, part, _, __, q1, src, lo, hi, token, spot_v, pick_v, part_v, token_v, sems):
    token_v[...] = jnp.zeros_like(token_v)
    copies = begin(
        sems,
        0,
        (spot, spot_v),
        (part.at[0], q1.at[0]),
        *[(part.at[v], part_v.at[v - 1]) for v in (1, 2, 3)],
        (token_v, token),
    )
    lane = iota((EL, 128), 1).astype(F32)
    copies[0].wait()
    for parity in range(2):
        number = spot_v[...] + 4.0 * parity
        for t in range(0, 1024, 128):
            pick_v[parity, :, t : t + 128] = jnp.where(lane + t == number, 1.0, 0.0).astype(BF16)
    for c in range(3):
        s = gather_source(got.at[:, 16 * c : 16 * c + 16, :], pick_v)
        src[c] = s.astype(BF16)
        copies[2 + c].wait()
        q1[1 + c] = part_v[c] + SOUND_STEP * s
    copies[1].wait()
    copies[5].wait()
    store_traces(
        [q1[v, :, 0:128] for v in range(4)],
        [q1[v, :, 384:512] for v in range(4)],
        lo,
        hi,
    )


def sound_one_body(q0, q1, src, dx, dy, dz, gcat, esrc, edst, after, part):
    terms = local_terms([q1[v].astype(BF16) for v in range(4)], dx, dy, dz, gcat, esrc, edst)
    for v in range(4):
        t = terms[v] if v == 0 else terms[v] + src[v - 1].astype(F32)
        part[v] = 0.75 * q0[v].astype(F32) + 0.25 * (q1[v] + SOUND_STEP * t)


def cross_body(scale, gx0, gx1, olo, ohi, bhi, alo, part, ends, lo, hi):
    first, last = cross_terms(gx0, gx1, olo, ohi, bhi, alo)
    tiles = [[], []]
    for v in range(4):
        a = part[v, :, 0:128] + scale * first[v]
        b = part[v, :, 384:512] + scale * last[v]
        ends[0, v] = a
        ends[1, v] = b
        tiles[0].append(a)
        tiles[1].append(b)
    store_traces(tiles[0], tiles[1], lo, hi)


def sound_two_body(q0, mid, ends, src, dx, dy, dz, gcat, esrc, edst, out, rest, hold, sems):
    q2 = [jnp.concatenate([ends[0, v], mid[v, :, 128:384], ends[1, v]], 1) for v in range(4)]
    terms = local_terms([t.astype(BF16) for t in q2], dx, dy, dz, gcat, esrc, edst)
    copies = []
    for v in range(4):
        t = terms[v] if v == 0 else terms[v] + src[v - 1].astype(F32)
        start = q0[v].astype(F32)
        t = start * (1.0 / 3.0) + (2.0 / 3.0) * (q2[v] + SOUND_STEP * t) - start
        hold[v] = t[:, 128:384]
        rest[0, v] = t[:, 0:128]
        rest[1, v] = t[:, 384:512]
        copies += begin(sems, v, (hold.at[v], out.at[v, :, 128:384]))
    finish(copies)


def final_body(scale, gx0, gx1, olo, ohi, bhi, alo, rest, given, out, hold, sems):
    first, last = cross_terms(gx0, gx1, olo, ohi, bhi, alo)
    copies = []
    for v in range(4):
        hold[0, v] = rest[0, v] + scale * first[v]
        hold[1, v] = rest[1, v] + scale * last[v]
        copies += begin(
            sems, 2 * v, (hold.at[0, v], out.at[v, :, 0:128]), (hold.at[1, v], out.at[v, :, 384:512])
        )
    finish(copies)


def swap(even, odd, axis):
    count = lax.axis_size(axis)
    by_even = [(i, i + 1 - 2 * (i % 2)) for i in range(count)]
    by_odd = [(i, (i - 1 + 2 * (i % 2)) % count) for i in range(count)]
    return lax.ppermute(even, axis, by_even), lax.ppermute(odd, axis, by_odd)


def local(flow_state, acoustic_state, dx, dy, dz, requests, elem_slot, neighbours):
    both = ("solver", "space")
    grid = full(5, 4, 128, 128)
    plane, column = full(5, 128, 128), full(128, 128)
    state = full(4, EL, NODES)
    traces = [half(2, EL, 128)] * 2
    keep = lambda *shape: pltpu.VMEM(shape, F32)
    keep_half = lambda *shape: pltpu.VMEM(shape, BF16)

    packs = call(
        edges_body,
        [plane, plane, column, column] + traces,
        "edges",
        (flow_state, acoustic_state),
        scratch=[keep(4, 5, 128, 128), keep_half(2, 4, EL, 128), dma(8)],
        far=(0, 1),
    )
    ue, uo, ze, zo, qe, qo = packs
    wanted = requests.reshape(128, 1, 4)
    wanted = lax.all_to_all(wanted, both, split_axis=0, concat_axis=0, tiled=True)
    ue, uo = swap(ue, uo, "space")
    ze, zo = swap(ze, zo, "solver")
    got_qe, got_qo = swap(qe, qo, "space")

    table = call(
        lamb_body,
        half(128, 768),
        "lamb",
        (flow_state, ue, uo, ze, zo),
        scratch=[keep(3, 6, 128, 128), keep(6, 128, 128)],
    )
    shapes = [(EL, 4 * EL), (EL, 2 * EL), (EL, 2 * EL), (512, 256), (256, 512)]
    gcat, ge, go, esrc, edst, spot = call(
        prepare_body,
        [half(*t) for t in shapes] + [full(EL, 128)],
        "prepare",
        (neighbours, elem_slot.reshape(1, EL), ue),
        scratch=[keep_half(*t) for t in shapes]
        + [keep(EL, 128), pltpu.VMEM((6, EL), I32), pltpu.VMEM((1, EL), I32), dma(8)],
        far=(0, 1, 2),
        far_out=range(6),
    )
    table, got_qe, got_qo = lax.optimization_barrier((table, got_qe, got_qo))
    send = call(
        send_body,
        half(128, 48, 128),
        "send",
        (wanted, table, gcat),
        scratch=[keep_half(3, 128, 16, 128), dma(3)],
        far=(2,),
        far_out=(0,),
    )
    got = lax.all_to_all(send, both, split_axis=0, concat_axis=0, tiled=True)

    first, ce, co, ye, yo = call(
        stage_one_body,
        [grid] + [half(5, 128, 128)] * 2 + [column, column],
        "flow_one",
        (flow_state, ue, uo, ze, zo),
        scratch=[
            keep(5, 6, 128, 128),
            keep(4, 5, 128, 128),
            keep_half(2, 5, 128, 128),
            keep(2, 128, 128),
            keep(2, 5, 128, 128),
            keep(2, 128, 128),
            dma(12),
        ],
        far=range(1, 5),
        far_out=range(5),
    )
    ye, yo = swap(ye, yo, "solver")
    ce, co = swap(ce, co, "space")

    given = (acoustic_state, esrc, gcat, edst, dx, dy, dz, ge, go, qe, qo)
    part = call(
        sound_zero_body,
        state,
        "sound_zero",
        given + (got_qe, got_qo, first, ye),
        scratch=[keep_half(*t.shape) for t in given] + [keep(4, EL, NODES), dma(15)],
        far=[*range(11), 13],
        far_out=(0,),
    )

    inner = call(
        stage_two_inner_body,
        grid,
        "flow_inner",
        (flow_state, first),
        scratch=[keep(5, 6, 128, 128), keep(4, 5, 128, 128), dma(4)],
        far_out=(0,),
    )
    q1, src, qe, qo, token = call(
        sources_body,
        [state, half(3, EL, NODES)] + traces + [full(8, 128)],
        "sources",
        (got, spot, part, yo, inner),
        scratch=[keep(EL, 128), keep_half(2, EL, 1024), keep(3, EL, NODES), keep(8, 128), dma(6)],
        far=(1, 2, 4),
        far_out=(4,),
    )
    mats = (dx, dy, dz, gcat, esrc, edst)
    got_qe, got_qo = swap(qe, qo, "space")
    flow_increment = call(
        stage_two_body,
        grid,
        "flow_two",
        (inner, ue, uo, ce, co, ye, yo, token),
        scratch=[keep(4, 5, 128, 128), keep(2, 5, 128, 128), dma(6)],
        far=(1, 2, 7),
        far_out=(0,),
    )
    part = call(
        sound_one_body,
        state,
        "sound_one",
        (acoustic_state, q1, src) + mats + (flow_increment,),
        far=(9,),
    )
    ends, qe, qo = call(
        lambda *r: cross_body(0.25 * SOUND_STEP, *r),
        [full(2, 4, EL, 128)] + traces,
        "cross_one",
        (ge, go, qe, qo, got_qe, got_qo, part),
    )
    got_qe, got_qo = swap(qe, qo, "space")
    out, rest = call(
        sound_two_body,
        [state, full(2, 4, EL, 128)],
        "sound_two",
        (acoustic_state, part, ends, src) + mats,
        scratch=[keep(4, EL, 256), dma(4)],
        far_out=(0,),
    )
    out = call(
        lambda *r: final_body(2.0 / 3.0 * SOUND_STEP, *r),
        state,
        "cross_two",
        (ge, go, qe, qo, got_qe, got_qo, rest, out),
        scratch=[keep(2, 4, EL, 128), dma(8)],
        far=(7,),
        far_out=(0,),
        aliases={7: 0},
    )
    return flow_increment, out


def solution(mesh):
    both = ("solver", "space")
    grid = P(None, "space", None, "solver")
    sound = P(None, both, None)
    in_specs = (grid, sound, P(), P(), P(), P(both, None, None), P(both), P(None, both))
    return jax.shard_map(
        local, mesh=mesh, in_specs=in_specs, out_specs=(grid, sound), check_vma=False
    )
```

```python
import jax
import jax.numpy as jnp
from jax import lax
from jax.experimental import pallas as pl
from jax.experimental.pallas import tpu as pltpu
from jax.sharding import PartitionSpec as P

F32 = jnp.float32
BF16 = jnp.bfloat16
I32 = jnp.int32

EL = 224
NODES = 512
FLOW_STEP = 0.2
SOUND_STEP = 0.2
VMEM_LIMIT = 20 * 1024 * 1024


def iota(shape, dim):
    return lax.broadcasted_iota(I32, shape, dim)


def full(*shape):
    return jax.ShapeDtypeStruct(shape, F32)


def half(*shape):
    return jax.ShapeDtypeStruct(shape, BF16)


def call(body, outs, name, args, scratch=(), aliases=None, far=(), far_out=()):
    space = [pl.BlockSpec(memory_space=pltpu.VMEM), pl.BlockSpec(memory_space=pltpu.HBM)]
    many = isinstance(outs, (list, tuple))
    outs = list(outs) if many else [outs]
    out_specs = [space[i in far_out] for i in range(len(outs))]
    outs = [pltpu.HBM(t.shape, t.dtype) if i in far_out else t for i, t in enumerate(outs)]
    args = [
        pltpu.with_memory_space_constraint(t, pltpu.HBM) if i in far else t
        for i, t in enumerate(args)
    ]
    return pl.pallas_call(
        body,
        out_shape=outs if many else outs[0],
        in_specs=[space[i in far] for i in range(len(args))],
        out_specs=out_specs if many else out_specs[0],
        scratch_shapes=list(scratch),
        name=name,
        input_output_aliases=aliases or {},
        compiler_params=pltpu.CompilerParams(vmem_limit_bytes=VMEM_LIMIT),
    )(*args)


def begin(sems, first, *pairs):
    out = []
    for i, (source, target) in enumerate(pairs):
        copy = pltpu.make_async_copy(source, target, sems.at[first + i])
        copy.start()
        out.append(copy)
    return out


def finish(copies):
    for copy in copies:
        copy.wait()


def is_even(axis):
    return lax.rem(lax.axis_index(axis), 2) == 0


def dma(n):
    return pltpu.SemaphoreType.DMA((n,))


def primitives(rows):
    inv = 1.0 / rows[0]
    v1, v2, v3 = rows[1] * inv, rows[2] * inv, rows[3] * inv
    p = 0.4 * (rows[4] - 0.5 * (rows[1] * v1 + rows[2] * v2 + rows[3] * v3))
    return (v1, v2, v3), p


def flux(rows, v, p, k):
    along = v[k]
    out = [rows[1 + k]]
    for c in range(3):
        t = rows[1 + c] * along
        out.append(t + p if c == k else t)
    out.append((rows[4] + p) * along)
    return out


def roll_y(f, step):
    return pltpu.roll(f, step % f.shape[0], 0)


def roll_z(f, step):
    return pltpu.roll(f, step % f.shape[1], 1)


def put_lane(acc, lane, f, source, target):
    return jnp.where(lane == target, roll_z(f, target - source), acc)


def diff_y(f):
    return roll_y(f, -1) - roll_y(f, 1)


def diff_z(f, lane, below, above, slot):
    up = jnp.where(lane == 127, roll_z(above, 127 - slot), roll_z(f, -1))
    down = jnp.where(lane == 0, roll_z(below, -slot), roll_z(f, 1))
    return up - down


def add_columns(x, fields, lane, lo, hi):
    for f, field in enumerate(fields):
        slot = f * 4 + x
        lo = put_lane(lo, lane, field, 0, slot)
        hi = put_lane(hi, lane, field, 127, slot)
    return lo, hi


def pair_lanes(tiles, upper):
    lane = iota((EL, 128), 1)
    out = []
    for w in range(2):
        a, b = tiles[2 * w], tiles[2 * w + 1]
        if upper:
            out.append(jnp.where(lane < 64, pltpu.roll(a, 64, 1), b))
        else:
            out.append(jnp.where(lane < 64, a, pltpu.roll(b, 64, 1)))
    return out


def store_traces(first_tiles, last_tiles, even_ref, odd_ref):
    lower, upper = pair_lanes(first_tiles, False), pair_lanes(last_tiles, True)
    even = is_even("space")
    for w in range(2):
        even_ref[w] = jnp.where(even, upper[w], lower[w]).astype(BF16)
        odd_ref[w] = jnp.where(even, lower[w], upper[w]).astype(BF16)


def edges_body(u, q, req, ue, uo, ze, zo, qe, qo, want, planes, ends, req_v, sems):
    even = is_even("space")
    ask = begin(sems, 8, (req, req_v))
    copies = begin(
        sems,
        0,
        *[(u.at[:, x], planes.at[x]) for x in range(4)],
        (q.at[:, :, 0:128], ends.at[0]),
        (q.at[:, :, 384:512], ends.at[1]),
        (u.at[:, jnp.where(even, 3, 0)], ue),
        (u.at[:, jnp.where(even, 0, 3)], uo),
    )
    lane = iota((128, 128), 1)
    lo = hi = jnp.zeros((128, 128), F32)
    eye = iota((128, 128), 0) == lane
    place = jnp.where(iota((512, 128), 0) // 128 == iota((512, 128), 1), 1.0, 0.0).astype(BF16)
    finish(ask)
    value = req_v[...].astype(F32)
    spread = [jnp.where(eye, value[c : c + 1], 0.0).astype(BF16) for c in range(4)]
    want[...] = jnp.dot(jnp.concatenate(spread, 1), place, preferred_element_type=F32)
    for x in range(4):
        copies[x].wait()
        rows = [planes[x, f] for f in range(5)]
        v, p = primitives(rows)
        lo, hi = add_columns(x, flux(rows, v, p, 2) + [v[0], v[1]], lane, lo, hi)
    even = is_even("solver")
    ze[...] = jnp.where(even, hi, lo)
    zo[...] = jnp.where(even, lo, hi)
    finish(copies[4:6])
    store_traces(
        [ends[0, v].astype(F32) for v in range(4)],
        [ends[1, v].astype(F32) for v in range(4)],
        qe,
        qo,
    )
    finish(copies[6:8])


def lamb_body(u, xe, xo, ze, zo, table, vel, pooled):
    lane = iota((128, 128), 1)
    for x in range(4):
        inv = 1.0 / u[0, x]
        for c in range(3):
            vel[c, x + 1] = u[1 + c, x] * inv
    even = is_even("space")
    by_link = []
    for link in (xe, xo):
        inv = 1.0 / link[0]
        by_link.append([link[1 + c] * inv for c in (1, 2)])
    for c in (1, 2):
        by_even, by_odd = by_link[0][c - 1], by_link[1][c - 1]
        vel[c, 0] = jnp.where(even, by_odd, by_even)
        vel[c, 5] = jnp.where(even, by_even, by_odd)
    even = is_even("solver")
    below = jnp.where(even, zo[...], ze[...])
    above = jnp.where(even, ze[...], zo[...])
    for pair in range(2):
        total = None
        for x in (2 * pair, 2 * pair + 1):
            v1, v2, v3 = vel[0, x + 1], vel[1, x + 1], vel[2, x + 1]
            w1 = diff_y(v3) - diff_z(v2, lane, below, above, 24 + x)
            w2 = diff_z(v1, lane, below, above, 20 + x) - (vel[2, x + 2] - vel[2, x])
            w3 = (vel[1, x + 2] - vel[1, x]) - diff_y(v1)
            lamb = [w2 * v3 - w3 * v2, w3 * v1 - w1 * v3, w1 * v2 - w2 * v1]
            total = lamb if total is None else [a + b for a, b in zip(total, lamb)]
        for c in range(3):
            pooled[c * 2 + pair] = total[c]
    even, odd = [], []
    for c in range(6):
        t = pooled.at[c]
        even.append(t[pl.ds(0, 32, stride=4), :] + t[pl.ds(1, 32, stride=4), :])
        odd.append(t[pl.ds(2, 32, stride=4), :] + t[pl.ds(3, 32, stride=4), :])
    rows = jnp.concatenate([jnp.concatenate(even, 0), jnp.concatenate(odd, 0)], 1)
    z, n = iota((256, 128), 0), iota((256, 128), 1)
    pool = jnp.where((z // 128) * 64 + (z % 128) // 2 == n, 0.0625, 0.0).astype(F32)
    coarse = jnp.dot(rows, pool, preferred_element_type=F32, precision=lax.Precision.HIGHEST)
    flat = pooled.at[0]
    hold = pooled.at[1]
    flat[...] = coarse[0:128]
    hold[0:64] = coarse[128:192]
    table[...] = jnp.zeros_like(table)
    for t in range(6):
        for par in range(2):
            c, inner = t // 2, (t % 2) * 2 + par
            src = flat if c < 2 else hold
            base = (c % 2) * 64
            piece = src[pl.ds(base + inner, 16, stride=4), :]
            table[par * 16 : par * 16 + 16, t * 128 : (t + 1) * 128] = piece.astype(BF16)


def tendency_plane(x, rows_of, along_a, below, above, lane):
    rows = rows_of(x)
    v, p = primitives(rows)
    fb = flux(rows, v, p, 1)
    fc = flux(rows, v, p, 2)
    out = []
    for f in range(5):
        total = along_a(x, f) + diff_y(fb[f])
        out.append(total + diff_z(fc[f], lane, below, above, f * 4 + x))
    return rows, out


def fill_flux_a(planes, fa):
    for x, rows in planes:
        v, p = primitives(rows)
        for f, t in enumerate(flux(rows, v, p, 0)):
            fa[f, x + 1] = t


def inner_planes(u):
    return [(x, [u[f, x] for f in range(5)]) for x in range(4)]


def stage_one_body(u, ue, uo, ze, zo, first, ce, co, ye, yo, *scratch):
    fa, hold, edge, zpack, halo, zhalo, sems = scratch
    lane = iota((128, 128), 1)
    even, even_z = is_even("space"), is_even("solver")
    e, o = jnp.where(even, 1, 0), jnp.where(even, 0, 1)
    ez, oz = jnp.where(even_z, 1, 0), jnp.where(even_z, 0, 1)
    fetch = begin(
        sems, 8, (ue, halo.at[e]), (uo, halo.at[o]), (ze, zhalo.at[ez]), (zo, zhalo.at[oz])
    )
    fill_flux_a(inner_planes(u), fa)
    finish(fetch)
    fill_flux_a([(x, [halo[i, f] for f in range(5)]) for i, x in enumerate((-1, 4))], fa)
    below, above = zhalo[0], zhalo[1]
    lo = hi = jnp.zeros((128, 128), F32)
    copies = []
    for i, x in enumerate((0, 3, 1, 2)):
        rows, out = tendency_plane(
            x,
            lambda x: [u[f, x] for f in range(5)],
            lambda x, f: fa[f, x + 2] - fa[f, x],
            below,
            above,
            lane,
        )
        now = [rows[f] - (FLOW_STEP * 0.5) * out[f] for f in range(5)]
        for f in range(5):
            hold[x, f] = now[f]
        copies += begin(sems, i, (hold.at[x], first.at[:, x]))
        if x in (0, 3):
            for f in range(5):
                edge[i, f] = ((-FLOW_STEP * 0.5) * out[f]).astype(BF16)
        v, p = primitives(now)
        lo, hi = add_columns(x, flux(now, v, p, 2), lane, lo, hi)
    zpack[0] = lo
    zpack[1] = hi
    copies += begin(
        sems, 4, (edge.at[e], ce), (edge.at[o], co), (zpack.at[ez], ye), (zpack.at[oz], yo)
    )
    finish(copies)


def stage_two_inner_body(u, first, part, fa, hold, sems):
    lane = iota((128, 128), 1)
    fill_flux_a(inner_planes(first), fa)
    copies = []
    for x, rows in inner_planes(first):
        v, p = primitives(rows)
        fb = flux(rows, v, p, 1)
        fc = flux(rows, v, p, 2)
        for f in range(5):
            total = diff_y(fb[f])
            total = total + jnp.where(lane == 127, 0.0, roll_z(fc[f], -1))
            total = total - jnp.where(lane == 0, 0.0, roll_z(fc[f], 1))
            if x < 3:
                total = total + fa[f, x + 2]
            if x > 0:
                total = total - fa[f, x]
            hold[x, f] = 0.5 * ((rows[f] - u[f, x]) - (FLOW_STEP * 0.5) * total)
        copies += begin(sems, x, (hold.at[x], part.at[:, x]))
    finish(copies)


def stage_two_body(part, ue, uo, ce, co, ze, zo, after, inc, *scratch):
    hold, halo, sems = scratch
    lane = iota((128, 128), 1)
    even, even_z = is_even("space"), is_even("solver")
    e, o = jnp.where(even, 1, 0), jnp.where(even, 0, 1)
    fetch = begin(sems, 4, (ue, halo.at[e]), (uo, halo.at[o]))
    below = jnp.where(even_z, zo[...], ze[...])
    above = jnp.where(even_z, ze[...], zo[...])
    outer, copies = {}, []
    for x in (1, 2, 0, 3):
        if x in (0, 3):
            if not outer:
                finish(fetch)
            i = x // 3
            rows = []
            for f in range(5):
                by_even, by_odd = ce[f].astype(F32), co[f].astype(F32)
                change = jnp.where(even, by_even, by_odd) if i else jnp.where(even, by_odd, by_even)
                rows.append(halo[i, f] + change)
            v, p = primitives(rows)
            outer[x] = flux(rows, v, p, 0)
        for f in range(5):
            slot = f * 4 + x
            extra = jnp.where(lane == 127, roll_z(above, 127 - slot), 0.0)
            extra = extra - jnp.where(lane == 0, roll_z(below, -slot), 0.0)
            if x == 0:
                extra = extra - outer[x][f]
            if x == 3:
                extra = extra + outer[x][f]
            hold[x, f] = part[f, x] - (FLOW_STEP * 0.25) * extra
        copies += begin(sems, x, (hold.at[x], inc.at[:, x]))
    finish(copies)


def send_body(req, table, _, send, hold, sems):
    wanted = req[...].astype(BF16)
    row, col = iota((1024, 128), 0), iota((1024, 128), 1)
    spread = jnp.where(row // 8 == col, 1.0, 0.0).astype(BF16)
    rep = jnp.dot(spread, wanted, preferred_element_type=F32)
    own = jnp.where(row % 4 == col, rep, 0.0).astype(BF16)
    value = jnp.dot(own, jnp.ones((128, 128), BF16), preferred_element_type=F32)
    target = value + ((row % 8) // 4 * 16).astype(F32)
    pick = jnp.where(col.astype(F32) == target, 1.0, 0.0).astype(BF16)
    copies = []
    for part in range(3):
        rows = jnp.dot(
            pick, table[:, 256 * part : 256 * part + 256], preferred_element_type=F32
        )
        a = rows[:, 0:128].reshape(128, 8, 128)
        b = rows[:, 128:256].reshape(128, 8, 128)
        hold[part] = jnp.concatenate([a, b], 1).astype(BF16)
        copies += begin(sems, part, (hold.at[part], send.at[:, 16 * part : 16 * part + 16, :]))
    finish(copies)


def gather_source(got, pick):
    t = got[...].astype(F32)
    rhs = jnp.concatenate(
        [
            t[:, 0:8, :].reshape(1024, 128).astype(BF16),
            t[:, 8:16, :].reshape(1024, 128).astype(BF16),
        ],
        1,
    )
    even = jnp.dot(pick[0], rhs, preferred_element_type=F32)
    odd = jnp.dot(pick[1], rhs, preferred_element_type=F32)
    return jnp.concatenate([even[:, 0:128], odd[:, 0:128], even[:, 128:256], odd[:, 128:256]], 1)


def prepare_body(nb_far, slot_far, _, gcat, ge, go, esrc, edst, spot_out, *scratch):
    gcat_v, gx0_v, gx1_v, esrc_v, edst_v, spot_v, nb, slot, sems = scratch
    fetch = begin(sems, 0, (nb_far, nb), (slot_far, slot))
    me = lax.axis_index("solver") * lax.axis_size("space") + lax.axis_index("space")
    finish(fetch)
    owner, row = nb[...] // EL, nb[...] % EL
    away = jnp.where(owner == me, 0, EL)
    spot = slot[...] // 4 * 8 + slot[...] % 4
    cols = [row[f : f + 1] + away[f : f + 1] for f in range(2)]
    even = is_even("space")
    cols = [jnp.where(even, cols[1], cols[0]), jnp.where(even, cols[0], cols[1])]
    cols += [row[f : f + 1] for f in range(2, 6)] + [spot]
    eye = iota((EL, EL), 0) == iota((EL, EL), 1)
    spread = [jnp.where(eye, c.astype(F32), 0.0) for c in cols]
    coarse = [jnp.floor(t * (1.0 / 32.0)) for t in spread]
    fine = [t - 32.0 * c for t, c in zip(spread, coarse)]
    ones = jnp.ones((EL, 128), BF16)
    coarse = jnp.dot(jnp.concatenate(coarse, 0).astype(BF16), ones, preferred_element_type=F32)
    fine = jnp.dot(jnp.concatenate(fine, 0).astype(BF16), ones, preferred_element_type=F32)
    column = 32.0 * coarse + fine
    lane = iota((EL, 128), 1).astype(F32)

    def onehot(ref, col, width):
        number = column[col * EL : (col + 1) * EL]
        for t in range(0, width, 128):
            n = min(128, width - t)
            hit = jnp.where(lane + t == number, 1.0, 0.0).astype(BF16)
            ref[:, t : t + n] = hit[:, :n]

    onehot(gx0_v, 0, 2 * EL)
    onehot(gx1_v, 1, 2 * EL)
    copies = begin(sems, 2, (gx0_v, ge), (gx1_v, go))
    for t in range(0, 4 * EL, 128):
        hit = jnp.zeros((EL, 128), jnp.bool_)
        for f in range(4):
            hit = hit | (lane + t == column[(2 + f) * EL : (3 + f) * EL] + f * EL)
        gcat_v[:, t : t + 128] = jnp.where(hit, 1.0, 0.0).astype(BF16)
    copies += begin(sems, 4, (gcat_v, gcat))
    spot_v[...] = column[6 * EL : 7 * EL]
    copies += begin(sems, 5, (spot_v, spot_out))

    def node(c, flip):
        face, a, b = c // 64, c % 64 // 8, c % 8
        low = face % 2 == (1 if flip else 0)
        spot = jnp.where(low, 0, 7)
        return jnp.where(face < 2, a * 64 + spot * 8 + b, a * 64 + b * 8 + spot)

    esrc_v[...] = jnp.where(
        iota((512, 256), 0) == node(iota((512, 256), 1), True), 1.0, 0.0
    ).astype(BF16)
    edst_v[...] = jnp.where(
        iota((256, 512), 1) == node(iota((256, 512), 0), False), 1.0, 0.0
    ).astype(BF16)
    copies += begin(sems, 6, (esrc_v, esrc), (edst_v, edst))
    finish(copies)


def face_count():
    n = iota((1, NODES), 1)
    count = jnp.zeros((1, NODES), I32)
    for part in (n // 64, n // 8 % 8, n % 8):
        count = count + jnp.where((part == 0) | (part == 7), 1, 0)
    return count.astype(F32)


def times(a, b):
    return lax.dot_general(a, b, (((1,), (1,)), ((), ())), preferred_element_type=F32)


def local_terms(q, dx, dy, dz, gcat, esrc, edst, ready=lambda *refs: None):
    traces = jnp.dot(jnp.concatenate(q, 0), esrc[...], preferred_element_type=F32).astype(BF16)
    wide = jnp.concatenate([traces[v * EL : (v + 1) * EL] for v in range(4)], 1)
    lane = iota((1, 1024), 1) % 256 // 64
    rhs = jnp.concatenate(
        [wide * jnp.where(lane == f, 1.0, 0.0).astype(BF16) for f in range(4)], 0
    )
    ready(gcat, edst)
    got = jnp.dot(gcat[...], rhs, preferred_element_type=F32).astype(BF16)
    count = face_count()
    out = []
    ready(dx, dy, dz)
    for v in range(4):
        pen = jnp.dot(got[:, v * 256 : (v + 1) * 256], edst[...], preferred_element_type=F32)
        pen = pen - count * q[v].astype(F32)
        if v == 0:
            vol = times(q[1], dx[...]) + times(q[2], dy[...]) + times(q[3], dz[...])
        else:
            vol = times(q[0], (dx, dy, dz)[v - 1][...])
        out.append(pen - vol)
    return out


def cross_terms(ge, go, own_e, own_o, got_e, got_o):
    lane = iota((EL, 128), 1)
    first, last = [], []
    by_even = jnp.concatenate([jnp.concatenate([own_o[w], got_e[w]], 0) for w in range(2)], 1)
    by_odd = jnp.concatenate([jnp.concatenate([own_e[w], got_o[w]], 0) for w in range(2)], 1)
    by_even = jnp.dot(ge[...], by_even, preferred_element_type=F32)
    by_odd = jnp.dot(go[...], by_odd, preferred_element_type=F32)
    even = is_even("space")
    low = jnp.where(even, by_odd, by_even)
    high = jnp.where(even, by_even, by_odd)
    for v in range(4):
        w = v // 2
        a = low[:, w * 128 : (w + 1) * 128]
        b = high[:, w * 128 : (w + 1) * 128]
        if v % 2 == 0:
            b = pltpu.roll(b, 64, 1)
        else:
            a = pltpu.roll(a, 64, 1)
        first.append(jnp.where(lane < 64, a, 0.0))
        last.append(jnp.where(lane < 64, 0.0, b))
    return first, last


def sound_zero_body(*refs):
    given, (bhi, alo, _, _, part, *here), (hold, sems) = refs[:11], refs[11:27], refs[27:]
    coming = {id(to): copy for to, copy in zip(here, begin(sems, 4, *zip(given, here)))}
    ready = lambda *names: finish([coming[id(t)] for t in names])
    q, esrc, gcat, edst, dx, dy, dz, gx0, gx1, olo, ohi = here
    ready(q, esrc)
    rounded = [q[v] for v in range(4)]
    terms = local_terms(rounded, dx, dy, dz, gcat, esrc, edst, ready)
    ready(gx0, gx1, olo, ohi)
    first, last = cross_terms(gx0, gx1, olo, ohi, bhi, alo)
    copies = []
    for v in range(4):
        full_term = jnp.concatenate(
            [
                terms[v][:, 0:128] + first[v],
                terms[v][:, 128:384],
                terms[v][:, 384:512] + last[v],
            ],
            1,
        )
        hold[v] = q[v].astype(F32) + SOUND_STEP * full_term
        copies += begin(sems, v, (hold.at[v], part.at[v]))
    finish(copies)


def sources_body(got, spot, part, _, __, q1, src, lo, hi, token, spot_v, pick_v, part_v, token_v, sems):
    token_v[...] = jnp.zeros_like(token_v)
    copies = begin(
        sems,
        0,
        (spot, spot_v),
        (part.at[0], q1.at[0]),
        *[(part.at[v], part_v.at[v - 1]) for v in (1, 2, 3)],
        (token_v, token),
    )
    lane = iota((EL, 128), 1).astype(F32)
    copies[0].wait()
    for parity in range(2):
        number = spot_v[...] + 4.0 * parity
        for t in range(0, 1024, 128):
            pick_v[parity, :, t : t + 128] = jnp.where(lane + t == number, 1.0, 0.0).astype(BF16)
    for c in range(3):
        s = gather_source(got.at[:, 16 * c : 16 * c + 16, :], pick_v)
        src[c] = s.astype(BF16)
        copies[2 + c].wait()
        q1[1 + c] = part_v[c] + SOUND_STEP * s
    copies[1].wait()
    copies[5].wait()
    store_traces(
        [q1[v, :, 0:128] for v in range(4)],
        [q1[v, :, 384:512] for v in range(4)],
        lo,
        hi,
    )


def sound_one_body(q0, q1, src, dx, dy, dz, gcat, esrc, edst, after, part):
    terms = local_terms([q1[v].astype(BF16) for v in range(4)], dx, dy, dz, gcat, esrc, edst)
    for v in range(4):
        t = terms[v] if v == 0 else terms[v] + src[v - 1].astype(F32)
        part[v] = 0.75 * q0[v].astype(F32) + 0.25 * (q1[v] + SOUND_STEP * t)


def cross_body(scale, gx0, gx1, olo, ohi, bhi, alo, part, ends, lo, hi):
    first, last = cross_terms(gx0, gx1, olo, ohi, bhi, alo)
    tiles = [[], []]
    for v in range(4):
        a = part[v, :, 0:128] + scale * first[v]
        b = part[v, :, 384:512] + scale * last[v]
        ends[0, v] = a
        ends[1, v] = b
        tiles[0].append(a)
        tiles[1].append(b)
    store_traces(tiles[0], tiles[1], lo, hi)


def sound_two_body(q0, mid, ends, src, dx, dy, dz, gcat, esrc, edst, out, rest, hold, sems):
    q2 = [jnp.concatenate([ends[0, v], mid[v, :, 128:384], ends[1, v]], 1) for v in range(4)]
    terms = local_terms([t.astype(BF16) for t in q2], dx, dy, dz, gcat, esrc, edst)
    copies = []
    for v in range(4):
        t = terms[v] if v == 0 else terms[v] + src[v - 1].astype(F32)
        start = q0[v].astype(F32)
        t = start * (1.0 / 3.0) + (2.0 / 3.0) * (q2[v] + SOUND_STEP * t) - start
        hold[v] = t[:, 128:384]
        rest[0, v] = t[:, 0:128]
        rest[1, v] = t[:, 384:512]
        copies += begin(sems, v, (hold.at[v], out.at[v, :, 128:384]))
    finish(copies)


def final_body(scale, gx0, gx1, olo, ohi, bhi, alo, rest, given, out, hold, sems):
    first, last = cross_terms(gx0, gx1, olo, ohi, bhi, alo)
    copies = []
    for v in range(4):
        hold[0, v] = rest[0, v] + scale * first[v]
        hold[1, v] = rest[1, v] + scale * last[v]
        copies += begin(
            sems, 2 * v, (hold.at[0, v], out.at[v, :, 0:128]), (hold.at[1, v], out.at[v, :, 384:512])
        )
    finish(copies)


def swap(even, odd, axis):
    count = lax.axis_size(axis)
    by_even = [(i, i + 1 - 2 * (i % 2)) for i in range(count)]
    by_odd = [(i, (i - 1 + 2 * (i % 2)) % count) for i in range(count)]
    return lax.ppermute(even, axis, by_even), lax.ppermute(odd, axis, by_odd)


def local(flow_state, acoustic_state, dx, dy, dz, requests, elem_slot, neighbours):
    both = ("solver", "space")
    grid = full(5, 4, 128, 128)
    plane, column = full(5, 128, 128), full(128, 128)
    state = full(4, EL, NODES)
    traces = [half(2, EL, 128)] * 2
    keep = lambda *shape: pltpu.VMEM(shape, F32)
    keep_half = lambda *shape: pltpu.VMEM(shape, BF16)

    packs = call(
        edges_body,
        [plane, plane, column, column] + traces + [column],
        "edges",
        (flow_state, acoustic_state, requests.reshape(128, 4).T),
        scratch=[keep(4, 5, 128, 128), keep_half(2, 4, EL, 128), pltpu.VMEM((4, 128), I32), dma(9)],
        far=(0, 1, 2),
    )
    ue, uo, ze, zo, qe, qo, wanted = packs
    wanted = lax.all_to_all(
        wanted.reshape(128, 1, 128), both, split_axis=0, concat_axis=0, tiled=True
    ).reshape(128, 128)
    ue, uo = swap(ue, uo, "space")
    ze, zo = swap(ze, zo, "solver")
    got_qe, got_qo = swap(qe, qo, "space")

    table = call(
        lamb_body,
        half(128, 768),
        "lamb",
        (flow_state, ue, uo, ze, zo),
        scratch=[keep(3, 6, 128, 128), keep(6, 128, 128)],
    )
    shapes = [(EL, 4 * EL), (EL, 2 * EL), (EL, 2 * EL), (512, 256), (256, 512)]
    gcat, ge, go, esrc, edst, spot = call(
        prepare_body,
        [half(*t) for t in shapes] + [full(EL, 128)],
        "prepare",
        (neighbours, elem_slot.reshape(1, EL), ue),
        scratch=[keep_half(*t) for t in shapes]
        + [keep(EL, 128), pltpu.VMEM((6, EL), I32), pltpu.VMEM((1, EL), I32), dma(8)],
        far=(0, 1, 2),
        far_out=range(6),
    )
    table, got_qe, got_qo = lax.optimization_barrier((table, got_qe, got_qo))
    send = call(
        send_body,
        half(128, 48, 128),
        "send",
        (wanted, table, gcat),
        scratch=[keep_half(3, 128, 16, 128), dma(3)],
        far=(2,),
        far_out=(0,),
    )
    got = lax.all_to_all(send, both, split_axis=0, concat_axis=0, tiled=True)

    first, ce, co, ye, yo = call(
        stage_one_body,
        [grid] + [half(5, 128, 128)] * 2 + [column, column],
        "flow_one",
        (flow_state, ue, uo, ze, zo),
        scratch=[
            keep(5, 6, 128, 128),
            keep(4, 5, 128, 128),
            keep_half(2, 5, 128, 128),
            keep(2, 128, 128),
            keep(2, 5, 128, 128),
            keep(2, 128, 128),
            dma(12),
        ],
        far=range(1, 5),
        far_out=range(5),
    )
    ye, yo = swap(ye, yo, "solver")
    ce, co = swap(ce, co, "space")

    given = (acoustic_state, esrc, gcat, edst, dx, dy, dz, ge, go, qe, qo)
    part = call(
        sound_zero_body,
        state,
        "sound_zero",
        given + (got_qe, got_qo, first, ye),
        scratch=[keep_half(*t.shape) for t in given] + [keep(4, EL, NODES), dma(15)],
        far=[*range(11), 13],
        far_out=(0,),
    )

    inner = call(
        stage_two_inner_body,
        grid,
        "flow_inner",
        (flow_state, first),
        scratch=[keep(5, 6, 128, 128), keep(4, 5, 128, 128), dma(4)],
        far_out=(0,),
    )
    q1, src, qe, qo, token = call(
        sources_body,
        [state, half(3, EL, NODES)] + traces + [full(8, 128)],
        "sources",
        (got, spot, part, yo, inner),
        scratch=[keep(EL, 128), keep_half(2, EL, 1024), keep(3, EL, NODES), keep(8, 128), dma(6)],
        far=(1, 2, 4),
        far_out=(4,),
    )
    mats = (dx, dy, dz, gcat, esrc, edst)
    got_qe, got_qo = swap(qe, qo, "space")
    flow_increment = call(
        stage_two_body,
        grid,
        "flow_two",
        (inner, ue, uo, ce, co, ye, yo, token),
        scratch=[keep(4, 5, 128, 128), keep(2, 5, 128, 128), dma(6)],
        far=(1, 2, 7),
        far_out=(0,),
    )
    part = call(
        sound_one_body,
        state,
        "sound_one",
        (acoustic_state, q1, src) + mats + (flow_increment,),
        far=(9,),
    )
    ends, qe, qo = call(
        lambda *r: cross_body(0.25 * SOUND_STEP, *r),
        [full(2, 4, EL, 128)] + traces,
        "cross_one",
        (ge, go, qe, qo, got_qe, got_qo, part),
    )
    got_qe, got_qo = swap(qe, qo, "space")
    out, rest = call(
        sound_two_body,
        [state, full(2, 4, EL, 128)],
        "sound_two",
        (acoustic_state, part, ends, src) + mats,
        scratch=[keep(4, EL, 256), dma(4)],
        far_out=(0,),
    )
    out = call(
        lambda *r: final_body(2.0 / 3.0 * SOUND_STEP, *r),
        state,
        "cross_two",
        (ge, go, qe, qo, got_qe, got_qo, rest, out),
        scratch=[keep(2, 4, EL, 128), dma(8)],
        far=(7,),
        far_out=(0,),
        aliases={7: 0},
    )
    return flow_increment, out


def solution(mesh):
    both = ("solver", "space")
    grid = P(None, "space", None, "solver")
    sound = P(None, both, None)
    in_specs = (grid, sound, P(), P(), P(), P(both, None, None), P(both), P(None, both))
    return jax.shard_map(
        local, mesh=mesh, in_specs=in_specs, out_specs=(grid, sound), check_vma=False
    )
```

```python
import jax
import jax.numpy as jnp
from jax import lax
from jax.experimental import pallas as pl
from jax.experimental.pallas import tpu as pltpu
from jax.sharding import PartitionSpec as P

F32 = jnp.float32
BF16 = jnp.bfloat16
I32 = jnp.int32

EL = 224
NODES = 512
FLOW_STEP = 0.2
SOUND_STEP = 0.2
VMEM_LIMIT = 20 * 1024 * 1024


def iota(shape, dim):
    return lax.broadcasted_iota(I32, shape, dim)


def full(*shape):
    return jax.ShapeDtypeStruct(shape, F32)


def half(*shape):
    return jax.ShapeDtypeStruct(shape, BF16)


def call(body, outs, name, args, scratch=(), aliases=None, far=(), far_out=()):
    space = [pl.BlockSpec(memory_space=pltpu.VMEM), pl.BlockSpec(memory_space=pltpu.HBM)]
    many = isinstance(outs, (list, tuple))
    outs = list(outs) if many else [outs]
    out_specs = [space[i in far_out] for i in range(len(outs))]
    outs = [pltpu.HBM(t.shape, t.dtype) if i in far_out else t for i, t in enumerate(outs)]
    args = [
        pltpu.with_memory_space_constraint(t, pltpu.HBM) if i in far else t
        for i, t in enumerate(args)
    ]
    return pl.pallas_call(
        body,
        out_shape=outs if many else outs[0],
        in_specs=[space[i in far] for i in range(len(args))],
        out_specs=out_specs if many else out_specs[0],
        scratch_shapes=list(scratch),
        name=name,
        input_output_aliases=aliases or {},
        compiler_params=pltpu.CompilerParams(vmem_limit_bytes=VMEM_LIMIT),
    )(*args)


def begin(sems, first, *pairs):
    out = []
    for i, (source, target) in enumerate(pairs):
        copy = pltpu.make_async_copy(source, target, sems.at[first + i])
        copy.start()
        out.append(copy)
    return out


def finish(copies):
    for copy in copies:
        copy.wait()


def is_even(axis):
    return lax.rem(lax.axis_index(axis), 2) == 0


def dma(n):
    return pltpu.SemaphoreType.DMA((n,))


def primitives(rows):
    v1, v2, v3 = rows[1] / rows[0], rows[2] / rows[0], rows[3] / rows[0]
    p = 0.4 * (rows[4] - 0.5 * (rows[1] * v1 + rows[2] * v2 + rows[3] * v3))
    return (v1, v2, v3), p


def flux(rows, v, p, k):
    along = v[k]
    out = [rows[1 + k]]
    for c in range(3):
        t = rows[1 + c] * along
        out.append(t + p if c == k else t)
    out.append((rows[4] + p) * along)
    return out


def roll_y(f, step):
    return pltpu.roll(f, step % f.shape[0], 0)


def roll_z(f, step):
    return pltpu.roll(f, step % f.shape[1], 1)


def put_lane(acc, lane, f, source, target):
    return jnp.where(lane == target, roll_z(f, target - source), acc)


def diff_y(f):
    return roll_y(f, -1) - roll_y(f, 1)


def diff_z(f, lane, below, above, slot):
    up = jnp.where(lane == 127, roll_z(above, 127 - slot), roll_z(f, -1))
    down = jnp.where(lane == 0, roll_z(below, -slot), roll_z(f, 1))
    return up - down


def add_columns(x, fields, lane, lo, hi):
    for f, field in enumerate(fields):
        slot = f * 4 + x
        lo = put_lane(lo, lane, field, 0, slot)
        hi = put_lane(hi, lane, field, 127, slot)
    return lo, hi


def pair_lanes(tiles, upper):
    lane = iota((EL, 128), 1)
    out = []
    for w in range(2):
        a, b = tiles[2 * w], tiles[2 * w + 1]
        if upper:
            out.append(jnp.where(lane < 64, pltpu.roll(a, 64, 1), b))
        else:
            out.append(jnp.where(lane < 64, a, pltpu.roll(b, 64, 1)))
    return out


def store_traces(first_tiles, last_tiles, even_ref, odd_ref):
    lower, upper = pair_lanes(first_tiles, False), pair_lanes(last_tiles, True)
    even = is_even("space")
    for w in range(2):
        even_ref[w] = jnp.where(even, upper[w], lower[w]).astype(BF16)
        odd_ref[w] = jnp.where(even, lower[w], upper[w]).astype(BF16)


def edges_body(u, q, req, ue, uo, ze, zo, qe, qo, want, planes, ends, req_v, sems):
    even = is_even("space")
    ask = begin(sems, 8, (req, req_v))
    copies = begin(
        sems,
        0,
        *[(u.at[:, x], planes.at[x]) for x in range(4)],
        (q.at[:, :, 0:128], ends.at[0]),
        (q.at[:, :, 384:512], ends.at[1]),
        (u.at[:, jnp.where(even, 3, 0)], ue),
        (u.at[:, jnp.where(even, 0, 3)], uo),
    )
    lane = iota((128, 128), 1)
    lo = hi = jnp.zeros((128, 128), F32)
    eye = iota((128, 128), 0) == lane
    place = jnp.where(iota((512, 128), 0) // 128 == iota((512, 128), 1), 1.0, 0.0).astype(BF16)
    finish(ask)
    value = req_v[...].astype(F32)
    spread = [jnp.where(eye, value[c : c + 1], 0.0).astype(BF16) for c in range(4)]
    want[...] = jnp.dot(jnp.concatenate(spread, 1), place, preferred_element_type=F32)
    for x in range(4):
        copies[x].wait()
        rows = [planes[x, f] for f in range(5)]
        v, p = primitives(rows)
        lo, hi = add_columns(x, flux(rows, v, p, 2) + [v[0], v[1]], lane, lo, hi)
    even = is_even("solver")
    ze[...] = jnp.where(even, hi, lo)
    zo[...] = jnp.where(even, lo, hi)
    finish(copies[4:6])
    store_traces(
        [ends[0, v].astype(F32) for v in range(4)],
        [ends[1, v].astype(F32) for v in range(4)],
        qe,
        qo,
    )
    finish(copies[6:8])


def lamb_body(u, xe, xo, ze, zo, table, vel, pooled):
    lane = iota((128, 128), 1)
    for x in range(4):
        for c in range(3):
            vel[c, x + 1] = u[1 + c, x] / u[0, x]
    even = is_even("space")
    by_link = []
    for link in (xe, xo):
        by_link.append([link[1 + c] / link[0] for c in (1, 2)])
    for c in (1, 2):
        by_even, by_odd = by_link[0][c - 1], by_link[1][c - 1]
        vel[c, 0] = jnp.where(even, by_odd, by_even)
        vel[c, 5] = jnp.where(even, by_even, by_odd)
    even = is_even("solver")
    below = jnp.where(even, zo[...], ze[...])
    above = jnp.where(even, ze[...], zo[...])
    for pair in range(2):
        total = None
        for x in (2 * pair, 2 * pair + 1):
            v1, v2, v3 = vel[0, x + 1], vel[1, x + 1], vel[2, x + 1]
            w1 = 0.5 * diff_y(v3) - 0.5 * diff_z(v2, lane, below, above, 24 + x)
            w2 = 0.5 * diff_z(v1, lane, below, above, 20 + x) - 0.5 * (vel[2, x + 2] - vel[2, x])
            w3 = 0.5 * (vel[1, x + 2] - vel[1, x]) - 0.5 * diff_y(v1)
            lamb = [w2 * v3 - w3 * v2, w3 * v1 - w1 * v3, w1 * v2 - w2 * v1]
            total = lamb if total is None else [a + b for a, b in zip(total, lamb)]
        for c in range(3):
            pooled[c * 2 + pair] = total[c]
    even, odd = [], []
    for c in range(6):
        t = pooled.at[c]
        even.append(t[pl.ds(0, 32, stride=4), :] + t[pl.ds(1, 32, stride=4), :])
        odd.append(t[pl.ds(2, 32, stride=4), :] + t[pl.ds(3, 32, stride=4), :])
    rows = jnp.concatenate([jnp.concatenate(even, 0), jnp.concatenate(odd, 0)], 1)
    z, n = iota((256, 128), 0), iota((256, 128), 1)
    pool = jnp.where((z // 128) * 64 + (z % 128) // 2 == n, 0.125, 0.0).astype(F32)
    coarse = jnp.dot(rows, pool, preferred_element_type=F32, precision=lax.Precision.HIGHEST)
    flat = pooled.at[0]
    hold = pooled.at[1]
    flat[...] = coarse[0:128]
    hold[0:64] = coarse[128:192]
    table[...] = jnp.zeros_like(table)
    for t in range(6):
        for par in range(2):
            c, inner = t // 2, (t % 2) * 2 + par
            src = flat if c < 2 else hold
            base = (c % 2) * 64
            piece = src[pl.ds(base + inner, 16, stride=4), :]
            table[par * 16 : par * 16 + 16, t * 128 : (t + 1) * 128] = piece.astype(BF16)


def tendency_plane(x, rows_of, along_a, below, above, lane):
    rows = rows_of(x)
    v, p = primitives(rows)
    fb = flux(rows, v, p, 1)
    fc = flux(rows, v, p, 2)
    out = []
    for f in range(5):
        total = 0.5 * along_a(x, f) + 0.5 * diff_y(fb[f])
        out.append(total + 0.5 * diff_z(fc[f], lane, below, above, f * 4 + x))
    return rows, out


def fill_flux_a(planes, fa):
    for x, rows in planes:
        v, p = primitives(rows)
        for f, t in enumerate(flux(rows, v, p, 0)):
            fa[f, x + 1] = t


def inner_planes(u):
    return [(x, [u[f, x] for f in range(5)]) for x in range(4)]


def stage_one_body(u, ue, uo, ze, zo, first, ce, co, ye, yo, *scratch):
    fa, hold, edge, zpack, halo, zhalo, sems = scratch
    lane = iota((128, 128), 1)
    even, even_z = is_even("space"), is_even("solver")
    e, o = jnp.where(even, 1, 0), jnp.where(even, 0, 1)
    ez, oz = jnp.where(even_z, 1, 0), jnp.where(even_z, 0, 1)
    fetch = begin(
        sems, 8, (ue, halo.at[e]), (uo, halo.at[o]), (ze, zhalo.at[ez]), (zo, zhalo.at[oz])
    )
    fill_flux_a(inner_planes(u), fa)
    finish(fetch)
    fill_flux_a([(x, [halo[i, f] for f in range(5)]) for i, x in enumerate((-1, 4))], fa)
    below, above = zhalo[0], zhalo[1]
    lo = hi = jnp.zeros((128, 128), F32)
    copies = []
    for i, x in enumerate((0, 3, 1, 2)):
        rows, out = tendency_plane(
            x,
            lambda x: [u[f, x] for f in range(5)],
            lambda x, f: fa[f, x + 2] - fa[f, x],
            below,
            above,
            lane,
        )
        now = [rows[f] - FLOW_STEP * out[f] for f in range(5)]
        for f in range(5):
            hold[x, f] = now[f]
        copies += begin(sems, i, (hold.at[x], first.at[:, x]))
        if x in (0, 3):
            for f in range(5):
                edge[i, f] = (-FLOW_STEP * out[f]).astype(BF16)
        v, p = primitives(now)
        lo, hi = add_columns(x, flux(now, v, p, 2), lane, lo, hi)
    zpack[0] = lo
    zpack[1] = hi
    copies += begin(
        sems, 4, (edge.at[e], ce), (edge.at[o], co), (zpack.at[ez], ye), (zpack.at[oz], yo)
    )
    finish(copies)


def stage_two_inner_body(u, first, part, fa, hold, sems):
    lane = iota((128, 128), 1)
    fill_flux_a(inner_planes(first), fa)
    copies = []
    for x, rows in inner_planes(first):
        v, p = primitives(rows)
        fb = flux(rows, v, p, 1)
        fc = flux(rows, v, p, 2)
        for f in range(5):
            along_c = jnp.where(lane == 127, 0.0, roll_z(fc[f], -1))
            along_c = along_c - jnp.where(lane == 0, 0.0, roll_z(fc[f], 1))
            if x == 0:
                along_a = fa[f, x + 2]
            elif x == 3:
                along_a = -fa[f, x]
            else:
                along_a = fa[f, x + 2] - fa[f, x]
            total = 0.5 * along_a + 0.5 * diff_y(fb[f]) + 0.5 * along_c
            hold[x, f] = 0.5 * ((rows[f] - u[f, x]) - FLOW_STEP * total)
        copies += begin(sems, x, (hold.at[x], part.at[:, x]))
    finish(copies)


def stage_two_body(part, ue, uo, ce, co, ze, zo, after, inc, *scratch):
    hold, halo, sems = scratch
    lane = iota((128, 128), 1)
    even, even_z = is_even("space"), is_even("solver")
    e, o = jnp.where(even, 1, 0), jnp.where(even, 0, 1)
    fetch = begin(sems, 4, (ue, halo.at[e]), (uo, halo.at[o]))
    below = jnp.where(even_z, zo[...], ze[...])
    above = jnp.where(even_z, ze[...], zo[...])
    outer, copies = {}, []
    for x in (1, 2, 0, 3):
        if x in (0, 3):
            if not outer:
                finish(fetch)
            i = x // 3
            rows = []
            for f in range(5):
                by_even, by_odd = ce[f].astype(F32), co[f].astype(F32)
                change = jnp.where(even, by_even, by_odd) if i else jnp.where(even, by_odd, by_even)
                rows.append(halo[i, f] + change)
            v, p = primitives(rows)
            outer[x] = flux(rows, v, p, 0)
        for f in range(5):
            slot = f * 4 + x
            extra = jnp.where(lane == 127, roll_z(above, 127 - slot), 0.0)
            extra = extra - jnp.where(lane == 0, roll_z(below, -slot), 0.0)
            if x == 0:
                extra = extra - outer[x][f]
            if x == 3:
                extra = extra + outer[x][f]
            hold[x, f] = part[f, x] - (FLOW_STEP * 0.25) * extra
        copies += begin(sems, x, (hold.at[x], inc.at[:, x]))
    finish(copies)


def send_body(req, table, _, send, hold, sems):
    wanted = req[...].astype(BF16)
    row, col = iota((1024, 128), 0), iota((1024, 128), 1)
    spread = jnp.where(row // 8 == col, 1.0, 0.0).astype(BF16)
    rep = jnp.dot(spread, wanted, preferred_element_type=F32)
    own = jnp.where(row % 4 == col, rep, 0.0).astype(BF16)
    value = jnp.dot(own, jnp.ones((128, 128), BF16), preferred_element_type=F32)
    target = value + ((row % 8) // 4 * 16).astype(F32)
    pick = jnp.where(col.astype(F32) == target, 1.0, 0.0).astype(BF16)
    copies = []
    for part in range(3):
        rows = jnp.dot(
            pick, table[:, 256 * part : 256 * part + 256], preferred_element_type=F32
        )
        a = rows[:, 0:128].reshape(128, 8, 128)
        b = rows[:, 128:256].reshape(128, 8, 128)
        hold[part] = jnp.concatenate([a, b], 1).astype(BF16)
        copies += begin(sems, part, (hold.at[part], send.at[:, 16 * part : 16 * part + 16, :]))
    finish(copies)


def gather_source(got, pick):
    t = got[...].astype(F32)
    rhs = jnp.concatenate(
        [
            t[:, 0:8, :].reshape(1024, 128).astype(BF16),
            t[:, 8:16, :].reshape(1024, 128).astype(BF16),
        ],
        1,
    )
    even = jnp.dot(pick[0], rhs, preferred_element_type=F32)
    odd = jnp.dot(pick[1], rhs, preferred_element_type=F32)
    return jnp.concatenate([even[:, 0:128], odd[:, 0:128], even[:, 128:256], odd[:, 128:256]], 1)


def prepare_body(nb_far, slot_far, _, gcat, ge, go, esrc, edst, spot_out, *scratch):
    gcat_v, gx0_v, gx1_v, esrc_v, edst_v, spot_v, nb, slot, sems = scratch
    fetch = begin(sems, 0, (nb_far, nb), (slot_far, slot))
    me = lax.axis_index("solver") * lax.axis_size("space") + lax.axis_index("space")
    finish(fetch)
    owner, row = nb[...] // EL, nb[...] % EL
    away = jnp.where(owner == me, 0, EL)
    spot = slot[...] // 4 * 8 + slot[...] % 4
    cols = [row[f : f + 1] + away[f : f + 1] for f in range(2)]
    even = is_even("space")
    cols = [jnp.where(even, cols[1], cols[0]), jnp.where(even, cols[0], cols[1])]
    cols += [row[f : f + 1] for f in range(2, 6)] + [spot]
    eye = iota((EL, EL), 0) == iota((EL, EL), 1)
    spread = [jnp.where(eye, c.astype(F32), 0.0) for c in cols]
    coarse = [jnp.floor(t * (1.0 / 32.0)) for t in spread]
    fine = [t - 32.0 * c for t, c in zip(spread, coarse)]
    ones = jnp.ones((EL, 128), BF16)
    coarse = jnp.dot(jnp.concatenate(coarse, 0).astype(BF16), ones, preferred_element_type=F32)
    fine = jnp.dot(jnp.concatenate(fine, 0).astype(BF16), ones, preferred_element_type=F32)
    column = 32.0 * coarse + fine
    lane = iota((EL, 128), 1).astype(F32)

    def onehot(ref, col, width):
        number = column[col * EL : (col + 1) * EL]
        for t in range(0, width, 128):
            n = min(128, width - t)
            hit = jnp.where(lane + t == number, 1.0, 0.0).astype(BF16)
            ref[:, t : t + n] = hit[:, :n]

    onehot(gx0_v, 0, 2 * EL)
    onehot(gx1_v, 1, 2 * EL)
    copies = begin(sems, 2, (gx0_v, ge), (gx1_v, go))
    for t in range(0, 4 * EL, 128):
        hit = jnp.zeros((EL, 128), jnp.bool_)
        for f in range(4):
            hit = hit | (lane + t == column[(2 + f) * EL : (3 + f) * EL] + f * EL)
        gcat_v[:, t : t + 128] = jnp.where(hit, 1.0, 0.0).astype(BF16)
    copies += begin(sems, 4, (gcat_v, gcat))
    spot_v[...] = column[6 * EL : 7 * EL]
    copies += begin(sems, 5, (spot_v, spot_out))

    def node(c, flip):
        face, a, b = c // 64, c % 64 // 8, c % 8
        low = face % 2 == (1 if flip else 0)
        spot = jnp.where(low, 0, 7)
        return jnp.where(face < 2, a * 64 + spot * 8 + b, a * 64 + b * 8 + spot)

    esrc_v[...] = jnp.where(
        iota((512, 256), 0) == node(iota((512, 256), 1), True), 1.0, 0.0
    ).astype(BF16)
    edst_v[...] = jnp.where(
        iota((256, 512), 1) == node(iota((256, 512), 0), False), 1.0, 0.0
    ).astype(BF16)
    copies += begin(sems, 6, (esrc_v, esrc), (edst_v, edst))
    finish(copies)


def face_count():
    n = iota((1, NODES), 1)
    count = jnp.zeros((1, NODES), I32)
    for part in (n // 64, n // 8 % 8, n % 8):
        count = count + jnp.where((part == 0) | (part == 7), 1, 0)
    return count.astype(F32)


def times(a, b):
    return lax.dot_general(a, b, (((1,), (1,)), ((), ())), preferred_element_type=F32)


def local_terms(q, dx, dy, dz, gcat, esrc, edst, ready=lambda *refs: None):
    traces = jnp.dot(jnp.concatenate(q, 0), esrc[...], preferred_element_type=F32).astype(BF16)
    wide = jnp.concatenate([traces[v * EL : (v + 1) * EL] for v in range(4)], 1)
    lane = iota((1, 1024), 1) % 256 // 64
    rhs = jnp.concatenate(
        [wide * jnp.where(lane == f, 1.0, 0.0).astype(BF16) for f in range(4)], 0
    )
    ready(gcat, edst)
    got = jnp.dot(gcat[...], rhs, preferred_element_type=F32).astype(BF16)
    count = face_count()
    out = []
    ready(dx, dy, dz)
    for v in range(4):
        pen = jnp.dot(got[:, v * 256 : (v + 1) * 256], edst[...], preferred_element_type=F32)
        pen = pen - count * q[v].astype(F32)
        if v == 0:
            vol = times(q[1], dx[...]) + times(q[2], dy[...]) + times(q[3], dz[...])
        else:
            vol = times(q[0], (dx, dy, dz)[v - 1][...])
        out.append(pen - vol)
    return out


def cross_terms(ge, go, own_e, own_o, got_e, got_o):
    lane = iota((EL, 128), 1)
    first, last = [], []
    by_even = jnp.concatenate([jnp.concatenate([own_o[w], got_e[w]], 0) for w in range(2)], 1)
    by_odd = jnp.concatenate([jnp.concatenate([own_e[w], got_o[w]], 0) for w in range(2)], 1)
    by_even = jnp.dot(ge[...], by_even, preferred_element_type=F32)
    by_odd = jnp.dot(go[...], by_odd, preferred_element_type=F32)
    even = is_even("space")
    low = jnp.where(even, by_odd, by_even)
    high = jnp.where(even, by_even, by_odd)
    for v in range(4):
        w = v // 2
        a = low[:, w * 128 : (w + 1) * 128]
        b = high[:, w * 128 : (w + 1) * 128]
        if v % 2 == 0:
            b = pltpu.roll(b, 64, 1)
        else:
            a = pltpu.roll(a, 64, 1)
        first.append(jnp.where(lane < 64, a, 0.0))
        last.append(jnp.where(lane < 64, 0.0, b))
    return first, last


def sound_zero_body(*refs):
    given, (bhi, alo, _, _, part, *here), (hold, sems) = refs[:11], refs[11:27], refs[27:]
    coming = {id(to): copy for to, copy in zip(here, begin(sems, 4, *zip(given, here)))}
    ready = lambda *names: finish([coming[id(t)] for t in names])
    q, esrc, gcat, edst, dx, dy, dz, gx0, gx1, olo, ohi = here
    ready(q, esrc)
    rounded = [q[v] for v in range(4)]
    terms = local_terms(rounded, dx, dy, dz, gcat, esrc, edst, ready)
    ready(gx0, gx1, olo, ohi)
    first, last = cross_terms(gx0, gx1, olo, ohi, bhi, alo)
    copies = []
    for v in range(4):
        full_term = jnp.concatenate(
            [
                terms[v][:, 0:128] + first[v],
                terms[v][:, 128:384],
                terms[v][:, 384:512] + last[v],
            ],
            1,
        )
        hold[v] = q[v].astype(F32) + SOUND_STEP * full_term
        copies += begin(sems, v, (hold.at[v], part.at[v]))
    finish(copies)


def sources_body(got, spot, part, _, __, src, even, odd, token, spot_v, pick_v, ends, token_v, sems):
    token_v[...] = jnp.zeros_like(token_v)
    copies = begin(
        sems,
        0,
        (spot, spot_v),
        (part.at[:, :, 0:128], ends.at[0]),
        (part.at[:, :, 384:512], ends.at[1]),
        (token_v, token),
    )
    lane = iota((EL, 128), 1).astype(F32)
    copies[0].wait()
    for parity in range(2):
        number = spot_v[...] + 4.0 * parity
        for t in range(0, 1024, 128):
            pick_v[parity, :, t : t + 128] = jnp.where(lane + t == number, 1.0, 0.0).astype(BF16)
    tiles = []
    for c in range(3):
        s = gather_source(got.at[:, 16 * c : 16 * c + 16, :], pick_v)
        src[c] = s.astype(BF16)
        tiles.append((SOUND_STEP * s[:, 0:128], SOUND_STEP * s[:, 384:512]))
    finish(copies[1:])
    store_traces(
        [ends[0, 0]] + [ends[0, 1 + c] + tiles[c][0] for c in range(3)],
        [ends[1, 0]] + [ends[1, 1 + c] + tiles[c][1] for c in range(3)],
        even,
        odd,
    )


def sound_one_body(q0, start, src, dx, dy, dz, gcat, esrc, edst, _, part):
    given = [src[c].astype(F32) for c in range(3)]
    q1 = [start[0]] + [start[1 + c] + SOUND_STEP * given[c] for c in range(3)]
    terms = local_terms([t.astype(BF16) for t in q1], dx, dy, dz, gcat, esrc, edst)
    for v in range(4):
        t = terms[v] if v == 0 else terms[v] + given[v - 1]
        part[v] = 0.75 * q0[v].astype(F32) + 0.25 * (q1[v] + SOUND_STEP * t)


def cross_body(scale, gx0, gx1, olo, ohi, bhi, alo, part, ends, lo, hi):
    first, last = cross_terms(gx0, gx1, olo, ohi, bhi, alo)
    tiles = [[], []]
    for v in range(4):
        a = part[v, :, 0:128] + scale * first[v]
        b = part[v, :, 384:512] + scale * last[v]
        ends[0, v] = a
        ends[1, v] = b
        tiles[0].append(a)
        tiles[1].append(b)
    store_traces(tiles[0], tiles[1], lo, hi)


def sound_two_body(q0, mid, ends, src, dx, dy, dz, gcat, esrc, edst, out, rest, hold, sems):
    q2 = [jnp.concatenate([ends[0, v], mid[v, :, 128:384], ends[1, v]], 1) for v in range(4)]
    terms = local_terms([t.astype(BF16) for t in q2], dx, dy, dz, gcat, esrc, edst)
    copies = []
    for v in range(4):
        t = terms[v] if v == 0 else terms[v] + src[v - 1].astype(F32)
        start = q0[v].astype(F32)
        t = start * (1.0 / 3.0) + (2.0 / 3.0) * (q2[v] + SOUND_STEP * t) - start
        hold[v] = t[:, 128:384]
        rest[0, v] = t[:, 0:128]
        rest[1, v] = t[:, 384:512]
        copies += begin(sems, v, (hold.at[v], out.at[v, :, 128:384]))
    finish(copies)


def final_body(scale, gx0, gx1, olo, ohi, bhi, alo, rest, given, out, hold, sems):
    first, last = cross_terms(gx0, gx1, olo, ohi, bhi, alo)
    copies = []
    for v in range(4):
        hold[0, v] = rest[0, v] + scale * first[v]
        hold[1, v] = rest[1, v] + scale * last[v]
        copies += begin(
            sems, 2 * v, (hold.at[0, v], out.at[v, :, 0:128]), (hold.at[1, v], out.at[v, :, 384:512])
        )
    finish(copies)


def swap(even, odd, axis):
    count = lax.axis_size(axis)
    by_even = [(i, i + 1 - 2 * (i % 2)) for i in range(count)]
    by_odd = [(i, (i - 1 + 2 * (i % 2)) % count) for i in range(count)]
    return lax.ppermute(even, axis, by_even), lax.ppermute(odd, axis, by_odd)


def local(flow_state, acoustic_state, dx, dy, dz, requests, elem_slot, neighbours):
    both = ("solver", "space")
    grid = full(5, 4, 128, 128)
    plane, column = full(5, 128, 128), full(128, 128)
    state = full(4, EL, NODES)
    traces = [half(2, EL, 128)] * 2
    keep = lambda *shape: pltpu.VMEM(shape, F32)
    keep_half = lambda *shape: pltpu.VMEM(shape, BF16)

    packs = call(
        edges_body,
        [plane, plane, column, column] + traces + [column],
        "edges",
        (flow_state, acoustic_state, requests.reshape(128, 4).T),
        scratch=[keep(4, 5, 128, 128), keep_half(2, 4, EL, 128), pltpu.VMEM((4, 128), I32), dma(9)],
        far=(0, 1, 2),
    )
    ue, uo, ze, zo, qe, qo, wanted = packs
    wanted = lax.all_to_all(
        wanted.reshape(128, 1, 128), both, split_axis=0, concat_axis=0, tiled=True
    ).reshape(128, 128)
    ue, uo = swap(ue, uo, "space")
    ze, zo = swap(ze, zo, "solver")
    got_qe, got_qo = swap(qe, qo, "space")

    table = call(
        lamb_body,
        half(128, 768),
        "lamb",
        (flow_state, ue, uo, ze, zo),
        scratch=[keep(3, 6, 128, 128), keep(6, 128, 128)],
    )
    shapes = [(EL, 4 * EL), (EL, 2 * EL), (EL, 2 * EL), (512, 256), (256, 512)]
    gcat, ge, go, esrc, edst, spot = call(
        prepare_body,
        [half(*t) for t in shapes] + [full(EL, 128)],
        "prepare",
        (neighbours, elem_slot.reshape(1, EL), ue),
        scratch=[keep_half(*t) for t in shapes]
        + [keep(EL, 128), pltpu.VMEM((6, EL), I32), pltpu.VMEM((1, EL), I32), dma(8)],
        far=(0, 1, 2),
        far_out=range(6),
    )
    table, got_qe, got_qo = lax.optimization_barrier((table, got_qe, got_qo))
    send = call(
        send_body,
        half(128, 48, 128),
        "send",
        (wanted, table, gcat),
        scratch=[keep_half(3, 128, 16, 128), dma(3)],
        far=(2,),
        far_out=(0,),
    )
    got = lax.all_to_all(send, both, split_axis=0, concat_axis=0, tiled=True)

    first, ce, co, ye, yo = call(
        stage_one_body,
        [grid] + [half(5, 128, 128)] * 2 + [column, column],
        "flow_one",
        (flow_state, ue, uo, ze, zo),
        scratch=[
            keep(5, 6, 128, 128),
            keep(4, 5, 128, 128),
            keep_half(2, 5, 128, 128),
            keep(2, 128, 128),
            keep(2, 5, 128, 128),
            keep(2, 128, 128),
            dma(12),
        ],
        far=range(1, 5),
        far_out=range(5),
    )
    ye, yo = swap(ye, yo, "solver")
    ce, co = swap(ce, co, "space")

    given = (acoustic_state, esrc, gcat, edst, dx, dy, dz, ge, go, qe, qo)
    part = call(
        sound_zero_body,
        state,
        "sound_zero",
        given + (got_qe, got_qo, first, ye),
        scratch=[keep_half(*t.shape) for t in given] + [keep(4, EL, NODES), dma(15)],
        far=[*range(11), 13],
        far_out=(0,),
    )

    inner = call(
        stage_two_inner_body,
        grid,
        "flow_inner",
        (flow_state, first),
        scratch=[keep(5, 6, 128, 128), keep(4, 5, 128, 128), dma(4)],
        far_out=(0,),
    )
    src, qe, qo, token = call(
        sources_body,
        [half(3, EL, NODES)] + traces + [full(8, 128)],
        "sources",
        (got, spot, part, yo, inner),
        scratch=[keep(EL, 128), keep_half(2, EL, 1024), keep(2, 4, EL, 128), keep(8, 128), dma(4)],
        far=(1, 2, 4),
        far_out=(3,),
    )
    mats = (dx, dy, dz, gcat, esrc, edst)
    got_qe, got_qo = swap(qe, qo, "space")
    flow_increment = call(
        stage_two_body,
        grid,
        "flow_two",
        (inner, ue, uo, ce, co, ye, yo, token),
        scratch=[keep(4, 5, 128, 128), keep(2, 5, 128, 128), dma(6)],
        far=(1, 2, 7),
        far_out=(0,),
    )
    part = call(
        sound_one_body,
        state,
        "sound_one",
        (acoustic_state, part, src) + mats + (flow_increment,),
        far=(9,),
    )
    ends, qe, qo = call(
        lambda *r: cross_body(0.25 * SOUND_STEP, *r),
        [full(2, 4, EL, 128)] + traces,
        "cross_one",
        (ge, go, qe, qo, got_qe, got_qo, part),
    )
    got_qe, got_qo = swap(qe, qo, "space")
    out, rest = call(
        sound_two_body,
        [state, full(2, 4, EL, 128)],
        "sound_two",
        (acoustic_state, part, ends, src) + mats,
        scratch=[keep(4, EL, 256), dma(4)],
        far_out=(0,),
    )
    out = call(
        lambda *r: final_body(2.0 / 3.0 * SOUND_STEP, *r),
        state,
        "cross_two",
        (ge, go, qe, qo, got_qe, got_qo, rest, out),
        scratch=[keep(2, 4, EL, 128), dma(8)],
        far=(7,),
        far_out=(0,),
        aliases={7: 0},
    )
    return flow_increment, out


def solution(mesh):
    both = ("solver", "space")
    grid = P(None, "space", None, "solver")
    sound = P(None, both, None)
    in_specs = (grid, sound, P(), P(), P(), P(both, None, None), P(both), P(None, both))
    return jax.shard_map(
        local, mesh=mesh, in_specs=in_specs, out_specs=(grid, sound), check_vma=False
    )
```

```python
import jax
import jax.numpy as jnp
from jax import lax
from jax.experimental import pallas as pl
from jax.experimental.pallas import tpu as pltpu
from jax.sharding import PartitionSpec as P

F32 = jnp.float32
BF16 = jnp.bfloat16
I32 = jnp.int32

EL = 224
NODES = 512
FLOW_STEP = 0.2
SOUND_STEP = 0.2
VMEM_LIMIT = 20 * 1024 * 1024


def iota(shape, dim):
    return lax.broadcasted_iota(I32, shape, dim)


def full(*shape):
    return jax.ShapeDtypeStruct(shape, F32)


def half(*shape):
    return jax.ShapeDtypeStruct(shape, BF16)


def call(body, outs, name, args, scratch=(), aliases=None, far=(), far_out=()):
    space = [pl.BlockSpec(memory_space=pltpu.VMEM), pl.BlockSpec(memory_space=pltpu.HBM)]
    many = isinstance(outs, (list, tuple))
    outs = list(outs) if many else [outs]
    out_specs = [space[i in far_out] for i in range(len(outs))]
    outs = [pltpu.HBM(t.shape, t.dtype) if i in far_out else t for i, t in enumerate(outs)]
    args = [
        pltpu.with_memory_space_constraint(t, pltpu.HBM) if i in far else t
        for i, t in enumerate(args)
    ]
    return pl.pallas_call(
        body,
        out_shape=outs if many else outs[0],
        in_specs=[space[i in far] for i in range(len(args))],
        out_specs=out_specs if many else out_specs[0],
        scratch_shapes=list(scratch),
        name=name,
        input_output_aliases=aliases or {},
        compiler_params=pltpu.CompilerParams(vmem_limit_bytes=VMEM_LIMIT),
    )(*args)


def begin(sems, first, *pairs):
    out = []
    for i, (source, target) in enumerate(pairs):
        copy = pltpu.make_async_copy(source, target, sems.at[first + i])
        copy.start()
        out.append(copy)
    return out


def finish(copies):
    for copy in copies:
        copy.wait()


def is_even(axis):
    return lax.rem(lax.axis_index(axis), 2) == 0


def dma(n):
    return pltpu.SemaphoreType.DMA((n,))


def primitives(rows):
    v1, v2, v3 = rows[1] / rows[0], rows[2] / rows[0], rows[3] / rows[0]
    p = 0.4 * (rows[4] - 0.5 * (rows[1] * v1 + rows[2] * v2 + rows[3] * v3))
    return (v1, v2, v3), p


def flux(rows, v, p, k):
    along = v[k]
    out = [rows[1 + k]]
    for c in range(3):
        t = rows[1 + c] * along
        out.append(t + p if c == k else t)
    out.append((rows[4] + p) * along)
    return out


def roll_y(f, step):
    return pltpu.roll(f, step % f.shape[0], 0)


def roll_z(f, step):
    return pltpu.roll(f, step % f.shape[1], 1)


def diff_y(f):
    return roll_y(f, -1) - roll_y(f, 1)


def diff_z(f, lane, below, above, slot):
    up = jnp.where(lane == 127, roll_z(above, 126 - 2 * slot), roll_z(f, -1))
    down = jnp.where(lane == 0, roll_z(below, -2 * slot), roll_z(f, 1))
    return up - down


def add_columns(x, fields, lane, pack):
    for f, field in enumerate(fields):
        slot = f * 4 + x
        pack = jnp.where(lane // 2 == slot, roll_z(field, 2 * slot + 1), pack)
    return pack


def pair_lanes(tiles, upper):
    lane = iota((EL, 128), 1)
    out = []
    for w in range(2):
        a, b = tiles[2 * w], tiles[2 * w + 1]
        if upper:
            out.append(jnp.where(lane < 64, pltpu.roll(a, 64, 1), b))
        else:
            out.append(jnp.where(lane < 64, a, pltpu.roll(b, 64, 1)))
    return out


def store_traces(first_tiles, last_tiles, even_ref, odd_ref):
    lower, upper = pair_lanes(first_tiles, False), pair_lanes(last_tiles, True)
    even = is_even("space")
    for w in range(2):
        even_ref[w] = jnp.where(even, upper[w], lower[w]).astype(BF16)
        odd_ref[w] = jnp.where(even, lower[w], upper[w]).astype(BF16)


def edges_body(u, q, req, ue, uo, ze, zo, qe, qo, want, planes, ends, req_v, sems):
    even = is_even("space")
    ask = begin(sems, 8, (req, req_v))
    copies = begin(
        sems,
        0,
        *[(u.at[:, x], planes.at[x]) for x in range(4)],
        (q.at[:, :, 0:128], ends.at[0]),
        (q.at[:, :, 384:512], ends.at[1]),
        (u.at[:, jnp.where(even, 3, 0)], ue),
        (u.at[:, jnp.where(even, 0, 3)], uo),
    )
    lane = iota((128, 128), 1)
    pack = jnp.zeros((128, 128), F32)
    eye = iota((128, 128), 0) == lane
    place = jnp.where(iota((512, 128), 0) // 128 == iota((512, 128), 1), 1.0, 0.0).astype(BF16)
    finish(ask)
    value = req_v[...].astype(F32)
    spread = [jnp.where(eye, value[c : c + 1], 0.0).astype(BF16) for c in range(4)]
    want[...] = jnp.dot(jnp.concatenate(spread, 1), place, preferred_element_type=F32)
    for x in range(4):
        copies[x].wait()
        rows = [planes[x, f] for f in range(5)]
        v, p = primitives(rows)
        pack = add_columns(x, flux(rows, v, p, 2) + [v[0], v[1]], lane, pack)
    ze[...] = pack
    zo[...] = pack
    finish(copies[4:6])
    store_traces(
        [ends[0, v].astype(F32) for v in range(4)],
        [ends[1, v].astype(F32) for v in range(4)],
        qe,
        qo,
    )
    finish(copies[6:8])


def lamb_body(u, xe, xo, ze, zo, table, vel, pooled):
    lane = iota((128, 128), 1)
    for x in range(4):
        for c in range(3):
            vel[c, x + 1] = u[1 + c, x] / u[0, x]
    even = is_even("space")
    by_link = []
    for link in (xe, xo):
        by_link.append([link[1 + c] / link[0] for c in (1, 2)])
    for c in (1, 2):
        by_even, by_odd = by_link[0][c - 1], by_link[1][c - 1]
        vel[c, 0] = jnp.where(even, by_odd, by_even)
        vel[c, 5] = jnp.where(even, by_even, by_odd)
    even = is_even("solver")
    below = jnp.where(even, zo[...], ze[...])
    above = jnp.where(even, ze[...], zo[...])
    for pair in range(2):
        total = None
        for x in (2 * pair, 2 * pair + 1):
            v1, v2, v3 = vel[0, x + 1], vel[1, x + 1], vel[2, x + 1]
            w1 = 0.5 * diff_y(v3) - 0.5 * diff_z(v2, lane, below, above, 24 + x)
            w2 = 0.5 * diff_z(v1, lane, below, above, 20 + x) - 0.5 * (vel[2, x + 2] - vel[2, x])
            w3 = 0.5 * (vel[1, x + 2] - vel[1, x]) - 0.5 * diff_y(v1)
            lamb = [w2 * v3 - w3 * v2, w3 * v1 - w1 * v3, w1 * v2 - w2 * v1]
            total = lamb if total is None else [a + b for a, b in zip(total, lamb)]
        for c in range(3):
            pooled[c * 2 + pair] = total[c]
    even, odd = [], []
    for c in range(6):
        t = pooled.at[c]
        even.append(t[pl.ds(0, 32, stride=4), :] + t[pl.ds(1, 32, stride=4), :])
        odd.append(t[pl.ds(2, 32, stride=4), :] + t[pl.ds(3, 32, stride=4), :])
    rows = jnp.concatenate([jnp.concatenate(even, 0), jnp.concatenate(odd, 0)], 1)
    z, n = iota((256, 128), 0), iota((256, 128), 1)
    pool = jnp.where((z // 128) * 64 + (z % 128) // 2 == n, 0.125, 0.0).astype(F32)
    coarse = jnp.dot(rows, pool, preferred_element_type=F32, precision=lax.Precision.HIGHEST)
    flat = pooled.at[0]
    hold = pooled.at[1]
    flat[...] = coarse[0:128]
    hold[0:64] = coarse[128:192]
    table[...] = jnp.zeros_like(table)
    for t in range(6):
        for par in range(2):
            c, inner = t // 2, (t % 2) * 2 + par
            src = flat if c < 2 else hold
            base = (c % 2) * 64
            piece = src[pl.ds(base + inner, 16, stride=4), :]
            table[par * 16 : par * 16 + 16, t * 128 : (t + 1) * 128] = piece.astype(BF16)


def tendency_plane(x, rows_of, along_a, below, above, lane):
    rows = rows_of(x)
    v, p = primitives(rows)
    fb = flux(rows, v, p, 1)
    fc = flux(rows, v, p, 2)
    out = []
    for f in range(5):
        total = 0.5 * along_a(x, f) + 0.5 * diff_y(fb[f])
        out.append(total + 0.5 * diff_z(fc[f], lane, below, above, f * 4 + x))
    return rows, out


def fill_flux_a(planes, fa):
    for x, rows in planes:
        v, p = primitives(rows)
        for f, t in enumerate(flux(rows, v, p, 0)):
            fa[f, x + 1] = t


def inner_planes(u):
    return [(x, [u[f, x] for f in range(5)]) for x in range(4)]


def stage_one_body(u, ue, uo, ze, zo, first, ce, co, ye, yo, *scratch):
    fa, hold, edge, zpack, halo, zhalo, sems = scratch
    lane = iota((128, 128), 1)
    even, even_z = is_even("space"), is_even("solver")
    e, o = jnp.where(even, 1, 0), jnp.where(even, 0, 1)
    ez, oz = jnp.where(even_z, 1, 0), jnp.where(even_z, 0, 1)
    fetch = begin(
        sems, 8, (ue, halo.at[e]), (uo, halo.at[o]), (ze, zhalo.at[ez]), (zo, zhalo.at[oz])
    )
    fill_flux_a(inner_planes(u), fa)
    finish(fetch)
    fill_flux_a([(x, [halo[i, f] for f in range(5)]) for i, x in enumerate((-1, 4))], fa)
    below, above = zhalo[0], zhalo[1]
    pack = jnp.zeros((128, 128), F32)
    copies = []
    for i, x in enumerate((0, 3, 1, 2)):
        rows, out = tendency_plane(
            x,
            lambda x: [u[f, x] for f in range(5)],
            lambda x, f: fa[f, x + 2] - fa[f, x],
            below,
            above,
            lane,
        )
        now = [rows[f] - FLOW_STEP * out[f] for f in range(5)]
        for f in range(5):
            hold[x, f] = now[f]
        copies += begin(sems, i, (hold.at[x], first.at[:, x]))
        if x in (0, 3):
            for f in range(5):
                edge[i, f] = (-FLOW_STEP * out[f]).astype(BF16)
        v, p = primitives(now)
        pack = add_columns(x, flux(now, v, p, 2), lane, pack)
    zpack[...] = pack
    copies += begin(
        sems, 4, (edge.at[e], ce), (edge.at[o], co), (zpack, ye), (zpack, yo)
    )
    finish(copies)


def stage_two_inner_body(u, first, part, fa, hold, sems):
    lane = iota((128, 128), 1)
    fill_flux_a(inner_planes(first), fa)
    copies = []
    for x, rows in inner_planes(first):
        v, p = primitives(rows)
        fb = flux(rows, v, p, 1)
        fc = flux(rows, v, p, 2)
        for f in range(5):
            along_c = jnp.where(lane == 127, 0.0, roll_z(fc[f], -1))
            along_c = along_c - jnp.where(lane == 0, 0.0, roll_z(fc[f], 1))
            if x == 0:
                along_a = fa[f, x + 2]
            elif x == 3:
                along_a = -fa[f, x]
            else:
                along_a = fa[f, x + 2] - fa[f, x]
            total = 0.5 * along_a + 0.5 * diff_y(fb[f]) + 0.5 * along_c
            hold[x, f] = 0.5 * ((rows[f] - u[f, x]) - FLOW_STEP * total)
        copies += begin(sems, x, (hold.at[x], part.at[:, x]))
    finish(copies)


def stage_two_body(part, ue, uo, ce, co, ze, zo, after, inc, *scratch):
    hold, halo, sems = scratch
    lane = iota((128, 128), 1)
    even, even_z = is_even("space"), is_even("solver")
    e, o = jnp.where(even, 1, 0), jnp.where(even, 0, 1)
    fetch = begin(sems, 4, (ue, halo.at[e]), (uo, halo.at[o]))
    below = jnp.where(even_z, zo[...], ze[...])
    above = jnp.where(even_z, ze[...], zo[...])
    outer, copies = {}, []
    for x in (1, 2, 0, 3):
        if x in (0, 3):
            if not outer:
                finish(fetch)
            i = x // 3
            rows = []
            for f in range(5):
                by_even, by_odd = ce[f].astype(F32), co[f].astype(F32)
                change = jnp.where(even, by_even, by_odd) if i else jnp.where(even, by_odd, by_even)
                rows.append(halo[i, f] + change)
            v, p = primitives(rows)
            outer[x] = flux(rows, v, p, 0)
        for f in range(5):
            slot = f * 4 + x
            extra = jnp.where(lane == 127, roll_z(above, 126 - 2 * slot), 0.0)
            extra = extra - jnp.where(lane == 0, roll_z(below, -2 * slot), 0.0)
            if x == 0:
                extra = extra - outer[x][f]
            if x == 3:
                extra = extra + outer[x][f]
            hold[x, f] = part[f, x] - (FLOW_STEP * 0.25) * extra
        copies += begin(sems, x, (hold.at[x], inc.at[:, x]))
    finish(copies)


def send_body(req, table, _, send, hold, sems):
    wanted = req[...].astype(BF16)
    row, col = iota((1024, 128), 0), iota((1024, 128), 1)
    spread = jnp.where(row // 8 == col, 1.0, 0.0).astype(BF16)
    rep = jnp.dot(spread, wanted, preferred_element_type=F32)
    own = jnp.where(row % 4 == col, rep, 0.0).astype(BF16)
    value = jnp.dot(own, jnp.ones((128, 128), BF16), preferred_element_type=F32)
    target = value + ((row % 8) // 4 * 16).astype(F32)
    pick = jnp.where(col.astype(F32) == target, 1.0, 0.0).astype(BF16)
    copies = []
    for part in range(3):
        rows = jnp.dot(
            pick, table[:, 256 * part : 256 * part + 256], preferred_element_type=F32
        )
        a = rows[:, 0:128].reshape(128, 8, 128)
        b = rows[:, 128:256].reshape(128, 8, 128)
        hold[part] = jnp.concatenate([a, b], 1).astype(BF16)
        copies += begin(sems, part, (hold.at[part], send.at[:, 16 * part : 16 * part + 16, :]))
    finish(copies)


def gather_source(got, pick):
    t = got[...].astype(F32)
    rhs = jnp.concatenate(
        [
            t[:, 0:8, :].reshape(1024, 128).astype(BF16),
            t[:, 8:16, :].reshape(1024, 128).astype(BF16),
        ],
        1,
    )
    even = jnp.dot(pick[0], rhs, preferred_element_type=F32)
    odd = jnp.dot(pick[1], rhs, preferred_element_type=F32)
    return jnp.concatenate([even[:, 0:128], odd[:, 0:128], even[:, 128:256], odd[:, 128:256]], 1)


def prepare_body(nb_far, slot_far, _, gcat, ge, go, esrc, edst, spot_out, *scratch):
    gcat_v, gx0_v, gx1_v, esrc_v, edst_v, spot_v, nb, slot, sems = scratch
    fetch = begin(sems, 0, (nb_far, nb), (slot_far, slot))
    me = lax.axis_index("solver") * lax.axis_size("space") + lax.axis_index("space")
    finish(fetch)
    owner, row = nb[...] // EL, nb[...] % EL
    away = jnp.where(owner == me, 0, EL)
    spot = slot[...] // 4 * 8 + slot[...] % 4
    cols = [row[f : f + 1] + away[f : f + 1] for f in range(2)]
    even = is_even("space")
    cols = [jnp.where(even, cols[1], cols[0]), jnp.where(even, cols[0], cols[1])]
    cols += [row[f : f + 1] for f in range(2, 6)] + [spot]
    eye = iota((EL, EL), 0) == iota((EL, EL), 1)
    spread = [jnp.where(eye, c.astype(F32), 0.0) for c in cols]
    coarse = [jnp.floor(t * (1.0 / 32.0)) for t in spread]
    fine = [t - 32.0 * c for t, c in zip(spread, coarse)]
    ones = jnp.ones((EL, 128), BF16)
    coarse = jnp.dot(jnp.concatenate(coarse, 0).astype(BF16), ones, preferred_element_type=F32)
    fine = jnp.dot(jnp.concatenate(fine, 0).astype(BF16), ones, preferred_element_type=F32)
    column = 32.0 * coarse + fine
    lane = iota((EL, 128), 1).astype(F32)

    def onehot(ref, col, width):
        number = column[col * EL : (col + 1) * EL]
        for t in range(0, width, 128):
            n = min(128, width - t)
            hit = jnp.where(lane + t == number, 1.0, 0.0).astype(BF16)
            ref[:, t : t + n] = hit[:, :n]

    onehot(gx0_v, 0, 2 * EL)
    onehot(gx1_v, 1, 2 * EL)
    copies = begin(sems, 2, (gx0_v, ge), (gx1_v, go))
    for t in range(0, 4 * EL, 128):
        hit = jnp.zeros((EL, 128), jnp.bool_)
        for f in range(4):
            hit = hit | (lane + t == column[(2 + f) * EL : (3 + f) * EL] + f * EL)
        gcat_v[:, t : t + 128] = jnp.where(hit, 1.0, 0.0).astype(BF16)
    copies += begin(sems, 4, (gcat_v, gcat))
    spot_v[...] = column[6 * EL : 7 * EL]
    copies += begin(sems, 5, (spot_v, spot_out))

    def node(c, flip):
        face, a, b = c // 64, c % 64 // 8, c % 8
        low = face % 2 == (1 if flip else 0)
        spot = jnp.where(low, 0, 7)
        return jnp.where(face < 2, a * 64 + spot * 8 + b, a * 64 + b * 8 + spot)

    esrc_v[...] = jnp.where(
        iota((512, 256), 0) == node(iota((512, 256), 1), True), 1.0, 0.0
    ).astype(BF16)
    edst_v[...] = jnp.where(
        iota((256, 512), 1) == node(iota((256, 512), 0), False), 1.0, 0.0
    ).astype(BF16)
    copies += begin(sems, 6, (esrc_v, esrc), (edst_v, edst))
    finish(copies)


def face_count():
    n = iota((1, NODES), 1)
    count = jnp.zeros((1, NODES), I32)
    for part in (n // 64, n // 8 % 8, n % 8):
        count = count + jnp.where((part == 0) | (part == 7), 1, 0)
    return count.astype(F32)


def times(a, b):
    return lax.dot_general(a, b, (((1,), (1,)), ((), ())), preferred_element_type=F32)


def local_terms(q, dx, dy, dz, gcat, esrc, edst, ready=lambda *refs: None):
    traces = jnp.dot(jnp.concatenate(q, 0), esrc[...], preferred_element_type=F32).astype(BF16)
    wide = jnp.concatenate([traces[v * EL : (v + 1) * EL] for v in range(4)], 1)
    lane = iota((1, 1024), 1) % 256 // 64
    rhs = jnp.concatenate(
        [wide * jnp.where(lane == f, 1.0, 0.0).astype(BF16) for f in range(4)], 0
    )
    ready(gcat, edst)
    got = jnp.dot(gcat[...], rhs, preferred_element_type=F32).astype(BF16)
    count = face_count()
    out = []
    ready(dx, dy, dz)
    for v in range(4):
        pen = jnp.dot(got[:, v * 256 : (v + 1) * 256], edst[...], preferred_element_type=F32)
        pen = pen - count * q[v].astype(F32)
        if v == 0:
            vol = times(q[1], dx[...]) + times(q[2], dy[...]) + times(q[3], dz[...])
        else:
            vol = times(q[0], (dx, dy, dz)[v - 1][...])
        out.append(pen - vol)
    return out


def cross_terms(ge, go, own_e, own_o, got_e, got_o):
    lane = iota((EL, 128), 1)
    first, last = [], []
    by_even = jnp.concatenate([jnp.concatenate([own_o[w], got_e[w]], 0) for w in range(2)], 1)
    by_odd = jnp.concatenate([jnp.concatenate([own_e[w], got_o[w]], 0) for w in range(2)], 1)
    by_even = jnp.dot(ge[...], by_even, preferred_element_type=F32)
    by_odd = jnp.dot(go[...], by_odd, preferred_element_type=F32)
    even = is_even("space")
    low = jnp.where(even, by_odd, by_even)
    high = jnp.where(even, by_even, by_odd)
    for v in range(4):
        w = v // 2
        a = low[:, w * 128 : (w + 1) * 128]
        b = high[:, w * 128 : (w + 1) * 128]
        if v % 2 == 0:
            b = pltpu.roll(b, 64, 1)
        else:
            a = pltpu.roll(a, 64, 1)
        first.append(jnp.where(lane < 64, a, 0.0))
        last.append(jnp.where(lane < 64, 0.0, b))
    return first, last


def sound_zero_body(*refs):
    given, (bhi, alo, _, _, part, *here), (hold, sems) = refs[:11], refs[11:27], refs[27:]
    coming = {id(to): copy for to, copy in zip(here, begin(sems, 4, *zip(given, here)))}
    ready = lambda *names: finish([coming[id(t)] for t in names])
    q, esrc, gcat, edst, dx, dy, dz, gx0, gx1, olo, ohi = here
    ready(q, esrc)
    rounded = [q[v] for v in range(4)]
    terms = local_terms(rounded, dx, dy, dz, gcat, esrc, edst, ready)
    ready(gx0, gx1, olo, ohi)
    first, last = cross_terms(gx0, gx1, olo, ohi, bhi, alo)
    copies = []
    for v in range(4):
        full_term = jnp.concatenate(
            [
                terms[v][:, 0:128] + first[v],
                terms[v][:, 128:384],
                terms[v][:, 384:512] + last[v],
            ],
            1,
        )
        hold[v] = q[v].astype(F32) + SOUND_STEP * full_term
        copies += begin(sems, v, (hold.at[v], part.at[v]))
    finish(copies)


def sources_body(got, spot, part, _, __, src, even, odd, token, spot_v, pick_v, ends, token_v, sems):
    token_v[...] = jnp.zeros_like(token_v)
    copies = begin(
        sems,
        0,
        (spot, spot_v),
        (part.at[:, :, 0:128], ends.at[0]),
        (part.at[:, :, 384:512], ends.at[1]),
        (token_v, token),
    )
    lane = iota((EL, 128), 1).astype(F32)
    copies[0].wait()
    for parity in range(2):
        number = spot_v[...] + 4.0 * parity
        for t in range(0, 1024, 128):
            pick_v[parity, :, t : t + 128] = jnp.where(lane + t == number, 1.0, 0.0).astype(BF16)
    tiles = []
    for c in range(3):
        s = gather_source(got.at[:, 16 * c : 16 * c + 16, :], pick_v)
        src[c] = s.astype(BF16)
        tiles.append((SOUND_STEP * s[:, 0:128], SOUND_STEP * s[:, 384:512]))
    finish(copies[1:])
    store_traces(
        [ends[0, 0]] + [ends[0, 1 + c] + tiles[c][0] for c in range(3)],
        [ends[1, 0]] + [ends[1, 1 + c] + tiles[c][1] for c in range(3)],
        even,
        odd,
    )


def sound_one_body(q0, start, src, dx, dy, dz, gcat, esrc, edst, _, part):
    given = [src[c].astype(F32) for c in range(3)]
    q1 = [start[0]] + [start[1 + c] + SOUND_STEP * given[c] for c in range(3)]
    terms = local_terms([t.astype(BF16) for t in q1], dx, dy, dz, gcat, esrc, edst)
    for v in range(4):
        t = terms[v] if v == 0 else terms[v] + given[v - 1]
        part[v] = 0.75 * q0[v].astype(F32) + 0.25 * (q1[v] + SOUND_STEP * t)


def cross_body(scale, gx0, gx1, olo, ohi, bhi, alo, part, ends, lo, hi):
    first, last = cross_terms(gx0, gx1, olo, ohi, bhi, alo)
    tiles = [[], []]
    for v in range(4):
        a = part[v, :, 0:128] + scale * first[v]
        b = part[v, :, 384:512] + scale * last[v]
        ends[0, v] = a
        ends[1, v] = b
        tiles[0].append(a)
        tiles[1].append(b)
    store_traces(tiles[0], tiles[1], lo, hi)


def sound_two_body(q0, mid, ends, src, dx, dy, dz, gcat, esrc, edst, out, rest, hold, sems):
    q2 = [jnp.concatenate([ends[0, v], mid[v, :, 128:384], ends[1, v]], 1) for v in range(4)]
    terms = local_terms([t.astype(BF16) for t in q2], dx, dy, dz, gcat, esrc, edst)
    copies = []
    for v in range(4):
        t = terms[v] if v == 0 else terms[v] + src[v - 1].astype(F32)
        start = q0[v].astype(F32)
        t = start * (1.0 / 3.0) + (2.0 / 3.0) * (q2[v] + SOUND_STEP * t) - start
        hold[v] = t[:, 128:384]
        rest[0, v] = t[:, 0:128]
        rest[1, v] = t[:, 384:512]
        copies += begin(sems, v, (hold.at[v], out.at[v, :, 128:384]))
    finish(copies)


def final_body(scale, gx0, gx1, olo, ohi, bhi, alo, rest, given, out, hold, sems):
    first, last = cross_terms(gx0, gx1, olo, ohi, bhi, alo)
    copies = []
    for v in range(4):
        hold[0, v] = rest[0, v] + scale * first[v]
        hold[1, v] = rest[1, v] + scale * last[v]
        copies += begin(
            sems, 2 * v, (hold.at[0, v], out.at[v, :, 0:128]), (hold.at[1, v], out.at[v, :, 384:512])
        )
    finish(copies)


def swap(even, odd, axis):
    count = lax.axis_size(axis)
    by_even = [(i, i + 1 - 2 * (i % 2)) for i in range(count)]
    by_odd = [(i, (i - 1 + 2 * (i % 2)) % count) for i in range(count)]
    return lax.ppermute(even, axis, by_even), lax.ppermute(odd, axis, by_odd)


def local(flow_state, acoustic_state, dx, dy, dz, requests, elem_slot, neighbours):
    both = ("solver", "space")
    grid = full(5, 4, 128, 128)
    plane, column = full(5, 128, 128), full(128, 128)
    state = full(4, EL, NODES)
    traces = [half(2, EL, 128)] * 2
    keep = lambda *shape: pltpu.VMEM(shape, F32)
    keep_half = lambda *shape: pltpu.VMEM(shape, BF16)

    packs = call(
        edges_body,
        [plane, plane, column, column] + traces + [column],
        "edges",
        (flow_state, acoustic_state, requests.reshape(128, 4).T),
        scratch=[keep(4, 5, 128, 128), keep_half(2, 4, EL, 128), pltpu.VMEM((4, 128), I32), dma(9)],
        far=(0, 1, 2),
    )
    ue, uo, ze, zo, qe, qo, wanted = packs
    wanted = lax.all_to_all(
        wanted.reshape(128, 1, 128), both, split_axis=0, concat_axis=0, tiled=True
    ).reshape(128, 128)
    ue, uo = swap(ue, uo, "space")
    ze, zo = swap(ze, zo, "solver")
    got_qe, got_qo = swap(qe, qo, "space")

    table = call(
        lamb_body,
        half(128, 768),
        "lamb",
        (flow_state, ue, uo, ze, zo),
        scratch=[keep(3, 6, 128, 128), keep(6, 128, 128)],
    )
    shapes = [(EL, 4 * EL), (EL, 2 * EL), (EL, 2 * EL), (512, 256), (256, 512)]
    gcat, ge, go, esrc, edst, spot = call(
        prepare_body,
        [half(*t) for t in shapes] + [full(EL, 128)],
        "prepare",
        (neighbours, elem_slot.reshape(1, EL), ue),
        scratch=[keep_half(*t) for t in shapes]
        + [keep(EL, 128), pltpu.VMEM((6, EL), I32), pltpu.VMEM((1, EL), I32), dma(8)],
        far=(0, 1, 2),
        far_out=range(6),
    )
    table, got_qe, got_qo = lax.optimization_barrier((table, got_qe, got_qo))
    send = call(
        send_body,
        half(128, 48, 128),
        "send",
        (wanted, table, gcat),
        scratch=[keep_half(3, 128, 16, 128), dma(3)],
        far=(2,),
        far_out=(0,),
    )
    got = lax.all_to_all(send, both, split_axis=0, concat_axis=0, tiled=True)

    first, ce, co, ye, yo = call(
        stage_one_body,
        [grid] + [half(5, 128, 128)] * 2 + [column, column],
        "flow_one",
        (flow_state, ue, uo, ze, zo),
        scratch=[
            keep(5, 6, 128, 128),
            keep(4, 5, 128, 128),
            keep_half(2, 5, 128, 128),
            keep(128, 128),
            keep(2, 5, 128, 128),
            keep(2, 128, 128),
            dma(12),
        ],
        far=range(1, 5),
        far_out=range(5),
    )
    ye, yo = swap(ye, yo, "solver")
    ce, co = swap(ce, co, "space")

    given = (acoustic_state, esrc, gcat, edst, dx, dy, dz, ge, go, qe, qo)
    part = call(
        sound_zero_body,
        state,
        "sound_zero",
        given + (got_qe, got_qo, first, ye),
        scratch=[keep_half(*t.shape) for t in given] + [keep(4, EL, NODES), dma(15)],
        far=[*range(11), 13],
        far_out=(0,),
    )

    inner = call(
        stage_two_inner_body,
        grid,
        "flow_inner",
        (flow_state, first),
        scratch=[keep(5, 6, 128, 128), keep(4, 5, 128, 128), dma(4)],
        far_out=(0,),
    )
    src, qe, qo, token = call(
        sources_body,
        [half(3, EL, NODES)] + traces + [full(8, 128)],
        "sources",
        (got, spot, part, yo, inner),
        scratch=[keep(EL, 128), keep_half(2, EL, 1024), keep(2, 4, EL, 128), keep(8, 128), dma(4)],
        far=(1, 2, 4),
        far_out=(3,),
    )
    mats = (dx, dy, dz, gcat, esrc, edst)
    got_qe, got_qo = swap(qe, qo, "space")
    flow_increment = call(
        stage_two_body,
        grid,
        "flow_two",
        (inner, ue, uo, ce, co, ye, yo, token),
        scratch=[keep(4, 5, 128, 128), keep(2, 5, 128, 128), dma(6)],
        far=(1, 2, 7),
        far_out=(0,),
    )
    part = call(
        sound_one_body,
        state,
        "sound_one",
        (acoustic_state, part, src) + mats + (flow_increment,),
        far=(9,),
    )
    ends, qe, qo = call(
        lambda *r: cross_body(0.25 * SOUND_STEP, *r),
        [full(2, 4, EL, 128)] + traces,
        "cross_one",
        (ge, go, qe, qo, got_qe, got_qo, part),
    )
    got_qe, got_qo = swap(qe, qo, "space")
    out, rest = call(
        sound_two_body,
        [state, full(2, 4, EL, 128)],
        "sound_two",
        (acoustic_state, part, ends, src) + mats,
        scratch=[keep(4, EL, 256), dma(4)],
        far_out=(0,),
    )
    out = call(
        lambda *r: final_body(2.0 / 3.0 * SOUND_STEP, *r),
        state,
        "cross_two",
        (ge, go, qe, qo, got_qe, got_qo, rest, out),
        scratch=[keep(2, 4, EL, 128), dma(8)],
        far=(7,),
        far_out=(0,),
        aliases={7: 0},
    )
    return flow_increment, out


def solution(mesh):
    both = ("solver", "space")
    grid = P(None, "space", None, "solver")
    sound = P(None, both, None)
    in_specs = (grid, sound, P(), P(), P(), P(both, None, None), P(both), P(None, both))
    return jax.shard_map(
        local, mesh=mesh, in_specs=in_specs, out_specs=(grid, sound), check_vma=False
    )
```
